512 devices in a mesh: ctx: 16 (over x, y_hi, core), exp: 32 (over y_lo, z).
Axes of the slice: x: 4, y: 4 (y_hi: 2, y_lo: 2; y = y_hi * 2 + y_lo), z: 16, core: 2. Of those that a mesh axis runs over, the one named last changes fastest.
Arguments:
- hidden_in: bfloat16 [3072, 4096], P('ctx', 'exp'), may hold values from -5 to 5
- query_nope: bfloat16 [3072, 4096], P('ctx', 'exp'), may hold values from -200 to 200
- query_rope: bfloat16 [3072, 2048], P('ctx', 'exp'), may hold values from -6 to 6
- key_nope: bfloat16 [3072, 4096], P('ctx', 'exp'), may hold values from -200 to 200
- key_rope: bfloat16 [3072, 32], P('ctx'), may hold values from -6 to 6
- values: bfloat16 [3072, 4096], P('ctx', 'exp'), may hold values from -6 to 6
- norm_gain: float32 [4096], P('exp'), may hold values from 0.5 to 1.5
- expert_route: int32 [3072], P('ctx'), may hold values from 0 to 31, as said below
- affinity: float32 [3072, 8], P('ctx'), may hold values from 0.05 to 1
- gate_weight: bfloat16 [32, 4096, 2048], P('exp', None, 'ctx'), may hold values from -0.09375 to 0.09375
- up_weight: bfloat16 [32, 4096, 2048], P('exp', None, 'ctx'), may hold values from -0.09375 to 0.09375
- down_weight: bfloat16 [32, 2048, 4096], P('exp', 'ctx'), may hold values from -0.125 to 0.125
- cotangent: bfloat16 [3072, 4096], P('ctx', 'exp'), may hold values from -6 to 6
Outputs:
- layer_out: bfloat16 [3072, 4096], P('ctx', 'exp')
- grad_hidden: bfloat16 [3072, 4096], P('ctx', 'exp')
- grad_query_nope: bfloat16 [3072, 4096], P('ctx', 'exp')
- grad_query_rope: bfloat16 [3072, 2048], P('ctx', 'exp')
- grad_key_nope: bfloat16 [3072, 4096], P('ctx', 'exp')
- grad_key_rope: bfloat16 [3072, 32], P('ctx')
- grad_values: bfloat16 [3072, 4096], P('ctx', 'exp')
The draws below stay inside these ranges and needn't reach their ends.
Inputs may be any that keep to these rules, and one draw needn't show every extreme that they name: `expert_route`: among the 192 positions of one block (block k holds positions k * 192 to (k + 1) * 192 - 1), at most 12 name one expert, and some expert is named exactly 12 times in every block.
All inputs are finite; a program needn't handle non-finite values.
Results may differ from the reference program's by a relative error of at most 0.03.
Values may be sent and summed in bfloat16 or wider, within the bound.
No kernel may reach another device: no remote copies, remote signals or barrier semaphores. Data moves between devices by JAX's collectives and lax.ppermute only.
A program may use at most 64 MiB of HBM per device.

```python
import math
import jax
import jax.numpy as jnp
from jax import lax

HEADS = 64
NOPE = 64
ROPE = 32
VDIM = 64
FF = 2048
TOPK = 8
TOK_DEV = 192
D = 4096
EXPERTS = 32
SEQ = 3072
CAP = 12
N_CTX = 16


def draw_hidden_in(key, part):
    base_key = jax.random.fold_in(key, 31)
    key_one = jax.random.fold_in(base_key, 0)
    column_place = jnp.arange(D).astype(jnp.float32) / max(D - 1, 1)
    columns = 0.1 * jnp.power(10.0, column_place)
    drawn = jnp.clip(jax.random.normal(key_one, (SEQ, D), jnp.float32), -5.0, 5.0) * columns[None, :]
    return jnp.clip(drawn, -5.0, 5.0).astype(jnp.bfloat16)


def query_key_pair(key):
    base_key = jax.random.fold_in(key, 11)
    key_one, key_two = jax.random.split(base_key, 2)
    full_shape = (SEQ, HEADS * NOPE)
    key_draw = jax.random.normal(key_one, full_shape, jnp.float32)
    queries = jax.random.normal(key_two, full_shape, jnp.float32)
    return (queries, key_draw)


def draw_query_nope(key, part):
    return query_key_pair(key)[0].astype(jnp.bfloat16)


def draw_key_nope(key, part):
    return query_key_pair(key)[1].astype(jnp.bfloat16)


def route_block(key):
    key_one, key_two, key_three = jax.random.split(key, 3)
    mean_load = TOK_DEV // EXPERTS
    half_count = EXPERTS // 2
    moved_rows = jax.random.randint(key_one, (half_count,), 0, mean_load + 1)
    moved_rows = moved_rows.at[0].set(mean_load)
    loads = jnp.concatenate([mean_load + moved_rows, mean_load - moved_rows]).astype(jnp.int32)
    expert_order = jax.random.permutation(key_two, EXPERTS)
    loads = jnp.zeros((EXPERTS,), jnp.int32).at[expert_order].set(loads)
    bounds = jnp.cumsum(loads)
    slot_index = jnp.arange(TOK_DEV, dtype=jnp.int32)
    owner_expert = jnp.searchsorted(bounds, slot_index, side='right').astype(jnp.int32)
    places = jax.random.permutation(key_three, TOK_DEV)
    return jnp.zeros((TOK_DEV,), jnp.int32).at[places].set(owner_expert)


def draw_expert_route(key, part):
    blocks = SEQ // TOK_DEV
    block_keys = jax.random.split(jax.random.fold_in(key, 23), blocks)
    return jax.vmap(route_block)(block_keys).reshape(SEQ)


def block_levels(own_key, shape, cuts, low, high):
    level, own = 1.0, jax.random.fold_in(own_key, 6)
    for axis_at, blocks in cuts:
        draws = jnp.exp(jax.random.uniform(jax.random.fold_in(own, axis_at), (blocks,), jnp.float32, low / len(cuts), high / len(cuts)))
        level = level * jnp.repeat(draws, shape[axis_at] // blocks).reshape([-1 if axis == axis_at else 1 for axis in range(len(shape))])
    return level


def centred(key, extent, spread, bound, cuts=(), kind=jnp.bfloat16):
    loudness = block_levels(key, extent, cuts, -0.22, 0.18) if cuts else 1.0
    result = jax.random.normal(key, extent, jnp.float32) * spread * loudness
    return jnp.minimum(jnp.maximum(result, -bound), bound).astype(kind)


def setup_inputs(seed: int = 0) -> dict:
    key_of = jax.random.split(jax.random.key(seed), 14)
    hidden_in = draw_hidden_in(jax.random.fold_in(key_of[13], 71), 0)
    query_nope = draw_query_nope(jax.random.fold_in(key_of[13], 71), 0)
    query_rope = centred(key_of[2], (SEQ, HEADS * ROPE), 1.0, 6.0, ((0, 16), (1, 32)))
    key_nope = draw_key_nope(jax.random.fold_in(key_of[13], 71), 0)
    key_rope = centred(key_of[4], (SEQ, ROPE), 1.0, 6.0, ((0, 16),))
    values = centred(key_of[5], (SEQ, HEADS * VDIM), 1.0, 6.0, ((0, 16), (1, 32)))
    norm_gain = jnp.clip(1.0 + 0.1 * jax.random.normal(key_of[6], (D,), jnp.float32), 0.5, 1.5)
    expert_route = draw_expert_route(jax.random.fold_in(key_of[13], 71), 0)
    affinity = jnp.clip(0.05 + 0.95 * jax.random.uniform(key_of[8], (SEQ, TOPK), jnp.float32) ** block_levels(key_of[8], (SEQ, TOPK), ((0, 16),), -0.2, 0.2), 0.05, 1.0)
    gate_weight = centred(key_of[9], (EXPERTS, D, FF), D ** -0.5, 0.09375, ((0, 32), (2, 16)))
    up_weight = centred(key_of[10], (EXPERTS, D, FF), D ** -0.5, 0.09375, ((0, 32), (2, 16)))
    down_weight = centred(key_of[11], (EXPERTS, FF, D), FF ** -0.5, 0.125, ((0, 32), (1, 16)))
    cotangent = centred(key_of[12], (SEQ, D), 1.0, 6.0, ((0, 16), (1, 32)))
    return dict(hidden_in=hidden_in, query_nope=query_nope, query_rope=query_rope, key_nope=key_nope, key_rope=key_rope, values=values, norm_gain=norm_gain, expert_route=expert_route, affinity=affinity, gate_weight=gate_weight, up_weight=up_weight, down_weight=down_weight, cotangent=cotangent)


norm_eps = 1e-06
route_scale = 2.5
masked_low = -1e+30
highest = lax.Precision.HIGHEST

def rounded(array_in):
    return lax.optimization_barrier(array_in.astype(jnp.bfloat16)).astype(jnp.float32)

def causal_scores(query_head, query_rot, key_head, key_rot):
    length = query_head.shape[0]
    score_scale = 1.0 / math.sqrt(NOPE + ROPE)
    first_part = jnp.dot(query_head, key_head.T, precision=highest)
    second_part = jnp.dot(query_rot, key_rot.T, precision=highest)
    places = jnp.arange(length)
    visible = places[None, :] <= places[:, None]
    return (jnp.where(visible, (first_part + second_part) * score_scale, masked_low), visible)

def by_head(array_in, width):
    return array_in.reshape(SEQ, HEADS, width).transpose(1, 0, 2).astype(jnp.float32)

def reference(hidden_in, query_nope, query_rope, key_nope, key_rope, values, norm_gain, expert_route, affinity, gate_weight, up_weight, down_weight, cotangent):
    key_rot = key_rope.astype(jnp.float32)
    query_heads = by_head(query_nope, NOPE)
    query_rots = by_head(query_rope, ROPE)
    key_heads = by_head(key_nope, NOPE)
    value_heads = by_head(values, VDIM)

    def forward_head(operands):
        query_head, query_rot, key_head, value_head = operands
        scores, visible = causal_scores(query_head, query_rot, key_head, key_rot)
        row_max = lax.optimization_barrier(jnp.max(scores, -1))
        weights = jnp.where(visible, jnp.exp(scores - row_max[:, None]), 0.0)
        row_total = lax.optimization_barrier(jnp.sum(weights, -1))
        mixed = jnp.dot(rounded(weights), value_head, precision=highest) / row_total[:, None]
        return (mixed.astype(jnp.bfloat16), row_max + jnp.log(row_total))
    attended_heads, log_total = lax.map(forward_head, (query_heads, query_rots, key_heads, value_heads))
    attended = attended_heads.transpose(1, 0, 2).reshape(SEQ, D)
    hidden = hidden_in.astype(jnp.float32) + attended.astype(jnp.float32)
    inverse = lax.rsqrt(lax.optimization_barrier(jnp.mean(hidden * hidden, -1)) + norm_eps)
    normed = (hidden * inverse[:, None] * norm_gain).astype(jnp.bfloat16)
    gate_share = route_scale * affinity[:, 0] / lax.optimization_barrier(jnp.sum(affinity, -1))
    grad_in = cotangent.astype(jnp.float32)
    grad_expert = (gate_share[:, None] * grad_in).astype(jnp.bfloat16)
    expert_hits = (expert_route[:, None] == jnp.arange(EXPERTS)[None, :]).astype(jnp.int32)
    rank_within = lax.optimization_barrier(jnp.sum((jnp.cumsum(expert_hits, 0) - expert_hits) * expert_hits, 1))
    row_most = N_CTX * CAP
    row_table = jnp.full((EXPERTS, row_most), SEQ, jnp.int32).at[expert_route, rank_within].set(jnp.arange(SEQ, dtype=jnp.int32))
    slice_width = FF // N_CTX
    padded_in = jnp.concatenate([normed, jnp.zeros((1, D), jnp.bfloat16)], 0)
    padded_grad = jnp.concatenate([grad_expert, jnp.zeros((1, D), jnp.bfloat16)], 0)

    def one_expert(operands):
        index_row, gate_mat, up_mat, down_mat = operands
        picked = padded_in[index_row]
        picked_grad = padded_grad[index_row]
        gate_val = jnp.dot(picked, gate_mat, preferred_element_type=jnp.float32)
        up_val = jnp.dot(picked, up_mat, preferred_element_type=jnp.float32)
        active = (jax.nn.silu(gate_val) * up_val).astype(jnp.bfloat16)
        pieces = jnp.einsum('rcf,cfd->crd', active.reshape(row_most, N_CTX, slice_width).astype(jnp.float32), down_mat.reshape(N_CTX, slice_width, D).astype(jnp.float32), precision=highest)
        expert_out = lax.optimization_barrier(jnp.sum(rounded(pieces), 0)).astype(jnp.bfloat16)
        grad_active = jnp.dot(picked_grad, down_mat.T, preferred_element_type=jnp.float32)
        sigmoid_gate = jax.nn.sigmoid(gate_val)
        grad_gate = (grad_active * up_val * (sigmoid_gate * (1.0 + gate_val * (1.0 - sigmoid_gate)))).astype(jnp.bfloat16)
        grad_up = (grad_active * jax.nn.silu(gate_val)).astype(jnp.bfloat16)
        back_pieces = jnp.einsum('rcf,cfd->crd', grad_gate.reshape(row_most, N_CTX, slice_width).astype(jnp.float32), gate_mat.T.reshape(N_CTX, slice_width, D).astype(jnp.float32), precision=highest)
        back_pieces = back_pieces + jnp.einsum('rcf,cfd->crd', grad_up.reshape(row_most, N_CTX, slice_width).astype(jnp.float32), up_mat.T.reshape(N_CTX, slice_width, D).astype(jnp.float32), precision=highest)
        expert_grad = lax.optimization_barrier(jnp.sum(rounded(back_pieces), 0)).astype(jnp.bfloat16)
        return (expert_out, expert_grad)
    expert_outs, expert_grads = lax.map(one_expert, (row_table, gate_weight, up_weight, down_weight))
    flat_index = row_table.reshape(-1)
    token_out = jnp.zeros((SEQ + 1, D), jnp.float32).at[flat_index].add(expert_outs.reshape(-1, D).astype(jnp.float32))[:SEQ]
    token_grad = jnp.zeros((SEQ + 1, D), jnp.float32).at[flat_index].add(expert_grads.reshape(-1, D).astype(jnp.float32))[:SEQ]
    layer_out = (hidden + gate_share[:, None] * token_out).astype(jnp.bfloat16)
    scaled = token_grad * norm_gain
    grad_hidden = (grad_in + inverse[:, None] * (scaled - hidden * (inverse * inverse)[:, None] * lax.optimization_barrier(jnp.mean(scaled * hidden, -1, keepdims=True)))).astype(jnp.bfloat16)
    grad_heads = by_head(grad_hidden, VDIM)
    score_scale = 1.0 / math.sqrt(NOPE + ROPE)

    def backward_head(operands):
        query_head, query_rot, key_head, value_head, out_head, log_row, grad_head = operands
        scores, visible = causal_scores(query_head, query_rot, key_head, key_rot)
        probs = jnp.where(visible, jnp.exp(scores - log_row[:, None]), 0.0)
        grad_vals = jnp.dot(rounded(probs).T, grad_head, precision=highest)
        grad_probs = jnp.dot(grad_head, value_head.T, precision=highest)
        row_dot = lax.optimization_barrier(jnp.sum(grad_head * out_head.astype(jnp.float32), -1))
        grad_scores = rounded(probs * (grad_probs - row_dot[:, None]))
        gq_nope = score_scale * jnp.dot(grad_scores, key_head, precision=highest)
        gq_rope = score_scale * jnp.dot(grad_scores, key_rot, precision=highest)
        gk_nope = score_scale * jnp.dot(grad_scores.T, query_head, precision=highest)
        gk_rope = score_scale * jnp.dot(grad_scores.T, query_rot, precision=highest)
        return (gq_nope.astype(jnp.bfloat16), gq_rope.astype(jnp.bfloat16), gk_nope.astype(jnp.bfloat16), gk_rope, grad_vals.astype(jnp.bfloat16))
    gq_nope, gq_rope, gk_nope, gk_rope, grad_vals = lax.map(backward_head, (query_heads, query_rots, key_heads, value_heads, attended_heads, log_total, grad_heads))

    def joined(array_in):
        return array_in.transpose(1, 0, 2).reshape(SEQ, -1)
    return (layer_out, grad_hidden, joined(gq_nope), joined(gq_rope), joined(gk_nope), lax.optimization_barrier(jnp.sum(gk_rope, 0)).astype(jnp.bfloat16), joined(grad_vals))
```

```python
import functools
import math

import jax
import jax.numpy as jnp
from jax import lax
from jax.experimental import pallas as pl
from jax.experimental.pallas import tpu as pltpu
from jax.sharding import PartitionSpec as P

NOPE = 64
ROPE = 32
VDIM = 64
D = 4096
CAP = 12
SLOT = 16
LANES = 128

norm_eps = 1e-06
route_scale = 2.5
masked_low = -1e30
score_scale = 1.0 / math.sqrt(NOPE + ROPE)

bf16 = jnp.bfloat16
f32 = jnp.float32
VMEM_LIMIT = 56 * 1024 * 1024

KEY = slice(0, 256)
QUERY = slice(128, 384)
VALUE = slice(384, 512)


def nt_dot(a, b):
    return lax.dot_general(a, b, (((1,), (1,)), ((), ())), preferred_element_type=f32)


def nn_dot(a, b):
    return jnp.dot(a, b, preferred_element_type=f32)


def lanes_of(shape):
    return lax.broadcasted_iota(jnp.int32, shape, len(shape) - 1)


def pieces_of(value, count):
    pieces = []
    for _ in range(count):
        piece = value.astype(bf16).astype(f32)
        pieces.append(piece)
        value = value - piece
    return pieces


def own_query(block, head):
    rows = block.shape[0]
    lane = lanes_of((rows, LANES))
    zero = jnp.zeros((rows, LANES), bf16)
    nope = jnp.where(lane // NOPE == head, block[:, 256:384], zero)
    start = ROPE + head * ROPE
    rot = pltpu.roll(block[:, 128:256].astype(f32), LANES - start, 1)
    rot = jnp.where(lane < ROPE, rot, 0.0).astype(bf16)
    return jnp.concatenate([nope, rot], 1)


def own_key(block, head):
    rows = block.shape[0]
    lane = lanes_of((rows, LANES))
    zero = jnp.zeros((rows, LANES), bf16)
    nope = jnp.where(lane // NOPE == head, block[:, 0:128], zero)
    start = ROPE + head * ROPE
    rot = pltpu.roll(block[:, 128:256].astype(f32), start, 1)
    rot = jnp.where(lane // ROPE == 1 + head, rot, 0.0).astype(bf16)
    return jnp.concatenate([rot, nope], 1)


def pair_places(rows, core):
    lane = lanes_of((rows, 2 * rows))
    return lane - jnp.where(lane >= rows, 2 * rows, 0) * core


def slots_along_rows(route_row, experts):
    count = route_row.shape[1]
    hits = (lax.broadcasted_iota(jnp.int32, (experts, count), 0) == route_row).astype(f32)
    before = lax.broadcasted_iota(jnp.int32, (count, count), 0) < lanes_of((count, count))
    ranks = nn_dot(hits.astype(bf16), before.astype(f32).astype(bf16))
    rank = jnp.sum(ranks * hits, 0, keepdims=True)
    return route_row * SLOT + rank.astype(jnp.int32)


def slots_along_columns(route_column, experts):
    count = route_column.shape[0]
    hits = (lanes_of((count, experts)) == route_column).astype(f32)
    before = lanes_of((count, count)) < lax.broadcasted_iota(jnp.int32, (count, count), 0)
    ranks = nn_dot(before.astype(f32).astype(bf16), hits.astype(bf16))
    rank = jnp.sum(ranks * hits, 1, keepdims=True)
    return route_column * SLOT + rank.astype(jnp.int32)


def gate_share_of(affinity):
    return route_scale * affinity[:, 0:1] / jnp.sum(affinity, 1, keepdims=True)


def forward_kernel(
    experts,
    place_ref,
    same_ref,
    cross_ref,
    block_ref,
    hidden_ref,
    gain_ref,
    route_ref,
    affinity_ref,
    cotangent_ref,
    attended_ref,
    log_ref,
    send_ref,
    query_ref,
):
    rows = block_ref.shape[0]
    place = place_ref[0]
    pair, core = place // 2, place % 2
    for head in range(2):
        query_ref[head] = own_query(block_ref[...], head)

    def load(pair_index, columns):
        at = pl.multiple_of(pair_index * rows, rows)
        return jnp.concatenate(
            [same_ref[pl.ds(at, rows), columns], cross_ref[pl.ds(at, rows), columns]], 0
        )

    keys = load(pair, KEY)
    vals = load(pair, VALUE)
    visible = pair_places(rows, core) <= lax.broadcasted_iota(jnp.int32, (rows, 2 * rows), 0)
    state = []
    for head in range(2):
        scores = jnp.where(visible, nt_dot(query_ref[head], keys) * score_scale, masked_low)
        top = jnp.max(scores, 1, keepdims=True)
        weights = jnp.where(visible, jnp.exp(scores - top), 0.0)
        total = jnp.sum(weights, 1, keepdims=True)
        state.extend([top, total, nn_dot(weights.astype(bf16), vals)])

    def step(index, state):
        keys = load(index, KEY)
        vals = load(index, VALUE)
        after = []
        for head in range(2):
            top, total, mixed = state[3 * head : 3 * head + 3]
            scores = nt_dot(query_ref[head], keys) * score_scale
            new_top = jnp.maximum(top, jnp.max(scores, 1, keepdims=True))
            weights = jnp.exp(scores - new_top)
            factor = jnp.exp(top - new_top)
            total = total * factor + jnp.sum(weights, 1, keepdims=True)
            mixed = mixed * factor + nn_dot(weights.astype(bf16), vals)
            after.extend([new_top, total, mixed])
        return tuple(after)

    state = lax.fori_loop(0, pair, step, tuple(state))
    first = lanes_of((rows, LANES)) < VDIM
    attended = jnp.where(first, state[2] / state[1], state[5] / state[4]).astype(bf16)
    attended_ref[...] = attended
    log_ref[...] = jnp.where(
        first, state[0] + jnp.log(state[1]), state[3] + jnp.log(state[4])
    )
    hidden = hidden_ref[...].astype(f32) + attended.astype(f32)
    raised = (hidden * gain_ref[...]).astype(bf16)
    share = gate_share_of(affinity_ref[...])
    grad = (share * cotangent_ref[...].astype(f32)).astype(bf16)
    slots = slots_along_rows(route_ref[...], experts)
    table = lax.broadcasted_iota(jnp.int32, (experts * SLOT, rows), 0) == slots
    table = table.astype(f32).astype(bf16)
    row = lax.broadcasted_iota(jnp.int32, (SLOT, LANES), 0)
    gains = jnp.zeros((SLOT, LANES), f32)
    for index, piece in enumerate(pieces_of(gain_ref[...], 3)):
        gains = jnp.where(row == CAP + index, piece, gains)
    gains = jnp.broadcast_to(gains[None], (experts, SLOT, LANES)).reshape(-1, LANES)
    send_ref[:, 0:LANES] = (nn_dot(table, raised) + gains).astype(bf16)
    send_ref[:, LANES:] = nn_dot(table, grad).astype(bf16)


def gathered_rows(ref, count, slices, column):
    parts = []
    for index in range(slices):
        part = ref[:, index * SLOT : (index + 1) * SLOT, column : column + LANES]
        parts.append(part.reshape(count * SLOT, LANES))
    return jnp.concatenate(parts, 1)


def gain_of(raised):
    pieces = raised[CAP : CAP + 3].astype(f32)
    return pieces[0:1] + pieces[1:2] + pieces[2:3]


def inverse_of(raised, gain):
    hidden = raised.astype(f32) / gain
    return lax.rsqrt(jnp.sum(hidden * hidden, 1, keepdims=True) / D + norm_eps)


def expert_kernel(
    rows_ref,
    gate_own_ref,
    up_own_ref,
    down_own_ref,
    gate_other_ref,
    up_other_ref,
    down_other_ref,
    out_ref,
):
    count, depth, _ = rows_ref.shape
    slices = depth // SLOT
    raised = gathered_rows(rows_ref, count, slices, 0)
    grad = gathered_rows(rows_ref, count, slices, LANES)
    inverse = inverse_of(raised, gain_of(raised[0:SLOT]))
    pairs = (
        (gate_own_ref, up_own_ref, down_own_ref),
        (gate_other_ref, up_other_ref, down_other_ref),
    )
    made = []
    for gate_ref, up_ref, down_ref in pairs:
        gate_val = inverse * nn_dot(raised, gate_ref[...])
        up_val = inverse * nn_dot(raised, up_ref[...])
        grad_active = nt_dot(grad, down_ref[...])
        sig = 1.0 / (1.0 + jnp.exp(-gate_val))
        silu = gate_val * sig
        active = (silu * up_val).astype(bf16)
        grad_gate = (grad_active * up_val * (sig * (1.0 + gate_val * (1.0 - sig)))).astype(bf16)
        grad_up = (grad_active * silu).astype(bf16)
        made.append((active, grad_gate, grad_up))
    for index in range(slices):
        at = slice(index * LANES, (index + 1) * LANES)
        out = jnp.zeros((count * SLOT, LANES), f32)
        back = jnp.zeros((count * SLOT, LANES), f32)
        for (gate_ref, up_ref, down_ref), (active, grad_gate, grad_up) in zip(pairs, made):
            out = out + nn_dot(active, down_ref[:, at])
            back = back + nt_dot(grad_gate, gate_ref[at, :]) + nt_dot(grad_up, up_ref[at, :])
        span = slice(index * SLOT, (index + 1) * SLOT)
        out_ref[:, span, 0:LANES] = out.astype(bf16).reshape(count, SLOT, LANES)
        out_ref[:, span, LANES:] = back.astype(bf16).reshape(count, SLOT, LANES)


def reduce_kernel(terms_ref, rows_ref, out_ref):
    count, depth, _ = terms_ref.shape
    slices = depth // SLOT
    total = terms_ref[0].astype(f32)
    for index in range(1, count):
        total = total + terms_ref[index].astype(f32)
    raised = rows_ref[:, 0:LANES].astype(f32).reshape(slices, SLOT, LANES)
    back = total[:, LANES:].reshape(slices, SLOT, LANES)
    gain = jnp.sum(raised[:, CAP : CAP + 3, :], 1, keepdims=True)
    hidden = raised / gain
    squares = jnp.sum(jnp.sum(hidden * hidden, 0), 1, keepdims=True)
    inverse = lax.rsqrt(squares / D + norm_eps)
    cross = jnp.sum(jnp.sum(back * raised, 0), 1, keepdims=True) / D
    grad = inverse[None] * (back * gain - hidden * (inverse * inverse * cross)[None])
    row = lax.broadcasted_iota(jnp.int32, (slices, SLOT, LANES), 1)
    grad = jnp.where(row < CAP, grad, 0.0)
    out_ref[:, 0:LANES] = total[:, 0:LANES].astype(bf16)
    out_ref[:, LANES:] = grad.astype(bf16).reshape(depth, LANES)


def combine_kernel(
    experts,
    home_ref,
    hidden_ref,
    attended_ref,
    log_ref,
    route_ref,
    affinity_ref,
    cotangent_ref,
    layer_ref,
    grad_ref,
    stats_ref,
):
    rows = hidden_ref.shape[0]
    slots = slots_along_columns(route_ref[...], experts)
    table = (lanes_of((rows, experts * SLOT)) == slots).astype(f32).astype(bf16)
    token = nn_dot(table, home_ref[...])
    attended = attended_ref[...].astype(f32)
    hidden = hidden_ref[...].astype(f32) + attended
    share = gate_share_of(affinity_ref[...])
    layer_ref[...] = (hidden + share * token[:, 0:LANES]).astype(bf16)
    grad = (cotangent_ref[...].astype(f32) + token[:, LANES:]).astype(bf16)
    grad_ref[...] = grad
    product = grad.astype(f32) * attended
    lane = lanes_of((rows, LANES))
    columns = []
    for head in range(2):
        dot = jnp.sum(jnp.where(lane // VDIM == head, product, 0.0), 1, keepdims=True)
        columns += pieces_of(dot, 3)
        columns += pieces_of(log_ref[:, head * VDIM : head * VDIM + 1], 3)
    stats = jnp.zeros((rows, LANES), f32)
    for index, column in enumerate(columns):
        stats = jnp.where(lane == index, column, stats)
    stats_ref[:, 0:LANES] = grad
    stats_ref[:, LANES:] = stats.astype(bf16)


def backward_kernel(
    place_ref,
    same_ref,
    cross_ref,
    grad_same_ref,
    grad_cross_ref,
    block_ref,
    stats_ref,
    query_nope_ref,
    query_rope_ref,
    key_nope_ref,
    values_ref,
    rope_ref,
    query_ref,
    key_ref,
    grads_ref,
    vals_ref,
    dq_ref,
    dk_ref,
    dv_ref,
):
    rows = block_ref.shape[0]
    place = place_ref[0]
    pair, core = place // 2, place % 2
    lane = lanes_of((rows, LANES))
    zero = jnp.zeros((rows, LANES), bf16)
    one = jnp.ones((rows, LANES), f32)
    logs, ones_log = [], []
    for head in range(2):
        base = 6 * head
        query_ref[head] = own_query(block_ref[...], head)
        key_ref[head] = own_key(block_ref[...], head)
        minus = jnp.where((lane >= base) & (lane < base + 3), -one, 0.0).astype(bf16)
        of_log = jnp.where((lane >= base + 3) & (lane < base + 6), one, 0.0).astype(bf16)
        ones_log.append(of_log)
        mine = lane // VDIM == head
        stats = stats_ref[:, LANES:].astype(f32)
        own = jnp.where(mine, stats_ref[:, 0:LANES], zero)
        value = jnp.where(mine, block_ref[:, VALUE], zero)
        grads_ref[head] = own
        vals_ref[head] = jnp.concatenate([value, minus], 1)
        dot = jnp.sum(jnp.where((lane >= base) & (lane < base + 3), stats, 0.0), 1, keepdims=True)
        log = jnp.sum(
            jnp.where((lane >= base + 3) & (lane < base + 6), stats, 0.0), 1, keepdims=True
        )
        logs.append((log, dot))
    dq_ref[...] = jnp.zeros_like(dq_ref)
    dk_ref[...] = jnp.zeros_like(dk_ref)
    dv_ref[...] = jnp.zeros_like(dv_ref)

    def load(first, second, pair_index, columns):
        at = pl.multiple_of(pair_index * rows, rows)
        return jnp.concatenate(
            [first[pl.ds(at, rows), columns], second[pl.ds(at, rows), columns]], 0
        )

    def query_side(index, visible):
        keys = load(same_ref, cross_ref, index, KEY)
        vals = load(same_ref, cross_ref, index, VALUE)
        for head in range(2):
            log, dot = logs[head]
            prob = jnp.exp(nt_dot(query_ref[head], keys) * score_scale - log)
            if visible is not None:
                prob = jnp.where(visible, prob, 0.0)
            grad_prob = nt_dot(grads_ref[head], vals)
            grad_score = (prob * (grad_prob - dot)).astype(bf16)
            dq_ref[head] += nn_dot(grad_score, keys)

    def key_side(index, visible):
        queries = load(same_ref, cross_ref, index, QUERY)
        grads = load(grad_same_ref, grad_cross_ref, index, slice(0, 2 * LANES))
        for head in range(2):
            log = nt_dot(ones_log[head], grads[:, LANES:])
            prob = jnp.exp(nt_dot(key_ref[head], queries) * score_scale - log)
            if visible is not None:
                prob = jnp.where(visible, prob, 0.0)
            dv_ref[head] += nn_dot(prob.astype(bf16), grads[:, 0:LANES])
            grad_prob = nt_dot(vals_ref[head], grads)
            grad_score = (prob * grad_prob).astype(bf16)
            dk_ref[head] += nn_dot(grad_score, queries)

    places = pair_places(rows, core)
    line = lax.broadcasted_iota(jnp.int32, (rows, 2 * rows), 0)
    query_side(pair, places <= line)
    key_side(pair, places >= line)

    def query_step(index, carry):
        query_side(index, None)
        return carry

    def key_step(index, carry):
        key_side(index, None)
        return carry

    lax.fori_loop(0, pair, query_step, 0)
    lax.fori_loop(pair + 1, same_ref.shape[0] // rows, key_step, 0)

    first = lane < NOPE
    query_nope_ref[...] = (
        score_scale * jnp.where(first, dq_ref[0, :, 0:LANES], dq_ref[1, :, 0:LANES])
    ).astype(bf16)
    rot = jnp.where(
        lane < ROPE, dq_ref[0, :, LANES:], pltpu.roll(dq_ref[1, :, LANES:], ROPE, 1)
    )
    query_rope_ref[...] = (score_scale * rot).astype(bf16)[:, 0 : 2 * ROPE]
    key_nope_ref[...] = (
        score_scale * jnp.where(first, dk_ref[0, :, LANES:], dk_ref[1, :, LANES:])
    ).astype(bf16)
    values_ref[...] = jnp.where(lane < VDIM, dv_ref[0], dv_ref[1]).astype(bf16)
    shared = pltpu.roll(dk_ref[0, :, 0:LANES], LANES - ROPE, 1) + pltpu.roll(
        dk_ref[1, :, 0:LANES], LANES - 2 * ROPE, 1
    )
    quarter = rows // 4
    packed = jnp.zeros((quarter, LANES), f32)
    small = lanes_of((quarter, LANES))
    for index in range(4):
        part = shared[index * quarter : (index + 1) * quarter]
        if index:
            part = pltpu.roll(part, index * ROPE, 1)
        packed = jnp.where(small // ROPE == index, part, packed)
    rope_ref[...] = (score_scale * packed).astype(bf16)


def rope_kernel(terms_ref, out_ref):
    total = terms_ref[0].astype(f32)
    for index in range(1, terms_ref.shape[0]):
        total = total + terms_ref[index].astype(f32)
    quarter = total.shape[0]
    for index in range(4):
        part = total if index == 0 else pltpu.roll(total, LANES - index * ROPE, 1)
        out_ref[index * quarter : (index + 1) * quarter, :] = part[:, 0:ROPE].astype(bf16)


def call(body, outs, scratch=(), scalars=0, count=0):
    place = [pl.BlockSpec(memory_space=pltpu.SMEM)] * scalars
    return pl.pallas_call(
        body,
        out_shape=outs,
        in_specs=place + [pl.BlockSpec(memory_space=pltpu.VMEM)] * count,
        out_specs=jax.tree.map(lambda _: pl.BlockSpec(memory_space=pltpu.VMEM), outs),
        scratch_shapes=list(scratch),
        compiler_params=pltpu.CompilerParams(vmem_limit_bytes=VMEM_LIMIT),
    )


def shape_of(*dims, dtype=bf16):
    return jax.ShapeDtypeStruct(dims, dtype)


def exchange(blocks, axis, groups=None):
    return lax.all_to_all(blocks, axis, 0, 0, tiled=True, axis_index_groups=groups)


def per_device(
    hidden_in,
    query_nope,
    query_rope,
    key_nope,
    key_rope,
    values,
    norm_gain,
    expert_route,
    affinity,
    gate_weight,
    up_weight,
    down_weight,
    cotangent,
):
    rows, width = hidden_in.shape
    ctx_count, experts = lax.axis_size("ctx"), lax.axis_size("exp")
    half = ctx_count // 2
    groups = [[core + 2 * index for index in range(half)] for core in range(2)]
    across = [(index, index ^ 1) for index in range(ctx_count)]
    depth = experts * SLOT

    def swap(value):
        return lax.ppermute(value, "ctx", across)

    def spread(block):
        copies = jnp.broadcast_to(block[None], (half,) + block.shape)
        return exchange(copies, "ctx", groups)

    place = lax.axis_index("ctx").astype(jnp.int32).reshape(1)
    mine = (gate_weight[0], up_weight[0], down_weight[0])
    others = [swap(weight) for weight in mine]
    block = jnp.concatenate(
        [key_nope, key_rope, query_rope, jnp.zeros((rows, ROPE), bf16), query_nope, values], 1
    )
    same = spread(block).reshape(half * rows, -1)
    cross = swap(same)
    gain_row = norm_gain.reshape(1, width)

    attended, logs, send = call(
        functools.partial(forward_kernel, experts),
        (shape_of(rows, width), shape_of(rows, width, dtype=f32), shape_of(depth, 2 * width)),
        [pltpu.VMEM((2, rows, 2 * width), bf16)],
        1,
        8,
    )(
        place,
        same,
        cross,
        block,
        hidden_in,
        gain_row,
        expert_route.reshape(1, rows),
        affinity,
        cotangent,
    )
    received = exchange(send.reshape(experts, SLOT, 2 * width), "exp").reshape(depth, 2 * width)
    rows_all = spread(received)
    partial = call(expert_kernel, shape_of(half, depth, 2 * width), count=7)(
        rows_all, *mine, *others
    )
    terms = exchange(partial, "ctx", groups)
    back = call(reduce_kernel, shape_of(depth, 2 * width), count=2)(terms, received)
    home = exchange(back.reshape(experts, SLOT, 2 * width), "exp").reshape(depth, 2 * width)
    layer_out, grad_hidden, stats = call(
        functools.partial(combine_kernel, experts),
        (shape_of(rows, width), shape_of(rows, width), shape_of(rows, 2 * width)),
        count=7,
    )(home, hidden_in, attended, logs, expert_route.reshape(rows, 1), affinity, cotangent)
    grad_same = spread(stats).reshape(half * rows, -1)
    grad_cross = swap(grad_same)
    quarter = rows // 4
    gq_nope, gq_rope, gk_nope, g_values, rope_part = call(
        backward_kernel,
        (
            shape_of(rows, width),
            shape_of(rows, 2 * ROPE),
            shape_of(rows, width),
            shape_of(rows, width),
            shape_of(quarter, LANES),
        ),
        [
            pltpu.VMEM((2, rows, 2 * width), bf16),
            pltpu.VMEM((2, rows, 2 * width), bf16),
            pltpu.VMEM((2, rows, width), bf16),
            pltpu.VMEM((2, rows, 2 * width), bf16),
            pltpu.VMEM((2, rows, 2 * width), f32),
            pltpu.VMEM((2, rows, 2 * width), f32),
            pltpu.VMEM((2, rows, width), f32),
        ],
        1,
        6,
    )(place, same, cross, grad_same, grad_cross, block, stats)
    rope_terms = exchange(jnp.broadcast_to(rope_part[None], (experts, quarter, LANES)), "exp")
    gk_rope = call(rope_kernel, shape_of(rows, ROPE), count=1)(rope_terms)
    return (layer_out, grad_hidden, gq_nope, gq_rope, gk_nope, gk_rope, g_values)


def solution(mesh):
    placed = (
        P("ctx", "exp"),
        P("ctx", "exp"),
        P("ctx", "exp"),
        P("ctx", "exp"),
        P("ctx", None),
        P("ctx", "exp"),
        P("exp"),
        P("ctx"),
        P("ctx", None),
        P("exp", None, "ctx"),
        P("exp", None, "ctx"),
        P("exp", "ctx", None),
        P("ctx", "exp"),
    )
    return jax.shard_map(
        per_device,
        mesh=mesh,
        in_specs=placed,
        out_specs=(
            P("ctx", "exp"),
            P("ctx", "exp"),
            P("ctx", "exp"),
            P("ctx", "exp"),
            P("ctx", "exp"),
            P("ctx", None),
            P("ctx", "exp"),
        ),
        check_vma=False,
    )
```

```python
import functools
import math

import jax
import jax.numpy as jnp
from jax import lax
from jax.experimental import pallas as pl
from jax.experimental.pallas import tpu as pltpu
from jax.sharding import PartitionSpec as P

NOPE = 64
ROPE = 32
VDIM = 64
D = 4096
CAP = 12
SLOT = 16
LANES = 128

norm_eps = 1e-06
route_scale = 2.5
masked_low = -1e30
score_scale = 1.0 / math.sqrt(NOPE + ROPE)

bf16 = jnp.bfloat16
f32 = jnp.float32
MIB = 1024 * 1024

KEY = slice(0, 256)
QUERY = slice(128, 384)
VALUE = slice(384, 512)


def nt_dot(a, b):
    return lax.dot_general(a, b, (((1,), (1,)), ((), ())), preferred_element_type=f32)


def nn_dot(a, b):
    return jnp.dot(a, b, preferred_element_type=f32)


def lanes_of(shape):
    return lax.broadcasted_iota(jnp.int32, shape, len(shape) - 1)


def pieces_of(value, count):
    pieces = []
    for _ in range(count):
        piece = value.astype(bf16).astype(f32)
        pieces.append(piece)
        value = value - piece
    return pieces


def own_query(block, head):
    rows = block.shape[0]
    lane = lanes_of((rows, LANES))
    zero = jnp.zeros((rows, LANES), bf16)
    nope = jnp.where(lane // NOPE == head, block[:, 256:384], zero)
    start = ROPE + head * ROPE
    rot = pltpu.roll(block[:, 128:256].astype(f32), LANES - start, 1)
    rot = jnp.where(lane < ROPE, rot, 0.0).astype(bf16)
    return jnp.concatenate([nope, rot], 1)


def own_key(block, head):
    rows = block.shape[0]
    lane = lanes_of((rows, LANES))
    zero = jnp.zeros((rows, LANES), bf16)
    nope = jnp.where(lane // NOPE == head, block[:, 0:128], zero)
    start = ROPE + head * ROPE
    rot = pltpu.roll(block[:, 128:256].astype(f32), start, 1)
    rot = jnp.where(lane // ROPE == 1 + head, rot, 0.0).astype(bf16)
    return jnp.concatenate([rot, nope], 1)


def pair_places(rows, core):
    lane = lanes_of((rows, 2 * rows))
    return lane - jnp.where(lane >= rows, 2 * rows, 0) * core


def slots_along_rows(route_row, experts):
    count = route_row.shape[1]
    hits = (lax.broadcasted_iota(jnp.int32, (experts, count), 0) == route_row).astype(f32)
    before = lax.broadcasted_iota(jnp.int32, (count, count), 0) < lanes_of((count, count))
    ranks = nn_dot(hits.astype(bf16), before.astype(f32).astype(bf16))
    rank = jnp.sum(ranks * hits, 0, keepdims=True)
    return route_row * SLOT + rank.astype(jnp.int32)


def slots_along_columns(route_column, experts):
    count = route_column.shape[0]
    hits = (lanes_of((count, experts)) == route_column).astype(f32)
    before = lanes_of((count, count)) < lax.broadcasted_iota(jnp.int32, (count, count), 0)
    ranks = nn_dot(before.astype(f32).astype(bf16), hits.astype(bf16))
    rank = jnp.sum(ranks * hits, 1, keepdims=True)
    return route_column * SLOT + rank.astype(jnp.int32)


def gate_share_of(affinity):
    return route_scale * affinity[:, 0:1] / jnp.sum(affinity, 1, keepdims=True)


def forward_kernel(
    experts,
    place_ref,
    same_ref,
    cross_ref,
    block_ref,
    hidden_ref,
    gain_ref,
    route_ref,
    affinity_ref,
    cotangent_ref,
    attended_ref,
    log_ref,
    send_ref,
    query_ref,
):
    rows = block_ref.shape[0]
    place = place_ref[0]
    pair, core = place // 2, place % 2
    for head in range(2):
        query_ref[head] = own_query(block_ref[...], head)

    def load(pair_index, columns):
        at = pl.multiple_of(pair_index * rows, rows)
        return jnp.concatenate(
            [same_ref[pl.ds(at, rows), columns], cross_ref[pl.ds(at, rows), columns]], 0
        )

    keys = load(pair, KEY)
    vals = load(pair, VALUE)
    visible = pair_places(rows, core) <= lax.broadcasted_iota(jnp.int32, (rows, 2 * rows), 0)
    state = []
    for head in range(2):
        scores = jnp.where(visible, nt_dot(query_ref[head], keys) * score_scale, masked_low)
        top = jnp.max(scores, 1, keepdims=True)
        weights = jnp.where(visible, jnp.exp(scores - top), 0.0)
        total = jnp.sum(weights, 1, keepdims=True)
        state.extend([top, total, nn_dot(weights.astype(bf16), vals)])

    def step(index, state):
        keys = load(index, KEY)
        vals = load(index, VALUE)
        after = []
        for head in range(2):
            top, total, mixed = state[3 * head : 3 * head + 3]
            scores = nt_dot(query_ref[head], keys) * score_scale
            new_top = jnp.maximum(top, jnp.max(scores, 1, keepdims=True))
            weights = jnp.exp(scores - new_top)
            factor = jnp.exp(top - new_top)
            total = total * factor + jnp.sum(weights, 1, keepdims=True)
            mixed = mixed * factor + nn_dot(weights.astype(bf16), vals)
            after.extend([new_top, total, mixed])
        return tuple(after)

    state = lax.fori_loop(0, pair, step, tuple(state))
    first = lanes_of((rows, LANES)) < VDIM
    attended = jnp.where(first, state[2] / state[1], state[5] / state[4]).astype(bf16)
    attended_ref[...] = attended
    log_ref[...] = jnp.where(
        first, state[0] + jnp.log(state[1]), state[3] + jnp.log(state[4])
    )
    hidden = hidden_ref[...].astype(f32) + attended.astype(f32)
    raised = (hidden * gain_ref[...]).astype(bf16)
    share = gate_share_of(affinity_ref[...])
    grad = (share * cotangent_ref[...].astype(f32)).astype(bf16)
    slots = slots_along_rows(route_ref[...], experts)
    table = lax.broadcasted_iota(jnp.int32, (experts * SLOT, rows), 0) == slots
    table = table.astype(f32).astype(bf16)
    row = lax.broadcasted_iota(jnp.int32, (SLOT, LANES), 0)
    gains = jnp.zeros((SLOT, LANES), f32)
    for index, piece in enumerate(pieces_of(gain_ref[...], 3)):
        gains = jnp.where(row == CAP + index, piece, gains)
    gains = jnp.broadcast_to(gains[None], (experts, SLOT, LANES)).reshape(-1, LANES)
    send_ref[:, 0:LANES] = (nn_dot(table, raised) + gains).astype(bf16)
    send_ref[:, LANES:] = nn_dot(table, grad).astype(bf16)


def gathered_rows(ref, count, slices, column):
    parts = []
    for index in range(slices):
        part = ref[:, index * SLOT : (index + 1) * SLOT, column : column + LANES]
        parts.append(part.reshape(count * SLOT, LANES))
    return jnp.concatenate(parts, 1)


def gain_of(raised):
    pieces = raised[CAP : CAP + 3].astype(f32)
    return pieces[0:1] + pieces[1:2] + pieces[2:3]


def inverse_of(raised, gain):
    hidden = raised.astype(f32) / gain
    return lax.rsqrt(jnp.sum(hidden * hidden, 1, keepdims=True) / D + norm_eps)


def expert_kernel(rows_ref, *refs):
    weight_refs, out_ref = refs[:-1], refs[-1]
    count, depth, _ = rows_ref.shape
    slices = depth // SLOT
    wide = 2 * LANES
    raised = gathered_rows(rows_ref, count, slices, 0)
    grad = gathered_rows(rows_ref, count, slices, LANES)
    inverse = inverse_of(raised, gain_of(raised[0:SLOT]))
    pairs = [weight_refs[at : at + 2] for at in range(0, len(weight_refs), 2)]

    def side_by_side(pair, base, index):
        at = slice(base + index * wide, base + (index + 1) * wide)
        return jnp.concatenate([pair[0][at, :], pair[1][at, :]], 1)

    def down_block(pair, index):
        at = 2 * D + index * wide
        halves = [
            jnp.concatenate([ref[at : at + LANES, :], ref[at + LANES : at + wide, :]], 1)
            for ref in pair
        ]
        return jnp.concatenate(halves, 0)

    made = []
    for pair in pairs:
        zero = jnp.zeros((count * SLOT, wide), f32)
        gate_val, up_val, grad_active = zero, zero, zero
        for index in range(slices // 2):
            at = slice(index * wide, (index + 1) * wide)
            gate_val = gate_val + nn_dot(raised[:, at], side_by_side(pair, 0, index))
            up_val = up_val + nn_dot(raised[:, at], side_by_side(pair, D, index))
            grad_active = grad_active + nt_dot(grad[:, at], down_block(pair, index))
        gate_val, up_val = inverse * gate_val, inverse * up_val
        sig = 1.0 / (1.0 + jnp.exp(-gate_val))
        silu = gate_val * sig
        active = (silu * up_val).astype(bf16)
        grad_gate = (grad_active * up_val * (sig * (1.0 + gate_val * (1.0 - sig)))).astype(bf16)
        grad_up = (grad_active * silu).astype(bf16)
        made.append((active, grad_gate, grad_up))
    for index in range(slices // 2):
        out = jnp.zeros((count * SLOT, wide), f32)
        back = jnp.zeros((count * SLOT, wide), f32)
        for pair, (active, grad_gate, grad_up) in zip(pairs, made):
            out = out + nn_dot(active, down_block(pair, index))
            back = back + nt_dot(grad_gate, side_by_side(pair, 0, index))
            back = back + nt_dot(grad_up, side_by_side(pair, D, index))
        out, back = out.astype(bf16), back.astype(bf16)
        for part in range(2):
            at = slice(part * LANES, (part + 1) * LANES)
            span = slice((2 * index + part) * SLOT, (2 * index + part + 1) * SLOT)
            out_ref[:, span, 0:LANES] = out[:, at].reshape(count, SLOT, LANES)
            out_ref[:, span, LANES:] = back[:, at].reshape(count, SLOT, LANES)


def reduce_kernel(terms_ref, rows_ref, out_ref):
    count, depth, _ = terms_ref.shape
    slices = depth // SLOT
    total = terms_ref[0].astype(f32)
    for index in range(1, count):
        total = total + terms_ref[index].astype(f32)
    raised = rows_ref[:, 0:LANES].astype(f32).reshape(slices, SLOT, LANES)
    back = total[:, LANES:].reshape(slices, SLOT, LANES)
    gain = jnp.sum(raised[:, CAP : CAP + 3, :], 1, keepdims=True)
    hidden = raised / gain
    squares = jnp.sum(jnp.sum(hidden * hidden, 0), 1, keepdims=True)
    inverse = lax.rsqrt(squares / D + norm_eps)
    cross = jnp.sum(jnp.sum(back * raised, 0), 1, keepdims=True) / D
    grad = inverse[None] * (back * gain - hidden * (inverse * inverse * cross)[None])
    row = lax.broadcasted_iota(jnp.int32, (slices, SLOT, LANES), 1)
    grad = jnp.where(row < CAP, grad, 0.0)
    out_ref[:, 0:LANES] = total[:, 0:LANES].astype(bf16)
    out_ref[:, LANES:] = grad.astype(bf16).reshape(depth, LANES)


def combine_kernel(
    experts,
    home_ref,
    hidden_ref,
    attended_ref,
    log_ref,
    route_ref,
    affinity_ref,
    cotangent_ref,
    layer_ref,
    grad_ref,
    stats_ref,
):
    rows = hidden_ref.shape[0]
    slots = slots_along_columns(route_ref[...], experts)
    table = (lanes_of((rows, experts * SLOT)) == slots).astype(f32).astype(bf16)
    token = nn_dot(table, home_ref[...])
    attended = attended_ref[...].astype(f32)
    hidden = hidden_ref[...].astype(f32) + attended
    share = gate_share_of(affinity_ref[...])
    layer_ref[...] = (hidden + share * token[:, 0:LANES]).astype(bf16)
    grad = (cotangent_ref[...].astype(f32) + token[:, LANES:]).astype(bf16)
    grad_ref[...] = grad
    product = grad.astype(f32) * attended
    lane = lanes_of((rows, LANES))
    columns = []
    for head in range(2):
        dot = jnp.sum(jnp.where(lane // VDIM == head, product, 0.0), 1, keepdims=True)
        columns += pieces_of(dot, 3)
        columns += pieces_of(log_ref[:, head * VDIM : head * VDIM + 1], 3)
    stats = jnp.zeros((rows, LANES), f32)
    for index, column in enumerate(columns):
        stats = jnp.where(lane == index, column, stats)
    stats_ref[:, 0:LANES] = grad
    stats_ref[:, LANES:] = stats.astype(bf16)


def backward_kernel(
    place_ref,
    same_ref,
    cross_ref,
    grad_same_ref,
    grad_cross_ref,
    block_ref,
    stats_ref,
    query_nope_ref,
    query_rope_ref,
    key_nope_ref,
    values_ref,
    rope_ref,
    query_ref,
    key_ref,
    grads_ref,
    vals_ref,
    dq_ref,
    dk_ref,
    dv_ref,
):
    rows = block_ref.shape[0]
    place = place_ref[0]
    pair, core = place // 2, place % 2
    lane = lanes_of((rows, LANES))
    zero = jnp.zeros((rows, LANES), bf16)
    one = jnp.ones((rows, LANES), f32)
    logs, ones_log = [], []
    for head in range(2):
        base = 6 * head
        query_ref[head] = own_query(block_ref[...], head)
        key_ref[head] = own_key(block_ref[...], head)
        minus = jnp.where((lane >= base) & (lane < base + 3), -one, 0.0).astype(bf16)
        of_log = jnp.where((lane >= base + 3) & (lane < base + 6), one, 0.0).astype(bf16)
        ones_log.append(of_log)
        mine = lane // VDIM == head
        stats = stats_ref[:, LANES:].astype(f32)
        own = jnp.where(mine, stats_ref[:, 0:LANES], zero)
        value = jnp.where(mine, block_ref[:, VALUE], zero)
        grads_ref[head] = own
        vals_ref[head] = jnp.concatenate([value, minus], 1)
        dot = jnp.sum(jnp.where((lane >= base) & (lane < base + 3), stats, 0.0), 1, keepdims=True)
        log = jnp.sum(
            jnp.where((lane >= base + 3) & (lane < base + 6), stats, 0.0), 1, keepdims=True
        )
        logs.append((log, dot))
    dq_ref[...] = jnp.zeros_like(dq_ref)
    dk_ref[...] = jnp.zeros_like(dk_ref)
    dv_ref[...] = jnp.zeros_like(dv_ref)

    def load(first, second, pair_index, columns):
        at = pl.multiple_of(pair_index * rows, rows)
        return jnp.concatenate(
            [first[pl.ds(at, rows), columns], second[pl.ds(at, rows), columns]], 0
        )

    def query_side(index, visible):
        keys = load(same_ref, cross_ref, index, KEY)
        vals = load(same_ref, cross_ref, index, VALUE)
        for head in range(2):
            log, dot = logs[head]
            prob = jnp.exp(nt_dot(query_ref[head], keys) * score_scale - log)
            if visible is not None:
                prob = jnp.where(visible, prob, 0.0)
            grad_prob = nt_dot(grads_ref[head], vals)
            grad_score = (prob * (grad_prob - dot)).astype(bf16)
            dq_ref[head] += nn_dot(grad_score, keys)

    def key_side(index, visible):
        queries = load(same_ref, cross_ref, index, QUERY)
        grads = load(grad_same_ref, grad_cross_ref, index, slice(0, 2 * LANES))
        for head in range(2):
            log = nt_dot(ones_log[head], grads[:, LANES:])
            prob = jnp.exp(nt_dot(key_ref[head], queries) * score_scale - log)
            if visible is not None:
                prob = jnp.where(visible, prob, 0.0)
            dv_ref[head] += nn_dot(prob.astype(bf16), grads[:, 0:LANES])
            grad_prob = nt_dot(vals_ref[head], grads)
            grad_score = (prob * grad_prob).astype(bf16)
            dk_ref[head] += nn_dot(grad_score, queries)

    places = pair_places(rows, core)
    line = lax.broadcasted_iota(jnp.int32, (rows, 2 * rows), 0)
    query_side(pair, places <= line)
    key_side(pair, places >= line)

    def query_step(index, carry):
        query_side(index, None)
        return carry

    def key_step(index, carry):
        key_side(index, None)
        return carry

    lax.fori_loop(0, pair, query_step, 0)
    lax.fori_loop(pair + 1, same_ref.shape[0] // rows, key_step, 0)

    first = lane < NOPE
    query_nope_ref[...] = (
        score_scale * jnp.where(first, dq_ref[0, :, 0:LANES], dq_ref[1, :, 0:LANES])
    ).astype(bf16)
    rot = jnp.where(
        lane < ROPE, dq_ref[0, :, LANES:], pltpu.roll(dq_ref[1, :, LANES:], ROPE, 1)
    )
    query_rope_ref[...] = (score_scale * rot).astype(bf16)[:, 0 : 2 * ROPE]
    key_nope_ref[...] = (
        score_scale * jnp.where(first, dk_ref[0, :, LANES:], dk_ref[1, :, LANES:])
    ).astype(bf16)
    values_ref[...] = jnp.where(lane < VDIM, dv_ref[0], dv_ref[1]).astype(bf16)
    shared = pltpu.roll(dk_ref[0, :, 0:LANES], LANES - ROPE, 1) + pltpu.roll(
        dk_ref[1, :, 0:LANES], LANES - 2 * ROPE, 1
    )
    quarter = rows // 4
    packed = jnp.zeros((quarter, LANES), f32)
    small = lanes_of((quarter, LANES))
    for index in range(4):
        part = shared[index * quarter : (index + 1) * quarter]
        if index:
            part = pltpu.roll(part, index * ROPE, 1)
        packed = jnp.where(small // ROPE == index, part, packed)
    rope_ref[...] = (score_scale * packed).astype(bf16)


def rope_kernel(terms_ref, out_ref):
    total = terms_ref[0].astype(f32)
    for index in range(1, terms_ref.shape[0]):
        total = total + terms_ref[index].astype(f32)
    quarter = total.shape[0]
    for index in range(4):
        part = total if index == 0 else pltpu.roll(total, LANES - index * ROPE, 1)
        out_ref[index * quarter : (index + 1) * quarter, :] = part[:, 0:ROPE].astype(bf16)


def call(body, limit, outs, scratch=(), scalars=0, count=0):
    place = [pl.BlockSpec(memory_space=pltpu.SMEM)] * scalars
    return pl.pallas_call(
        body,
        out_shape=outs,
        in_specs=place + [pl.BlockSpec(memory_space=pltpu.VMEM)] * count,
        out_specs=jax.tree.map(lambda _: pl.BlockSpec(memory_space=pltpu.VMEM), outs),
        scratch_shapes=list(scratch),
        compiler_params=pltpu.CompilerParams(vmem_limit_bytes=limit * MIB),
    )


def shape_of(*dims, dtype=bf16):
    return jax.ShapeDtypeStruct(dims, dtype)


def exchange(blocks, axis, groups=None):
    return lax.all_to_all(blocks, axis, 0, 0, tiled=True, axis_index_groups=groups)


def per_device(
    hidden_in,
    query_nope,
    query_rope,
    key_nope,
    key_rope,
    values,
    norm_gain,
    expert_route,
    affinity,
    gate_weight,
    up_weight,
    down_weight,
    cotangent,
):
    rows, width = hidden_in.shape
    ctx_count, experts = lax.axis_size("ctx"), lax.axis_size("exp")
    half, quarter_ctx = ctx_count // 2, ctx_count // 4
    by_core = [[core + 2 * index for index in range(half)] for core in range(2)]
    by_four = [[part + 4 * index for index in range(quarter_ctx)] for part in range(4)]
    depth = experts * SLOT

    def swap(value, distance=1):
        route = [(index, index ^ distance) for index in range(ctx_count)]
        return lax.ppermute(value, "ctx", route)

    def spread(block, groups):
        count = len(groups[0])
        copies = jnp.broadcast_to(block[None], (count,) + block.shape)
        return exchange(copies, "ctx", groups)

    place = lax.axis_index("ctx").astype(jnp.int32).reshape(1)
    down = down_weight[0].reshape(-1, D // LANES, LANES).transpose(1, 0, 2).reshape(-1, LANES)
    weights = [jnp.concatenate([gate_weight[0], up_weight[0], down], 0)]
    weights.append(swap(weights[0]))
    block = jnp.concatenate(
        [key_nope, key_rope, query_rope, jnp.zeros((rows, ROPE), bf16), query_nope, values], 1
    )
    same = spread(block, by_core).reshape(half * rows, -1)
    cross = swap(same)
    far, same = lax.optimization_barrier((weights[0], same))
    weights.append(swap(far, 2))
    gain_row = norm_gain.reshape(1, width)

    attended, logs, send = call(
        functools.partial(forward_kernel, experts),
        14,
        (shape_of(rows, width), shape_of(rows, width, dtype=f32), shape_of(depth, 2 * width)),
        [pltpu.VMEM((2, rows, 2 * width), bf16)],
        1,
        8,
    )(
        place,
        same,
        cross,
        block,
        hidden_in,
        gain_row,
        expert_route.reshape(1, rows),
        affinity,
        cotangent,
    )
    received = exchange(send.reshape(experts, SLOT, 2 * width), "exp").reshape(depth, 2 * width)
    far, received = lax.optimization_barrier((weights[2], received))
    weights.append(swap(far))
    rows_all = spread(received, by_four)
    partial = call(expert_kernel, 32, shape_of(quarter_ctx, depth, 2 * width), count=5)(
        rows_all, *weights
    )
    terms = exchange(partial, "ctx", by_four)
    back = call(reduce_kernel, 10, shape_of(depth, 2 * width), count=2)(terms, received)
    home = exchange(back.reshape(experts, SLOT, 2 * width), "exp").reshape(depth, 2 * width)
    layer_out, grad_hidden, stats = call(
        functools.partial(combine_kernel, experts),
        6,
        (shape_of(rows, width), shape_of(rows, width), shape_of(rows, 2 * width)),
        count=7,
    )(home, hidden_in, attended, logs, expert_route.reshape(rows, 1), affinity, cotangent)
    grad_same = spread(stats, by_core).reshape(half * rows, -1)
    grad_cross = swap(grad_same)
    quarter = rows // 4
    gq_nope, gq_rope, gk_nope, g_values, rope_part = call(
        backward_kernel,
        20,
        (
            shape_of(rows, width),
            shape_of(rows, 2 * ROPE),
            shape_of(rows, width),
            shape_of(rows, width),
            shape_of(quarter, LANES),
        ),
        [
            pltpu.VMEM((2, rows, 2 * width), bf16),
            pltpu.VMEM((2, rows, 2 * width), bf16),
            pltpu.VMEM((2, rows, width), bf16),
            pltpu.VMEM((2, rows, 2 * width), bf16),
            pltpu.VMEM((2, rows, 2 * width), f32),
            pltpu.VMEM((2, rows, 2 * width), f32),
            pltpu.VMEM((2, rows, width), f32),
        ],
        1,
        6,
    )(place, same, cross, grad_same, grad_cross, block, stats)
    rope_terms = exchange(jnp.broadcast_to(rope_part[None], (experts, quarter, LANES)), "exp")
    gk_rope = call(rope_kernel, 4, shape_of(rows, ROPE), count=1)(rope_terms)
    return (layer_out, grad_hidden, gq_nope, gq_rope, gk_nope, gk_rope, g_values)


def solution(mesh):
    placed = (
        P("ctx", "exp"),
        P("ctx", "exp"),
        P("ctx", "exp"),
        P("ctx", "exp"),
        P("ctx", None),
        P("ctx", "exp"),
        P("exp"),
        P("ctx"),
        P("ctx", None),
        P("exp", None, "ctx"),
        P("exp", None, "ctx"),
        P("exp", "ctx", None),
        P("ctx", "exp"),
    )
    return jax.shard_map(
        per_device,
        mesh=mesh,
        in_specs=placed,
        out_specs=(
            P("ctx", "exp"),
            P("ctx", "exp"),
            P("ctx", "exp"),
            P("ctx", "exp"),
            P("ctx", "exp"),
            P("ctx", None),
            P("ctx", "exp"),
        ),
        check_vma=False,
    )
```

```python
import functools
import math

import jax
import jax.numpy as jnp
from jax import lax
from jax.experimental import pallas as pl
from jax.experimental.pallas import tpu as pltpu
from jax.sharding import PartitionSpec as P

NOPE = 64
ROPE = 32
VDIM = 64
D = 4096
CAP = 12
SLOT = 16
LANES = 128

norm_eps = 1e-06
route_scale = 2.5
masked_low = -1e30
score_scale = 1.0 / math.sqrt(NOPE + ROPE)

bf16 = jnp.bfloat16
f32 = jnp.float32
MIB = 1024 * 1024

KEY = slice(0, 256)
QUERY = slice(128, 384)
VALUE = slice(384, 512)


def nt_dot(a, b):
    return lax.dot_general(a, b, (((1,), (1,)), ((), ())), preferred_element_type=f32)


def nn_dot(a, b):
    return jnp.dot(a, b, preferred_element_type=f32)


def lanes_of(shape):
    return lax.broadcasted_iota(jnp.int32, shape, len(shape) - 1)


def pieces_of(value, count):
    pieces = []
    for _ in range(count):
        piece = value.astype(bf16).astype(f32)
        pieces.append(piece)
        value = value - piece
    return pieces


def own_query(block, head):
    rows = block.shape[0]
    lane = lanes_of((rows, LANES))
    zero = jnp.zeros((rows, LANES), bf16)
    nope = jnp.where(lane // NOPE == head, block[:, 256:384], zero)
    start = ROPE + head * ROPE
    rot = pltpu.roll(block[:, 128:256].astype(f32), LANES - start, 1)
    rot = jnp.where(lane < ROPE, rot, 0.0).astype(bf16)
    return jnp.concatenate([nope, rot], 1)


def own_key(block, head):
    rows = block.shape[0]
    lane = lanes_of((rows, LANES))
    zero = jnp.zeros((rows, LANES), bf16)
    nope = jnp.where(lane // NOPE == head, block[:, 0:128], zero)
    start = ROPE + head * ROPE
    rot = pltpu.roll(block[:, 128:256].astype(f32), start, 1)
    rot = jnp.where(lane // ROPE == 1 + head, rot, 0.0).astype(bf16)
    return jnp.concatenate([rot, nope], 1)


def pair_places(rows, core):
    lane = lanes_of((rows, 2 * rows))
    return lane - jnp.where(lane >= rows, 2 * rows, 0) * core


def slots_along_rows(route_row, experts):
    count = route_row.shape[1]
    hits = (lax.broadcasted_iota(jnp.int32, (experts, count), 0) == route_row).astype(f32)
    before = lax.broadcasted_iota(jnp.int32, (count, count), 0) < lanes_of((count, count))
    ranks = nn_dot(hits.astype(bf16), before.astype(f32).astype(bf16))
    rank = jnp.sum(ranks * hits, 0, keepdims=True)
    return route_row * SLOT + rank.astype(jnp.int32)


def column_of(row):
    count = row.shape[1]
    shape = (count, count)
    match = lax.broadcasted_iota(jnp.int32, shape, 0) == lanes_of(shape)
    return jnp.sum(jnp.where(match, row, jnp.zeros_like(row)), 1, keepdims=True)


def unit_matrix(rows, columns, offset=0):
    shape = (rows, columns)
    match = lax.broadcasted_iota(jnp.int32, shape, 0) + offset == lanes_of(shape)
    return match.astype(f32).astype(bf16)


def slots_along_columns(route_row, experts):
    route_column = column_of(route_row)
    count = route_column.shape[0]
    hits = (lanes_of((count, experts)) == route_column).astype(f32)
    before = lanes_of((count, count)) < lax.broadcasted_iota(jnp.int32, (count, count), 0)
    ranks = nn_dot(before.astype(f32).astype(bf16), hits.astype(bf16))
    rank = jnp.sum(ranks * hits, 1, keepdims=True)
    return route_column * SLOT + rank.astype(jnp.int32)


def gate_share_of(affinity):
    return column_of(route_scale * affinity[0:1] / jnp.sum(affinity, 0, keepdims=True))


def pack_kernel(key_nope_ref, key_rope_ref, query_rope_ref, query_nope_ref, values_ref, *outs):
    block_ref, copies_ref = outs
    rows = key_nope_ref.shape[0]
    rots = jnp.concatenate(
        [key_rope_ref[...], query_rope_ref[...], jnp.zeros((ROPE, rows), bf16)], 0
    )
    block_ref[:, 0:128] = key_nope_ref[...]
    block_ref[:, 128:256] = nt_dot(unit_matrix(rows, rows), rots).astype(bf16)
    block_ref[:, 256:384] = query_nope_ref[...]
    block_ref[:, 384:512] = values_ref[...]
    block = block_ref[...]
    for index in range(copies_ref.shape[0]):
        copies_ref[index] = block


def forward_kernel(
    experts,
    place_ref,
    same_ref,
    cross_ref,
    block_ref,
    hidden_ref,
    gain_ref,
    route_ref,
    affinity_ref,
    cotangent_ref,
    attended_ref,
    log_ref,
    send_ref,
    query_ref,
):
    rows = block_ref.shape[0]
    place = place_ref[0]
    pair, core = place // 2, place % 2
    for head in range(2):
        query_ref[head] = own_query(block_ref[...], head)

    def load(pair_index, columns):
        at = pl.multiple_of(pair_index * rows, rows)
        return jnp.concatenate(
            [same_ref[pl.ds(at, rows), columns], cross_ref[pl.ds(at, rows), columns]], 0
        )

    keys = load(pair, KEY)
    vals = load(pair, VALUE)
    visible = pair_places(rows, core) <= lax.broadcasted_iota(jnp.int32, (rows, 2 * rows), 0)
    state = []
    for head in range(2):
        scores = jnp.where(visible, nt_dot(query_ref[head], keys) * score_scale, masked_low)
        top = jnp.max(scores, 1, keepdims=True)
        weights = jnp.where(visible, jnp.exp(scores - top), 0.0)
        total = jnp.sum(weights, 1, keepdims=True)
        state.extend([top, total, nn_dot(weights.astype(bf16), vals)])

    def step(index, state):
        keys = load(index, KEY)
        vals = load(index, VALUE)
        after = []
        for head in range(2):
            top, total, mixed = state[3 * head : 3 * head + 3]
            scores = nt_dot(query_ref[head], keys) * score_scale
            new_top = jnp.maximum(top, jnp.max(scores, 1, keepdims=True))
            weights = jnp.exp(scores - new_top)
            factor = jnp.exp(top - new_top)
            total = total * factor + jnp.sum(weights, 1, keepdims=True)
            mixed = mixed * factor + nn_dot(weights.astype(bf16), vals)
            after.extend([new_top, total, mixed])
        return tuple(after)

    state = lax.fori_loop(0, pair, step, tuple(state))
    first = lanes_of((rows, LANES)) < VDIM
    attended = jnp.where(first, state[2] / state[1], state[5] / state[4]).astype(bf16)
    attended_ref[...] = attended
    log_ref[...] = jnp.where(
        first, state[0] + jnp.log(state[1]), state[3] + jnp.log(state[4])
    )
    hidden = hidden_ref[...].astype(f32) + attended.astype(f32)
    raised = (hidden * gain_ref[...]).astype(bf16)
    share = gate_share_of(affinity_ref[...])
    grad = (share * cotangent_ref[...].astype(f32)).astype(bf16)
    slots = slots_along_rows(route_ref[...], experts)
    table = lax.broadcasted_iota(jnp.int32, (experts * SLOT, rows), 0) == slots
    table = table.astype(f32).astype(bf16)
    row = lax.broadcasted_iota(jnp.int32, (SLOT, LANES), 0)
    gains = jnp.zeros((SLOT, LANES), f32)
    for index, piece in enumerate(pieces_of(gain_ref[...], 3)):
        gains = jnp.where(row == CAP + index, piece, gains)
    gains = jnp.broadcast_to(gains[None], (experts, SLOT, LANES)).reshape(-1, LANES)
    send_ref[:, 0:LANES] = (nn_dot(table, raised) + gains).astype(bf16)
    send_ref[:, LANES:] = nn_dot(table, grad).astype(bf16)


def gathered_rows(ref, count, slices, column):
    parts = []
    for index in range(slices):
        part = ref[:, index * SLOT : (index + 1) * SLOT, column : column + LANES]
        parts.append(part.reshape(count * SLOT, LANES))
    return jnp.concatenate(parts, 1)


def gain_of(raised):
    pieces = raised[CAP : CAP + 3].astype(f32)
    return pieces[0:1] + pieces[1:2] + pieces[2:3]


def inverse_of(raised, gain):
    hidden = raised.astype(f32) / gain
    return lax.rsqrt(jnp.sum(hidden * hidden, 1, keepdims=True) / D + norm_eps)


def expert_kernel(rows_ref, *refs):
    gates, ups, downs, out_ref = refs[0:2], refs[2:4], refs[4:6], refs[6]
    count, depth, _ = rows_ref.shape
    slices = depth // SLOT
    wide = 2 * LANES
    raised = gathered_rows(rows_ref, count, slices, 0)
    grad = gathered_rows(rows_ref, count, slices, LANES)
    inverse = inverse_of(raised, gain_of(raised[0:SLOT]))

    def columns_of(refs, index):
        at = slice(index * wide, (index + 1) * wide)
        return jnp.concatenate([ref[at, :] for ref in refs], 1)

    def rows_of(refs, index):
        at = slice(index * wide, (index + 1) * wide)
        return jnp.concatenate([ref[:, at] for ref in refs], 0)

    zero = jnp.zeros((count * SLOT, wide), f32)
    gate_val, up_val, grad_active = zero, zero, zero
    for index in range(slices // 2):
        at = slice(index * wide, (index + 1) * wide)
        gate_val = gate_val + nn_dot(raised[:, at], columns_of(gates, index))
        up_val = up_val + nn_dot(raised[:, at], columns_of(ups, index))
        grad_active = grad_active + nt_dot(grad[:, at], rows_of(downs, index))
    gate_val, up_val = inverse * gate_val, inverse * up_val
    sig = 1.0 / (1.0 + jnp.exp(-gate_val))
    silu = gate_val * sig
    active = (silu * up_val).astype(bf16)
    grad_gate = (grad_active * up_val * (sig * (1.0 + gate_val * (1.0 - sig)))).astype(bf16)
    grad_up = (grad_active * silu).astype(bf16)
    for index in range(slices // 2):
        out = nn_dot(active, rows_of(downs, index)).astype(bf16)
        back = nt_dot(grad_gate, columns_of(gates, index))
        back = (back + nt_dot(grad_up, columns_of(ups, index))).astype(bf16)
        for part in range(2):
            at = slice(part * LANES, (part + 1) * LANES)
            span = slice((2 * index + part) * SLOT, (2 * index + part + 1) * SLOT)
            out_ref[:, span, 0:LANES] = out[:, at].reshape(count, SLOT, LANES)
            out_ref[:, span, LANES:] = back[:, at].reshape(count, SLOT, LANES)


def reduce_kernel(terms_ref, rows_ref, out_ref):
    count, depth, _ = terms_ref.shape
    slices = depth // SLOT
    total = terms_ref[0].astype(f32)
    for index in range(1, count):
        total = total + terms_ref[index].astype(f32)
    raised = rows_ref[:, 0:LANES].astype(f32).reshape(slices, SLOT, LANES)
    back = total[:, LANES:].reshape(slices, SLOT, LANES)
    gain = jnp.sum(raised[:, CAP : CAP + 3, :], 1, keepdims=True)
    hidden = raised / gain
    squares = jnp.sum(jnp.sum(hidden * hidden, 0), 1, keepdims=True)
    inverse = lax.rsqrt(squares / D + norm_eps)
    cross = jnp.sum(jnp.sum(back * raised, 0), 1, keepdims=True) / D
    grad = inverse[None] * (back * gain - hidden * (inverse * inverse * cross)[None])
    row = lax.broadcasted_iota(jnp.int32, (slices, SLOT, LANES), 1)
    grad = jnp.where(row < CAP, grad, 0.0)
    out_ref[:, 0:LANES] = total[:, 0:LANES].astype(bf16)
    out_ref[:, LANES:] = grad.astype(bf16).reshape(depth, LANES)


def combine_kernel(
    experts,
    home_ref,
    hidden_ref,
    attended_ref,
    log_ref,
    route_ref,
    affinity_ref,
    cotangent_ref,
    layer_ref,
    grad_ref,
    stats_ref,
):
    rows = hidden_ref.shape[0]
    slots = slots_along_columns(route_ref[...], experts)
    table = (lanes_of((rows, experts * SLOT)) == slots).astype(f32).astype(bf16)
    token = nn_dot(table, home_ref[...])
    attended = attended_ref[...].astype(f32)
    hidden = hidden_ref[...].astype(f32) + attended
    share = gate_share_of(affinity_ref[...])
    layer_ref[...] = (hidden + share * token[:, 0:LANES]).astype(bf16)
    grad = (cotangent_ref[...].astype(f32) + token[:, LANES:]).astype(bf16)
    grad_ref[...] = grad
    product = grad.astype(f32) * attended
    lane = lanes_of((rows, LANES))
    columns = []
    for head in range(2):
        dot = jnp.sum(jnp.where(lane // VDIM == head, product, 0.0), 1, keepdims=True)
        columns += pieces_of(dot, 3)
        columns += pieces_of(log_ref[:, head * VDIM : head * VDIM + 1], 3)
    stats = jnp.zeros((rows, LANES), f32)
    for index, column in enumerate(columns):
        stats = jnp.where(lane == index, column, stats)
    stats = stats.astype(bf16)
    for index in range(stats_ref.shape[0]):
        stats_ref[index, :, 0:LANES] = grad
        stats_ref[index, :, LANES:] = stats


def backward_kernel(
    place_ref,
    same_ref,
    cross_ref,
    grad_same_ref,
    grad_cross_ref,
    block_ref,
    stats_ref,
    query_nope_ref,
    query_rope_ref,
    key_nope_ref,
    values_ref,
    rope_ref,
    query_ref,
    key_ref,
    grads_ref,
    vals_ref,
    dq_ref,
    dk_ref,
    dv_ref,
):
    rows = block_ref.shape[0]
    place = place_ref[0]
    pair, core = place // 2, place % 2
    lane = lanes_of((rows, LANES))
    zero = jnp.zeros((rows, LANES), bf16)
    one = jnp.ones((rows, LANES), f32)
    logs, ones_log = [], []
    for head in range(2):
        base = 6 * head
        query_ref[head] = own_query(block_ref[...], head)
        key_ref[head] = own_key(block_ref[...], head)
        minus = jnp.where((lane >= base) & (lane < base + 3), -one, 0.0).astype(bf16)
        of_log = jnp.where((lane >= base + 3) & (lane < base + 6), one, 0.0).astype(bf16)
        ones_log.append(of_log)
        mine = lane // VDIM == head
        stats = stats_ref[0, :, LANES:].astype(f32)
        own = jnp.where(mine, stats_ref[0, :, 0:LANES], zero)
        value = jnp.where(mine, block_ref[:, VALUE], zero)
        grads_ref[head] = own
        vals_ref[head] = jnp.concatenate([value, minus], 1)
        dot = jnp.sum(jnp.where((lane >= base) & (lane < base + 3), stats, 0.0), 1, keepdims=True)
        log = jnp.sum(
            jnp.where((lane >= base + 3) & (lane < base + 6), stats, 0.0), 1, keepdims=True
        )
        logs.append((log, dot))
    dq_ref[...] = jnp.zeros_like(dq_ref)
    dk_ref[...] = jnp.zeros_like(dk_ref)
    dv_ref[...] = jnp.zeros_like(dv_ref)

    def load(first, second, pair_index, columns):
        at = pl.multiple_of(pair_index * rows, rows)
        return jnp.concatenate(
            [first[pl.ds(at, rows), columns], second[pl.ds(at, rows), columns]], 0
        )

    def query_side(index, visible):
        keys = load(same_ref, cross_ref, index, KEY)
        vals = load(same_ref, cross_ref, index, VALUE)
        for head in range(2):
            log, dot = logs[head]
            prob = jnp.exp(nt_dot(query_ref[head], keys) * score_scale - log)
            if visible is not None:
                prob = jnp.where(visible, prob, 0.0)
            grad_prob = nt_dot(grads_ref[head], vals)
            grad_score = (prob * (grad_prob - dot)).astype(bf16)
            dq_ref[head] += nn_dot(grad_score, keys)

    def key_side(index, visible):
        queries = load(same_ref, cross_ref, index, QUERY)
        grads = load(grad_same_ref, grad_cross_ref, index, slice(0, 2 * LANES))
        for head in range(2):
            log = nt_dot(ones_log[head], grads[:, LANES:])
            prob = jnp.exp(nt_dot(key_ref[head], queries) * score_scale - log)
            if visible is not None:
                prob = jnp.where(visible, prob, 0.0)
            dv_ref[head] += nn_dot(prob.astype(bf16), grads[:, 0:LANES])
            grad_prob = nt_dot(vals_ref[head], grads)
            grad_score = (prob * grad_prob).astype(bf16)
            dk_ref[head] += nn_dot(grad_score, queries)

    places = pair_places(rows, core)
    line = lax.broadcasted_iota(jnp.int32, (rows, 2 * rows), 0)
    query_side(pair, places <= line)
    key_side(pair, places >= line)

    def query_step(index, carry):
        query_side(index, None)
        return carry

    def key_step(index, carry):
        key_side(index, None)
        return carry

    lax.fori_loop(0, pair, query_step, 0)
    lax.fori_loop(pair + 1, same_ref.shape[0] // rows, key_step, 0)

    first = lane < NOPE
    query_nope_ref[...] = (
        score_scale * jnp.where(first, dq_ref[0, :, 0:LANES], dq_ref[1, :, 0:LANES])
    ).astype(bf16)
    rot = jnp.where(
        lane < ROPE, dq_ref[0, :, LANES:], pltpu.roll(dq_ref[1, :, LANES:], ROPE, 1)
    )
    rot = (score_scale * rot).astype(bf16)
    query_rope_ref[...] = nt_dot(unit_matrix(2 * ROPE, LANES), rot).astype(bf16)
    key_nope_ref[...] = (
        score_scale * jnp.where(first, dk_ref[0, :, LANES:], dk_ref[1, :, LANES:])
    ).astype(bf16)
    values_ref[...] = jnp.where(lane < VDIM, dv_ref[0], dv_ref[1]).astype(bf16)
    shared = pltpu.roll(dk_ref[0, :, 0:LANES], LANES - ROPE, 1) + pltpu.roll(
        dk_ref[1, :, 0:LANES], LANES - 2 * ROPE, 1
    )
    quarter = rows // 4
    packed = jnp.zeros((quarter, LANES), f32)
    small = lanes_of((quarter, LANES))
    for index in range(4):
        part = shared[index * quarter : (index + 1) * quarter]
        if index:
            part = pltpu.roll(part, index * ROPE, 1)
        packed = jnp.where(small // ROPE == index, part, packed)
    packed = (score_scale * packed).astype(bf16)
    for index in range(rope_ref.shape[0]):
        rope_ref[index] = packed


def rope_kernel(terms_ref, out_ref):
    total = terms_ref[0].astype(f32)
    for index in range(1, terms_ref.shape[0]):
        total = total + terms_ref[index].astype(f32)
    total = total.astype(bf16)
    quarter = total.shape[0]
    out = jnp.zeros((ROPE, 4 * quarter), f32)
    for index in range(4):
        part = nt_dot(unit_matrix(ROPE, LANES, index * ROPE), total).astype(bf16)
        out = out + nn_dot(part, unit_matrix(quarter, 4 * quarter, index * quarter))
    out_ref[...] = out.astype(bf16)


def call(body, limit, outs, scratch=(), scalars=0, count=0):
    place = [pl.BlockSpec(memory_space=pltpu.SMEM)] * scalars
    return pl.pallas_call(
        body,
        out_shape=outs,
        in_specs=place + [pl.BlockSpec(memory_space=pltpu.VMEM)] * count,
        out_specs=jax.tree.map(lambda _: pl.BlockSpec(memory_space=pltpu.VMEM), outs),
        scratch_shapes=list(scratch),
        compiler_params=pltpu.CompilerParams(vmem_limit_bytes=limit * MIB),
    )


def shape_of(*dims, dtype=bf16):
    return jax.ShapeDtypeStruct(dims, dtype)


def exchange(blocks, axis, groups=None):
    return lax.all_to_all(blocks, axis, 0, 0, tiled=True, axis_index_groups=groups)


def per_device(
    hidden_in,
    query_nope,
    query_rope,
    key_nope,
    key_rope,
    values,
    norm_gain,
    expert_route,
    affinity,
    gate_weight,
    up_weight,
    down_weight,
    cotangent,
):
    rows, width = hidden_in.shape
    ctx_count, experts = lax.axis_size("ctx"), lax.axis_size("exp")
    half = ctx_count // 2
    by_core = [[core + 2 * index for index in range(half)] for core in range(2)]
    across = [(index, index ^ 1) for index in range(ctx_count)]
    depth = experts * SLOT
    quarter = rows // 4

    def swap(value):
        return lax.ppermute(value, "ctx", across)

    place = lax.axis_index("ctx").astype(jnp.int32).reshape(1)
    route = expert_route.reshape(1, rows)
    affinity = affinity.T
    weights = []
    for weight in (gate_weight[0], up_weight[0], down_weight[0]):
        weights += [weight, swap(weight)]
    block, copies = call(
        pack_kernel, 8, (shape_of(rows, 512), shape_of(half, rows, 512)), count=5
    )(key_nope, key_rope.T, query_rope.T, query_nope, values)
    same = exchange(copies, "ctx", by_core)
    same, weights = lax.optimization_barrier((same, weights))
    same = same.reshape(half * rows, -1)
    cross = swap(same)

    attended, logs, send = call(
        functools.partial(forward_kernel, experts),
        14,
        (shape_of(rows, width), shape_of(rows, width, dtype=f32), shape_of(depth, 2 * width)),
        [pltpu.VMEM((2, rows, 2 * width), bf16)],
        1,
        8,
    )(
        place,
        same,
        cross,
        block,
        hidden_in,
        norm_gain.reshape(1, width),
        route,
        affinity,
        cotangent,
    )
    received = exchange(send.reshape(experts, SLOT, 2 * width), "exp").reshape(depth, 2 * width)
    copies = jnp.broadcast_to(received[None], (half, depth, 2 * width))
    rows_all = exchange(copies, "ctx", by_core)
    partial = call(expert_kernel, 28, shape_of(half, depth, 2 * width), count=7)(
        rows_all, *weights
    )
    terms = exchange(partial, "ctx", by_core)
    back = call(reduce_kernel, 10, shape_of(depth, 2 * width), count=2)(terms, received)
    home = exchange(back.reshape(experts, SLOT, 2 * width), "exp").reshape(depth, 2 * width)
    layer_out, grad_hidden, stats = call(
        functools.partial(combine_kernel, experts),
        8,
        (shape_of(rows, width), shape_of(rows, width), shape_of(half, rows, 2 * width)),
        count=7,
    )(home, hidden_in, attended, logs, route, affinity, cotangent)
    grad_same = exchange(stats, "ctx", by_core).reshape(half * rows, -1)
    grad_cross = swap(grad_same)
    *grads, rope_part = call(
        backward_kernel,
        20,
        (
            shape_of(rows, width),
            shape_of(2 * ROPE, rows),
            shape_of(rows, width),
            shape_of(rows, width),
            shape_of(experts, quarter, LANES),
        ),
        [
            pltpu.VMEM((2, rows, 2 * width), bf16),
            pltpu.VMEM((2, rows, 2 * width), bf16),
            pltpu.VMEM((2, rows, width), bf16),
            pltpu.VMEM((2, rows, 2 * width), bf16),
            pltpu.VMEM((2, rows, 2 * width), f32),
            pltpu.VMEM((2, rows, 2 * width), f32),
            pltpu.VMEM((2, rows, width), f32),
        ],
        1,
        6,
    )(place, same, cross, grad_same, grad_cross, block, stats)
    grads, layer_out, grad_hidden, rope_part = lax.optimization_barrier(
        (grads, layer_out, grad_hidden, rope_part)
    )
    rope_terms = exchange(rope_part, "exp")
    grads, layer_out, grad_hidden, rope_terms = lax.optimization_barrier(
        (grads, layer_out, grad_hidden, rope_terms)
    )
    gk_rope = call(rope_kernel, 4, shape_of(ROPE, rows), count=1)(rope_terms)
    gq_nope, gq_rope, gk_nope, g_values = grads
    return (layer_out, grad_hidden, gq_nope, gq_rope.T, gk_nope, gk_rope.T, g_values)


def solution(mesh):
    placed = (
        P("ctx", "exp"),
        P("ctx", "exp"),
        P("ctx", "exp"),
        P("ctx", "exp"),
        P("ctx", None),
        P("ctx", "exp"),
        P("exp"),
        P("ctx"),
        P("ctx", None),
        P("exp", None, "ctx"),
        P("exp", None, "ctx"),
        P("exp", "ctx", None),
        P("ctx", "exp"),
    )
    return jax.shard_map(
        per_device,
        mesh=mesh,
        in_specs=placed,
        out_specs=(
            P("ctx", "exp"),
            P("ctx", "exp"),
            P("ctx", "exp"),
            P("ctx", "exp"),
            P("ctx", "exp"),
            P("ctx", None),
            P("ctx", "exp"),
        ),
        check_vma=False,
    )
```

```python
import functools
import math

import jax
import jax.numpy as jnp
from jax import lax
from jax.experimental import pallas as pl
from jax.experimental.pallas import tpu as pltpu
from jax.sharding import PartitionSpec as P

NOPE = 64
ROPE = 32
VDIM = 64
D = 4096
CAP = 12
SLOT = 16
LANES = 128

norm_eps = 1e-06
route_scale = 2.5
masked_low = -1e30
score_scale = 1.0 / math.sqrt(NOPE + ROPE)

bf16 = jnp.bfloat16
f32 = jnp.float32
MIB = 1024 * 1024

LEFT = slice(0, LANES)
RIGHT = slice(LANES, 2 * LANES)


def nt_dot(a, b):
    return lax.dot_general(a, b, (((1,), (1,)), ((), ())), preferred_element_type=f32)


def nn_dot(a, b):
    return jnp.dot(a, b, preferred_element_type=f32)


def lanes_of(shape):
    return lax.broadcasted_iota(jnp.int32, shape, len(shape) - 1)


def pieces_of(value, count):
    pieces = []
    for _ in range(count):
        piece = value.astype(bf16).astype(f32)
        pieces.append(piece)
        value = value - piece
    return pieces


def own_query(queries, head):
    rows = queries.shape[0]
    lane = lanes_of((rows, LANES))
    nope = jnp.where(lane // NOPE == head, queries[:, LEFT], jnp.zeros((rows, LANES), bf16))
    rot = queries[:, RIGHT].astype(f32)
    if head:
        rot = pltpu.roll(rot, LANES - head * ROPE, 1)
    rot = jnp.where(lane < ROPE, rot, 0.0).astype(bf16)
    return jnp.concatenate([nope, rot], 1)


def own_key(keys, head):
    rows = keys.shape[0]
    lane = lanes_of((rows, LANES))
    nope = jnp.where(lane // NOPE == head, keys[:, LEFT], jnp.zeros((rows, LANES), bf16))
    rot = keys[:, RIGHT].astype(f32)
    if head:
        rot = pltpu.roll(rot, head * ROPE, 1)
    return jnp.concatenate([nope, rot.astype(bf16)], 1)


def upright(narrow):
    count, rows = narrow.shape
    full = jnp.concatenate([narrow, jnp.zeros((LANES - count, rows), bf16)], 0)
    return nt_dot(unit_matrix(rows, rows), full).astype(bf16)


def keys_of(message, rows):
    rot = upright(message[rows : rows + ROPE, :][:, 0:rows])
    return jnp.concatenate([message[0:rows, LEFT], rot], 1)


def pair_places(rows, core):
    lane = lanes_of((rows, 2 * rows))
    return lane - jnp.where(lane >= rows, 2 * rows, 0) * core


def slots_along_rows(route_row, experts):
    count = route_row.shape[1]
    hits = (lax.broadcasted_iota(jnp.int32, (experts, count), 0) == route_row).astype(f32)
    before = lax.broadcasted_iota(jnp.int32, (count, count), 0) < lanes_of((count, count))
    ranks = nn_dot(hits.astype(bf16), before.astype(f32).astype(bf16))
    rank = jnp.sum(ranks * hits, 0, keepdims=True)
    return route_row * SLOT + rank.astype(jnp.int32)


def column_of(row):
    count = row.shape[1]
    shape = (count, count)
    match = lax.broadcasted_iota(jnp.int32, shape, 0) == lanes_of(shape)
    return jnp.sum(jnp.where(match, row, jnp.zeros_like(row)), 1, keepdims=True)


def unit_matrix(rows, columns, offset=0):
    shape = (rows, columns)
    match = lax.broadcasted_iota(jnp.int32, shape, 0) + offset == lanes_of(shape)
    return match.astype(f32).astype(bf16)


def slots_along_columns(route_row, experts):
    route_column = column_of(route_row)
    count = route_column.shape[0]
    hits = (lanes_of((count, experts)) == route_column).astype(f32)
    before = lanes_of((count, count)) < lax.broadcasted_iota(jnp.int32, (count, count), 0)
    ranks = nn_dot(before.astype(f32).astype(bf16), hits.astype(bf16))
    rank = jnp.sum(ranks * hits, 1, keepdims=True)
    return route_column * SLOT + rank.astype(jnp.int32)


def gate_share_of(affinity):
    return column_of(route_scale * affinity[0:1] / jnp.sum(affinity, 0, keepdims=True))


def pack_kernel(
    place_ref,
    key_nope_hbm,
    key_rope_hbm,
    query_rope_hbm,
    query_nope_hbm,
    values_hbm,
    gate_hbm,
    up_hbm,
    down_hbm,
    own_key_ref,
    own_query_ref,
    message_ref,
    weights_ref,
    key_nope_ref,
    key_rope_ref,
    query_rope_ref,
    query_nope_ref,
    values_ref,
    sems,
):
    pairs = (
        (key_rope_hbm, key_rope_ref),
        (query_rope_hbm, query_rope_ref),
        (key_nope_hbm, key_nope_ref),
        (values_hbm, values_ref),
        (query_nope_hbm, query_nope_ref),
    )
    copies = [
        pltpu.make_async_copy(source, target, sems.at[index])
        for index, (source, target) in enumerate(pairs)
    ]
    moves = [(gate_hbm, weights_ref.at[0:D, :]), (up_hbm, weights_ref.at[D : 2 * D, :])]
    for index in range(D // LANES):
        start = 2 * D + index * LANES
        source = down_hbm.at[:, index * LANES : (index + 1) * LANES]
        moves.append((source, weights_ref.at[start : start + LANES, :]))
    moves = [
        pltpu.make_async_copy(source, target, sems.at[len(pairs) + index])
        for index, (source, target) in enumerate(moves)
    ]
    for copy in copies + moves:
        copy.start()
    for copy in copies:
        copy.wait()
    rows = key_nope_ref.shape[0]
    place = place_ref[0]
    pair, core = place // 2, place % 2
    own_key_ref[:, LEFT] = key_nope_ref[...]
    own_key_ref[:, RIGHT] = upright(key_rope_ref[...])
    own_query_ref[:, LEFT] = query_nope_ref[...]
    own_query_ref[:, RIGHT] = upright(query_rope_ref[...])
    rot = jnp.concatenate([key_rope_ref[...], jnp.zeros((ROPE, 2 * LANES - rows), bf16)], 1)
    empty = jnp.zeros((ROPE, 2 * LANES), bf16)
    for index in range(message_ref.shape[0]):
        to_later = (index > pair) | ((index == pair) & (core == 0))

        @pl.when(to_later)
        def _():
            message_ref[index, 0:rows, LEFT] = key_nope_ref[...]
            message_ref[index, 0:rows, RIGHT] = values_ref[...]
            message_ref[index, rows:, :] = rot

        @pl.when(jnp.logical_not(to_later))
        def _():
            message_ref[index, 0:rows, :] = own_query_ref[...]
            message_ref[index, rows:, :] = empty

    for copy in moves:
        copy.wait()


def forward_kernel(
    experts,
    place_ref,
    same_ref,
    cross_ref,
    own_key_ref,
    own_query_ref,
    values_ref,
    hidden_ref,
    gain_ref,
    route_ref,
    affinity_ref,
    cotangent_ref,
    attended_ref,
    log_ref,
    send_ref,
    query_ref,
):
    rows = own_key_ref.shape[0]
    place = place_ref[0]
    pair, core = place // 2, place % 2
    for head in range(2):
        query_ref[head] = own_query(own_query_ref[...], head)

    cross = cross_ref[pair]
    keys = jnp.concatenate([own_key_ref[...], keys_of(cross, rows)], 0)
    vals = jnp.concatenate([values_ref[...], cross[0:rows, RIGHT]], 0)
    visible = pair_places(rows, core) <= lax.broadcasted_iota(jnp.int32, (rows, 2 * rows), 0)
    state = []
    for head in range(2):
        scores = jnp.where(visible, nt_dot(query_ref[head], keys) * score_scale, masked_low)
        top = jnp.max(scores, 1, keepdims=True)
        weights = jnp.where(visible, jnp.exp(scores - top), 0.0)
        total = jnp.sum(weights, 1, keepdims=True)
        state.extend([top, total, nn_dot(weights.astype(bf16), vals)])

    def step(index, state):
        same, cross = same_ref[index], cross_ref[index]
        keys = jnp.concatenate([keys_of(same, rows), keys_of(cross, rows)], 0)
        vals = jnp.concatenate([same[0:rows, RIGHT], cross[0:rows, RIGHT]], 0)
        after = []
        for head in range(2):
            top, total, mixed = state[3 * head : 3 * head + 3]
            scores = nt_dot(query_ref[head], keys) * score_scale
            new_top = jnp.maximum(top, jnp.max(scores, 1, keepdims=True))
            weights = jnp.exp(scores - new_top)
            factor = jnp.exp(top - new_top)
            total = total * factor + jnp.sum(weights, 1, keepdims=True)
            mixed = mixed * factor + nn_dot(weights.astype(bf16), vals)
            after.extend([new_top, total, mixed])
        return tuple(after)

    state = lax.fori_loop(0, pair, step, tuple(state))
    first = lanes_of((rows, LANES)) < VDIM
    attended = jnp.where(first, state[2] / state[1], state[5] / state[4]).astype(bf16)
    attended_ref[...] = attended
    log_ref[...] = jnp.where(
        first, state[0] + jnp.log(state[1]), state[3] + jnp.log(state[4])
    )
    hidden = hidden_ref[...].astype(f32) + attended.astype(f32)
    raised = (hidden * gain_ref[...]).astype(bf16)
    share = gate_share_of(affinity_ref[...])
    grad = (share * cotangent_ref[...].astype(f32)).astype(bf16)
    slots = slots_along_rows(route_ref[...], experts)
    table = lax.broadcasted_iota(jnp.int32, (experts * SLOT, rows), 0) == slots
    table = table.astype(f32).astype(bf16)
    row = lax.broadcasted_iota(jnp.int32, (SLOT, LANES), 0)
    gains = jnp.zeros((SLOT, LANES), f32)
    for index, piece in enumerate(pieces_of(gain_ref[...], 3)):
        gains = jnp.where(row == CAP + index, piece, gains)
    gains = jnp.broadcast_to(gains[None], (experts, SLOT, LANES)).reshape(-1, LANES)
    send_ref[:, 0:LANES] = (nn_dot(table, raised) + gains).astype(bf16)
    send_ref[:, LANES:] = nn_dot(table, grad).astype(bf16)


def gathered_rows(ref, count, slices, column):
    parts = []
    for index in range(slices):
        part = ref[:, index * SLOT : (index + 1) * SLOT, column : column + LANES]
        parts.append(part.reshape(count * SLOT, LANES))
    return jnp.concatenate(parts, 1)


def gain_of(raised):
    pieces = raised[CAP : CAP + 3].astype(f32)
    return pieces[0:1] + pieces[1:2] + pieces[2:3]


def inverse_of(raised, gain):
    hidden = raised.astype(f32) / gain
    return lax.rsqrt(jnp.sum(hidden * hidden, 1, keepdims=True) / D + norm_eps)


def expert_kernel(rows_ref, *refs):
    weight_refs, out_ref = refs[:-1], refs[-1]
    count, depth, _ = rows_ref.shape
    slices = depth // SLOT
    wide = 2 * LANES
    raised = gathered_rows(rows_ref, count, slices, 0)
    grad = gathered_rows(rows_ref, count, slices, LANES)
    inverse = inverse_of(raised, gain_of(raised[0:SLOT]))
    pairs = [weight_refs[at : at + 2] for at in range(0, len(weight_refs), 2)]

    def side_by_side(pair, base, index):
        at = slice(base + index * wide, base + (index + 1) * wide)
        return jnp.concatenate([pair[0][at, :], pair[1][at, :]], 1)

    def down_block(pair, index):
        at = 2 * D + index * wide
        halves = [
            jnp.concatenate([ref[at : at + LANES, :], ref[at + LANES : at + wide, :]], 1)
            for ref in pair
        ]
        return jnp.concatenate(halves, 0)

    made = []
    for pair in pairs:
        zero = jnp.zeros((count * SLOT, wide), f32)
        gate_val, up_val, grad_active = zero, zero, zero
        for index in range(slices // 2):
            at = slice(index * wide, (index + 1) * wide)
            gate_val = gate_val + nn_dot(raised[:, at], side_by_side(pair, 0, index))
            up_val = up_val + nn_dot(raised[:, at], side_by_side(pair, D, index))
            grad_active = grad_active + nt_dot(grad[:, at], down_block(pair, index))
        gate_val, up_val = inverse * gate_val, inverse * up_val
        sig = 1.0 / (1.0 + jnp.exp(-gate_val))
        silu = gate_val * sig
        active = (silu * up_val).astype(bf16)
        grad_gate = (grad_active * up_val * (sig * (1.0 + gate_val * (1.0 - sig)))).astype(bf16)
        grad_up = (grad_active * silu).astype(bf16)
        made.append((active, grad_gate, grad_up))
    for index in range(slices // 2):
        out = jnp.zeros((count * SLOT, wide), f32)
        back = jnp.zeros((count * SLOT, wide), f32)
        for pair, (active, grad_gate, grad_up) in zip(pairs, made):
            out = out + nn_dot(active, down_block(pair, index))
            back = back + nt_dot(grad_gate, side_by_side(pair, 0, index))
            back = back + nt_dot(grad_up, side_by_side(pair, D, index))
        out, back = out.astype(bf16), back.astype(bf16)
        for part in range(2):
            at = slice(part * LANES, (part + 1) * LANES)
            span = slice((2 * index + part) * SLOT, (2 * index + part + 1) * SLOT)
            out_ref[:, span, 0:LANES] = out[:, at].reshape(count, SLOT, LANES)
            out_ref[:, span, LANES:] = back[:, at].reshape(count, SLOT, LANES)


def reduce_kernel(terms_ref, rows_ref, out_ref):
    count, depth, _ = terms_ref.shape
    slices = depth // SLOT
    total = terms_ref[0].astype(f32)
    for index in range(1, count):
        total = total + terms_ref[index].astype(f32)
    raised = rows_ref[:, 0:LANES].astype(f32).reshape(slices, SLOT, LANES)
    back = total[:, LANES:].reshape(slices, SLOT, LANES)
    gain = jnp.sum(raised[:, CAP : CAP + 3, :], 1, keepdims=True)
    hidden = raised / gain
    squares = jnp.sum(jnp.sum(hidden * hidden, 0), 1, keepdims=True)
    inverse = lax.rsqrt(squares / D + norm_eps)
    cross = jnp.sum(jnp.sum(back * raised, 0), 1, keepdims=True) / D
    grad = inverse[None] * (back * gain - hidden * (inverse * inverse * cross)[None])
    row = lax.broadcasted_iota(jnp.int32, (slices, SLOT, LANES), 1)
    grad = jnp.where(row < CAP, grad, 0.0)
    out_ref[:, 0:LANES] = total[:, 0:LANES].astype(bf16)
    out_ref[:, LANES:] = grad.astype(bf16).reshape(depth, LANES)


def combine_kernel(
    experts,
    home_ref,
    hidden_ref,
    attended_ref,
    log_ref,
    route_ref,
    affinity_ref,
    cotangent_ref,
    layer_ref,
    grad_ref,
    stats_ref,
    message_ref,
):
    rows = hidden_ref.shape[0]
    slots = slots_along_columns(route_ref[...], experts)
    table = (lanes_of((rows, experts * SLOT)) == slots).astype(f32).astype(bf16)
    token = nn_dot(table, home_ref[...])
    attended = attended_ref[...].astype(f32)
    hidden = hidden_ref[...].astype(f32) + attended
    share = gate_share_of(affinity_ref[...])
    layer_ref[...] = (hidden + share * token[:, 0:LANES]).astype(bf16)
    grad = (cotangent_ref[...].astype(f32) + token[:, LANES:]).astype(bf16)
    grad_ref[...] = grad
    product = grad.astype(f32) * attended
    lane = lanes_of((rows, LANES))
    stats, pieces = jnp.zeros((rows, LANES), f32), jnp.zeros((rows, LANES), f32)
    for head in range(2):
        dot = jnp.sum(jnp.where(lane // VDIM == head, product, 0.0), 1, keepdims=True)
        log = log_ref[:, head * VDIM : head * VDIM + 1]
        stats = jnp.where(lane == 2 * head, dot, jnp.where(lane == 2 * head + 1, log, stats))
        for index, piece in enumerate(pieces_of(dot, 3) + pieces_of(log, 3)):
            pieces = jnp.where(lane == 6 * head + index, piece, pieces)
    stats_ref[...] = stats
    pieces = jnp.concatenate(
        [pieces.astype(bf16), jnp.zeros((2 * LANES - rows, LANES), bf16)], 0
    )
    lines = nt_dot(unit_matrix(SLOT, LANES), pieces).astype(bf16)
    for index in range(message_ref.shape[0]):
        message_ref[index, 0:rows, :] = grad
        message_ref[index, rows : rows + SLOT, :] = lines[:, LEFT]
        message_ref[index, rows + SLOT :, :] = lines[:, RIGHT]


def query_kernel(
    place_ref,
    same_ref,
    cross_ref,
    own_key_ref,
    own_query_ref,
    values_ref,
    grad_ref,
    stats_ref,
    query_nope_ref,
    query_rope_ref,
    query_ref,
    grads_ref,
    dq_ref,
):
    rows = own_key_ref.shape[0]
    place = place_ref[0]
    pair, core = place // 2, place % 2
    lane = lanes_of((rows, LANES))
    for head in range(2):
        query_ref[head] = own_query(own_query_ref[...], head)
        grads_ref[head] = jnp.where(
            lane // VDIM == head, grad_ref[...], jnp.zeros((rows, LANES), bf16)
        )

    def part(head, keys, vals, visible):
        dot = stats_ref[:, 2 * head : 2 * head + 1]
        log = stats_ref[:, 2 * head + 1 : 2 * head + 2]
        prob = jnp.exp(nt_dot(query_ref[head], keys) * score_scale - log)
        if visible is not None:
            prob = jnp.where(visible, prob, 0.0)
        grad_prob = nt_dot(grads_ref[head], vals)
        grad_score = (prob * (grad_prob - dot)).astype(bf16)
        return nn_dot(grad_score, keys)

    cross = cross_ref[pair]
    keys = jnp.concatenate([own_key_ref[...], keys_of(cross, rows)], 0)
    vals = jnp.concatenate([values_ref[...], cross[0:rows, RIGHT]], 0)
    visible = pair_places(rows, core) <= lax.broadcasted_iota(jnp.int32, (rows, 2 * rows), 0)
    for head in range(2):
        dq_ref[head] = part(head, keys, vals, visible)

    def step(index, carry):
        same, cross = same_ref[index], cross_ref[index]
        keys = jnp.concatenate([keys_of(same, rows), keys_of(cross, rows)], 0)
        vals = jnp.concatenate([same[0:rows, RIGHT], cross[0:rows, RIGHT]], 0)
        for head in range(2):
            dq_ref[head] += part(head, keys, vals, None)
        return carry

    lax.fori_loop(0, pair, step, 0)
    query_nope_ref[...] = (
        score_scale * jnp.where(lane < NOPE, dq_ref[0, :, LEFT], dq_ref[1, :, LEFT])
    ).astype(bf16)
    rot = jnp.where(lane < ROPE, dq_ref[0, :, RIGHT], pltpu.roll(dq_ref[1, :, RIGHT], ROPE, 1))
    rot = (score_scale * rot).astype(bf16)
    query_rope_ref[...] = nt_dot(unit_matrix(2 * ROPE, LANES), rot).astype(bf16)


def key_kernel(
    place_ref,
    same_ref,
    cross_ref,
    grad_same_ref,
    grad_cross_ref,
    own_key_ref,
    own_query_ref,
    values_ref,
    own_grad_ref,
    key_nope_ref,
    grad_values_ref,
    rope_ref,
    key_ref,
    vals_ref,
    dk_ref,
    dv_ref,
):
    rows = own_key_ref.shape[0]
    place = place_ref[0]
    pair, core = place // 2, place % 2
    lane = lanes_of((rows, LANES))
    for head in range(2):
        key_ref[head] = own_key(own_key_ref[...], head)
        vals_ref[head] = jnp.where(
            lane // VDIM == head, values_ref[...], jnp.zeros((rows, LANES), bf16)
        )

    def lines_of(first, second):
        zero = jnp.zeros((SLOT, LANES), f32)
        parts = []
        for message in (first, second):
            low = message[rows : rows + SLOT].astype(f32)
            high = message[rows + SLOT :].astype(f32)
            parts.append(jnp.concatenate([low, high, zero], 1))
        moved = pltpu.roll(parts[1], rows, 1)
        return jnp.where(lanes_of(moved.shape) < rows, parts[0], moved)

    def part(head, queries, grads, lines, visible):
        at = 6 * head
        dot = lines[at : at + 1] + lines[at + 1 : at + 2] + lines[at + 2 : at + 3]
        log = lines[at + 3 : at + 4] + lines[at + 4 : at + 5] + lines[at + 5 : at + 6]
        prob = jnp.exp(nt_dot(key_ref[head], queries) * score_scale - log)
        if visible is not None:
            prob = jnp.where(visible, prob, 0.0)
        grad_prob = nt_dot(vals_ref[head], grads)
        grad_score = (prob * (grad_prob - dot)).astype(bf16)
        return nn_dot(grad_score, queries), nn_dot(prob.astype(bf16), grads)

    def both(first, second, first_grad, second_grad, visible):
        queries = jnp.concatenate([first, second], 0)
        grads = jnp.concatenate([first_grad[0:rows], second_grad[0:rows]], 0)
        lines = lines_of(first_grad, second_grad)
        return [part(head, queries, grads, lines, visible) for head in range(2)]

    visible = pair_places(rows, core) >= lax.broadcasted_iota(jnp.int32, (rows, 2 * rows), 0)
    made = both(
        own_query_ref[...],
        cross_ref[pair][0:rows],
        own_grad_ref[0],
        grad_cross_ref[pair],
        visible,
    )
    for head in range(2):
        dk_ref[head], dv_ref[head] = made[head]

    def step(index, carry):
        made = both(
            same_ref[index][0:rows],
            cross_ref[index][0:rows],
            grad_same_ref[index],
            grad_cross_ref[index],
            None,
        )
        for head in range(2):
            dk_ref[head] += made[head][0]
            dv_ref[head] += made[head][1]
        return carry

    lax.fori_loop(pair + 1, same_ref.shape[0], step, 0)
    key_nope_ref[...] = (
        score_scale * jnp.where(lane < NOPE, dk_ref[0, :, LEFT], dk_ref[1, :, LEFT])
    ).astype(bf16)
    grad_values_ref[...] = jnp.where(lane < VDIM, dv_ref[0], dv_ref[1]).astype(bf16)
    shared = dk_ref[0, :, RIGHT] + pltpu.roll(dk_ref[1, :, RIGHT], LANES - ROPE, 1)
    quarter = rows // 4
    packed = jnp.zeros((quarter, LANES), f32)
    small = lanes_of((quarter, LANES))
    for index in range(4):
        piece = shared[index * quarter : (index + 1) * quarter]
        if index:
            piece = pltpu.roll(piece, index * ROPE, 1)
        packed = jnp.where(small // ROPE == index, piece, packed)
    packed = (score_scale * packed).astype(bf16)
    for index in range(rope_ref.shape[0]):
        rope_ref[index] = packed


def rope_kernel(terms_ref, out_ref):
    total = terms_ref[0].astype(f32)
    for index in range(1, terms_ref.shape[0]):
        total = total + terms_ref[index].astype(f32)
    total = total.astype(bf16)
    quarter = total.shape[0]
    out = jnp.zeros((ROPE, 4 * quarter), f32)
    for index in range(4):
        part = nt_dot(unit_matrix(ROPE, LANES, index * ROPE), total).astype(bf16)
        out = out + nn_dot(part, unit_matrix(quarter, 4 * quarter, index * quarter))
    out_ref[...] = out.astype(bf16)


def call(body, limit, outs, scratch=(), scalars=0, count=0, space=pltpu.VMEM):
    place = [pl.BlockSpec(memory_space=pltpu.SMEM)] * scalars
    return pl.pallas_call(
        body,
        out_shape=outs,
        in_specs=place + [pl.BlockSpec(memory_space=space)] * count,
        out_specs=jax.tree.map(lambda _: pl.BlockSpec(memory_space=pltpu.VMEM), outs),
        scratch_shapes=list(scratch),
        compiler_params=pltpu.CompilerParams(vmem_limit_bytes=limit * MIB),
    )


def shape_of(*dims, dtype=bf16):
    return jax.ShapeDtypeStruct(dims, dtype)


def held(value):
    return pltpu.with_memory_space_constraint(value, pltpu.HBM)


def exchange(blocks, axis, groups=None):
    return lax.all_to_all(blocks, axis, 0, 0, tiled=True, axis_index_groups=groups)


def per_device(
    hidden_in,
    query_nope,
    query_rope,
    key_nope,
    key_rope,
    values,
    norm_gain,
    expert_route,
    affinity,
    gate_weight,
    up_weight,
    down_weight,
    cotangent,
):
    rows, width = hidden_in.shape
    ctx_count, experts = lax.axis_size("ctx"), lax.axis_size("exp")
    half = ctx_count // 2
    by_core = [[core + 2 * index for index in range(half)] for core in range(2)]
    across = [(index, index ^ 1) for index in range(ctx_count)]
    depth = experts * SLOT
    quarter = rows // 4

    def swap(value):
        return lax.ppermute(value, "ctx", across)

    place = lax.axis_index("ctx").astype(jnp.int32).reshape(1)
    route = expert_route.reshape(1, rows)
    affinity = affinity.T
    tall = rows + ROPE
    own_key_rows, own_query_rows, messages, weights = call(
        pack_kernel,
        12,
        (
            shape_of(rows, 2 * width),
            shape_of(rows, 2 * width),
            shape_of(half, tall, 2 * width),
            shape_of(3 * D, LANES),
        ),
        [
            pltpu.VMEM((rows, width), bf16),
            pltpu.VMEM((ROPE, rows), bf16),
            pltpu.VMEM((2 * ROPE, rows), bf16),
            pltpu.VMEM((rows, width), bf16),
            pltpu.VMEM((rows, width), bf16),
            pltpu.SemaphoreType.DMA((7 + D // LANES,)),
        ],
        1,
        8,
        pltpu.HBM,
    )(
        place,
        *(held(value) for value in (key_nope, key_rope.T, query_rope.T, query_nope, values)),
        *(held(value[0]) for value in (gate_weight, up_weight, down_weight)),
    )
    own = (own_key_rows, own_query_rows, held(values))
    same = exchange(messages, "ctx", by_core)
    weights = (weights, swap(weights))
    same, weights = lax.optimization_barrier((same, weights))
    cross = swap(same)

    attended, logs, send = call(
        functools.partial(forward_kernel, experts),
        14,
        (shape_of(rows, width), shape_of(rows, width, dtype=f32), shape_of(depth, 2 * width)),
        [pltpu.VMEM((2, rows, 2 * width), bf16)],
        1,
        10,
    )(
        place,
        same,
        cross,
        *own,
        *(held(value) for value in (hidden_in, norm_gain.reshape(1, width))),
        *(held(value) for value in (route, affinity, cotangent)),
    )
    received = exchange(send.reshape(experts, SLOT, 2 * width), "exp").reshape(depth, 2 * width)
    copies = jnp.broadcast_to(received[None], (half, depth, 2 * width))
    rows_all = exchange(copies, "ctx", by_core)
    partial = call(expert_kernel, 28, shape_of(half, depth, 2 * width), count=3)(
        rows_all, *weights
    )
    terms = exchange(partial, "ctx", by_core)
    back = call(reduce_kernel, 10, shape_of(depth, 2 * width), count=2)(terms, received)
    home = exchange(back.reshape(experts, SLOT, 2 * width), "exp").reshape(depth, 2 * width)
    layer_out, grad_hidden, stats, messages = call(
        functools.partial(combine_kernel, experts),
        8,
        (
            shape_of(rows, width),
            shape_of(rows, width),
            shape_of(rows, width, dtype=f32),
            shape_of(half, tall, width),
        ),
        count=7,
    )(home, hidden_in, attended, logs, route, affinity, cotangent)
    grad_same = exchange(messages, "ctx", by_core)
    grad_cross = swap(grad_same)
    gk_nope, g_values, rope_part = call(
        key_kernel,
        14,
        (shape_of(rows, width), shape_of(rows, width), shape_of(experts, quarter, LANES)),
        [
            pltpu.VMEM((2, rows, 2 * width), bf16),
            pltpu.VMEM((2, rows, width), bf16),
            pltpu.VMEM((2, rows, 2 * width), f32),
            pltpu.VMEM((2, rows, width), f32),
        ],
        1,
        8,
    )(place, same, cross, grad_same, grad_cross, *own, messages)
    rope_terms = exchange(rope_part, "exp")
    gq_nope, gq_rope = call(
        query_kernel,
        14,
        (shape_of(rows, width), shape_of(2 * ROPE, rows)),
        [
            pltpu.VMEM((2, rows, 2 * width), bf16),
            pltpu.VMEM((2, rows, width), bf16),
            pltpu.VMEM((2, rows, 2 * width), f32),
        ],
        1,
        7,
    )(place, same, cross, *own, grad_hidden, stats)
    gk_rope = call(rope_kernel, 4, shape_of(ROPE, rows), count=1)(rope_terms)
    return (layer_out, grad_hidden, gq_nope, gq_rope.T, gk_nope, gk_rope.T, g_values)


def solution(mesh):
    placed = (
        P("ctx", "exp"),
        P("ctx", "exp"),
        P("ctx", "exp"),
        P("ctx", "exp"),
        P("ctx", None),
        P("ctx", "exp"),
        P("exp"),
        P("ctx"),
        P("ctx", None),
        P("exp", None, "ctx"),
        P("exp", None, "ctx"),
        P("exp", "ctx", None),
        P("ctx", "exp"),
    )
    return jax.shard_map(
        per_device,
        mesh=mesh,
        in_specs=placed,
        out_specs=(
            P("ctx", "exp"),
            P("ctx", "exp"),
            P("ctx", "exp"),
            P("ctx", "exp"),
            P("ctx", "exp"),
            P("ctx", None),
            P("ctx", "exp"),
        ),
        check_vma=False,
    )
```

```python
import functools
import math

import jax
import jax.numpy as jnp
from jax import lax
from jax.experimental import pallas as pl
from jax.experimental.pallas import tpu as pltpu
from jax.sharding import PartitionSpec as P

NOPE = 64
ROPE = 32
VDIM = 64
D = 4096
CAP = 12
PAIR = 2 * CAP
TALL = 32
LINES = 16
LANES = 128

norm_eps = 1e-06
route_scale = 2.5
masked_low = -1e30
score_scale = 1.0 / math.sqrt(NOPE + ROPE)

bf16 = jnp.bfloat16
f32 = jnp.float32
MIB = 1024 * 1024

LEFT = slice(0, LANES)
RIGHT = slice(LANES, 2 * LANES)


def nt_dot(a, b):
    return lax.dot_general(a, b, (((1,), (1,)), ((), ())), preferred_element_type=f32)


def nn_dot(a, b):
    return jnp.dot(a, b, preferred_element_type=f32)


def lanes_of(shape):
    return lax.broadcasted_iota(jnp.int32, shape, len(shape) - 1)


def pieces_of(value, count):
    pieces = []
    for _ in range(count):
        piece = value.astype(bf16).astype(f32)
        pieces.append(piece)
        value = value - piece
    return pieces


def own_query(queries, head):
    rows = queries.shape[0]
    lane = lanes_of((rows, LANES))
    nope = jnp.where(lane // NOPE == head, queries[:, LEFT], jnp.zeros((rows, LANES), bf16))
    rot = queries[:, RIGHT].astype(f32)
    if head:
        rot = pltpu.roll(rot, LANES - head * ROPE, 1)
    rot = jnp.where(lane < ROPE, rot, 0.0).astype(bf16)
    return jnp.concatenate([nope, rot], 1)


def own_key(keys, head):
    rows = keys.shape[0]
    lane = lanes_of((rows, LANES))
    nope = jnp.where(lane // NOPE == head, keys[:, LEFT], jnp.zeros((rows, LANES), bf16))
    rot = keys[:, RIGHT].astype(f32)
    if head:
        rot = pltpu.roll(rot, head * ROPE, 1)
    return jnp.concatenate([nope, rot.astype(bf16)], 1)


def upright(narrow):
    count, rows = narrow.shape
    full = jnp.concatenate([narrow, jnp.zeros((LANES - count, rows), bf16)], 0)
    return nt_dot(unit_matrix(rows, rows), full).astype(bf16)


def keys_of(message, rows):
    rot = upright(message[rows : rows + ROPE, :][:, 0:rows])
    return jnp.concatenate([message[0:rows, LEFT], rot], 1)


def pair_places(rows, core):
    lane = lanes_of((rows, 2 * rows))
    return lane - jnp.where(lane >= rows, 2 * rows, 0) * core


def slots_along_rows(route_row, experts):
    count = route_row.shape[1]
    hits = (lax.broadcasted_iota(jnp.int32, (experts, count), 0) == route_row).astype(f32)
    before = lax.broadcasted_iota(jnp.int32, (count, count), 0) < lanes_of((count, count))
    ranks = nn_dot(hits.astype(bf16), before.astype(f32).astype(bf16))
    rank = jnp.sum(ranks * hits, 0, keepdims=True)
    return route_row * TALL + rank.astype(jnp.int32)


def column_of(row):
    count = row.shape[1]
    shape = (count, count)
    match = lax.broadcasted_iota(jnp.int32, shape, 0) == lanes_of(shape)
    return jnp.sum(jnp.where(match, row, jnp.zeros_like(row)), 1, keepdims=True)


def unit_matrix(rows, columns, offset=0):
    shape = (rows, columns)
    match = lax.broadcasted_iota(jnp.int32, shape, 0) + offset == lanes_of(shape)
    return match.astype(f32).astype(bf16)


def slots_along_columns(route_row, experts):
    route_column = column_of(route_row)
    count = route_column.shape[0]
    hits = (lanes_of((count, experts)) == route_column).astype(f32)
    before = lanes_of((count, count)) < lax.broadcasted_iota(jnp.int32, (count, count), 0)
    ranks = nn_dot(before.astype(f32).astype(bf16), hits.astype(bf16))
    rank = jnp.sum(ranks * hits, 1, keepdims=True)
    return route_column * PAIR + rank.astype(jnp.int32)


def gate_share_of(affinity):
    return column_of(route_scale * affinity[0:1] / jnp.sum(affinity, 0, keepdims=True))


def pack_kernel(
    place_ref,
    key_nope_hbm,
    key_rope_hbm,
    query_rope_hbm,
    query_nope_hbm,
    values_hbm,
    gate_hbm,
    up_hbm,
    down_hbm,
    own_key_ref,
    own_query_ref,
    message_ref,
    weights_ref,
    key_nope_ref,
    key_rope_ref,
    query_rope_ref,
    query_nope_ref,
    values_ref,
    sems,
):
    pairs = (
        (key_rope_hbm, key_rope_ref),
        (query_rope_hbm, query_rope_ref),
        (key_nope_hbm, key_nope_ref),
        (values_hbm, values_ref),
        (query_nope_hbm, query_nope_ref),
    )
    copies = [
        pltpu.make_async_copy(source, target, sems.at[index])
        for index, (source, target) in enumerate(pairs)
    ]
    moves = [(gate_hbm, weights_ref.at[0:D, :]), (up_hbm, weights_ref.at[D : 2 * D, :])]
    for index in range(D // LANES):
        start = 2 * D + index * LANES
        source = down_hbm.at[:, index * LANES : (index + 1) * LANES]
        moves.append((source, weights_ref.at[start : start + LANES, :]))
    moves = [
        pltpu.make_async_copy(source, target, sems.at[len(pairs) + index])
        for index, (source, target) in enumerate(moves)
    ]
    for copy in copies + moves:
        copy.start()
    for copy in copies:
        copy.wait()
    rows = key_nope_ref.shape[0]
    place = place_ref[0]
    pair, core = place // 2, place % 2
    own_key_ref[:, LEFT] = key_nope_ref[...]
    own_key_ref[:, RIGHT] = upright(key_rope_ref[...])
    own_query_ref[:, LEFT] = query_nope_ref[...]
    own_query_ref[:, RIGHT] = upright(query_rope_ref[...])
    rot = jnp.concatenate([key_rope_ref[...], jnp.zeros((ROPE, 2 * LANES - rows), bf16)], 1)
    empty = jnp.zeros((ROPE, 2 * LANES), bf16)
    for index in range(message_ref.shape[0]):
        to_later = (index > pair) | ((index == pair) & (core == 0))

        @pl.when(to_later)
        def _():
            message_ref[index, 0:rows, LEFT] = key_nope_ref[...]
            message_ref[index, 0:rows, RIGHT] = values_ref[...]
            message_ref[index, rows:, :] = rot

        @pl.when(jnp.logical_not(to_later))
        def _():
            message_ref[index, 0:rows, :] = own_query_ref[...]
            message_ref[index, rows:, :] = empty

    for copy in moves:
        copy.wait()


def forward_kernel(
    experts,
    place_ref,
    same_ref,
    cross_ref,
    own_key_ref,
    own_query_ref,
    values_ref,
    hidden_ref,
    gain_ref,
    route_ref,
    affinity_ref,
    cotangent_ref,
    attended_ref,
    log_ref,
    send_ref,
    all_keys_ref,
    all_vals_ref,
    scores_ref,
):
    rows = own_key_ref.shape[0]
    place = place_ref[0]
    pair, core = place // 2, place % 2
    count = same_ref.shape[0]
    for index in range(count):
        for part, ref in enumerate((same_ref, cross_ref)):
            at = slice(part * rows, (part + 1) * rows)
            rot = ref[index, rows : rows + ROPE, :][:, 0:rows]
            all_keys_ref[index, at, LEFT] = ref[index, 0:rows, LEFT]
            all_keys_ref[index, at, RIGHT] = upright(rot)
            all_vals_ref[index, at, :] = ref[index, 0:rows, RIGHT]
    all_keys_ref[pair, 0:rows, :] = own_key_ref[...]
    all_vals_ref[pair, 0:rows, :] = values_ref[...]
    queries = [own_query(own_query_ref[...], head) for head in range(2)]
    ahead = pair_places(rows, core) - lax.broadcasted_iota(jnp.int32, (rows, 2 * rows), 0)
    tops = [None, None]
    for index in range(count):
        visible = ahead <= (pair - index) * (2 * rows)
        for head in range(2):
            scores = nt_dot(queries[head], all_keys_ref[index]) * score_scale
            scores = jnp.where(visible, scores, masked_low)
            scores_ref[head, index] = scores
            tops[head] = scores if index == 0 else jnp.maximum(tops[head], scores)
    state = []
    for head in range(2):
        top = jnp.max(tops[head], 1, keepdims=True)
        total = jnp.zeros((rows, 2 * rows), f32)
        mixed = jnp.zeros((rows, LANES), f32)
        for index in range(count):
            weights = jnp.exp(scores_ref[head, index] - top)
            total = total + weights
            mixed = mixed + nn_dot(weights.astype(bf16), all_vals_ref[index])
        state.extend([top, jnp.sum(total, 1, keepdims=True), mixed])
    first = lanes_of((rows, LANES)) < VDIM
    attended = jnp.where(first, state[2] / state[1], state[5] / state[4]).astype(bf16)
    attended_ref[...] = attended
    log_ref[...] = jnp.where(
        first, state[0] + jnp.log(state[1]), state[3] + jnp.log(state[4])
    )
    hidden = hidden_ref[...].astype(f32) + attended.astype(f32)
    raised = (hidden * gain_ref[...]).astype(bf16)
    share = gate_share_of(affinity_ref[...])
    grad = (share * cotangent_ref[...].astype(f32)).astype(bf16)
    slots = slots_along_rows(route_ref[...], experts)
    line = lax.broadcasted_iota(jnp.int32, (experts * TALL, rows), 0)
    raised_table = (line == slots).astype(f32).astype(bf16)
    grad_table = (line == slots + CAP).astype(f32).astype(bf16)
    row = lax.broadcasted_iota(jnp.int32, (TALL, LANES), 0)
    gains = jnp.zeros((TALL, LANES), f32)
    for index, piece in enumerate(pieces_of(gain_ref[...], 3)):
        gains = jnp.where(row == PAIR + index, piece, gains)
    gains = jnp.broadcast_to(gains[None], (experts, TALL, LANES)).reshape(-1, LANES)
    sent = nn_dot(raised_table, raised) + nn_dot(grad_table, grad) + gains
    send_ref[...] = sent.astype(bf16)


def unfold_kernel(received_ref, rows_ref, own_ref, gain_ref):
    for index in range(received_ref.shape[0] // TALL):
        at = slice(index * LANES, (index + 1) * LANES)
        start = index * TALL
        tile = received_ref[start : start + PAIR, :]
        own_ref[:, at] = tile
        for copy in range(rows_ref.shape[0]):
            rows_ref[copy, :, at] = tile
        pieces = received_ref[start : start + TALL, :].astype(f32)[PAIR : PAIR + 3]
        gain_ref[:, at] = pieces[0:1] + pieces[1:2] + pieces[2:3]


def expert_kernel(rows_ref, gain_ref, own_ref, other_ref, out_ref):
    count = rows_ref.shape[0]
    wide = 2 * LANES
    refs = (own_ref, other_ref)

    def side_by_side(base, index):
        at = slice(base + index * wide, base + (index + 1) * wide)
        return jnp.concatenate([ref[at, :] for ref in refs], 1)

    def down_block(index):
        at = 2 * D + index * wide
        halves = [
            jnp.concatenate([ref[at : at + LANES, :], ref[at + LANES : at + wide, :]], 1)
            for ref in refs
        ]
        return jnp.concatenate(halves, 0)

    zero = jnp.zeros((count, wide), f32)
    gate_val, up_val, grad_active, squares = zero, zero, zero, zero
    for index in range(D // wide):
        at = slice(index * wide, (index + 1) * wide)
        rows = rows_ref[:, at]
        hidden = rows.astype(f32) / gain_ref[:, at]
        squares = squares + hidden * hidden
        gate_val = gate_val + nn_dot(rows, side_by_side(0, index))
        up_val = up_val + nn_dot(rows, side_by_side(D, index))
        grad_active = grad_active + nt_dot(rows, down_block(index))
    inverse = lax.rsqrt(jnp.sum(squares, 1, keepdims=True) / D + norm_eps)
    gate_val, up_val = inverse * gate_val, inverse * up_val
    grad_active = pltpu.roll(grad_active, count - CAP, 0)
    upper = lax.rem(lax.broadcasted_iota(jnp.int32, (count, wide), 0), PAIR) < CAP
    sig = 1.0 / (1.0 + jnp.exp(-gate_val))
    silu = gate_val * sig
    active = jnp.where(upper, silu * up_val, 0.0).astype(bf16)
    grad_gate = grad_active * up_val * (sig * (1.0 + gate_val * (1.0 - sig)))
    grad_gate = pltpu.roll(jnp.where(upper, grad_gate, 0.0), CAP, 0).astype(bf16)
    grad_up = pltpu.roll(jnp.where(upper, grad_active * silu, 0.0), CAP, 0).astype(bf16)
    for index in range(D // wide):
        out = nn_dot(active, down_block(index))
        out = out + nt_dot(grad_gate, side_by_side(0, index))
        out = out + nt_dot(grad_up, side_by_side(D, index))
        out_ref[:, index * wide : (index + 1) * wide] = out.astype(bf16)


def reduce_kernel(terms_ref, own_ref, gain_ref, out_ref):
    total = terms_ref[0].astype(f32)
    for index in range(1, terms_ref.shape[0]):
        total = total + terms_ref[index].astype(f32)
    raised = own_ref[...].astype(f32)
    gain = gain_ref[...]
    back = jnp.concatenate([total[CAP:], total[:CAP]], 0)
    hidden = raised / gain
    inverse = lax.rsqrt(jnp.sum(hidden * hidden, 1, keepdims=True) / D + norm_eps)
    cross = jnp.sum(back * raised, 1, keepdims=True) / D
    grad = inverse * (back * gain - hidden * (inverse * inverse * cross))
    out = jnp.concatenate([total[:CAP], grad[:CAP]], 0).astype(bf16)
    for index in range(out_ref.shape[0]):
        out_ref[index] = out[:, index * LANES : (index + 1) * LANES]


def combine_kernel(
    experts,
    home_ref,
    hidden_ref,
    attended_ref,
    log_ref,
    route_ref,
    affinity_ref,
    cotangent_ref,
    layer_ref,
    grad_ref,
    stats_ref,
    message_ref,
):
    rows = hidden_ref.shape[0]
    slots = slots_along_columns(route_ref[...], experts)
    column = lanes_of((rows, experts * PAIR))
    home = home_ref[...]
    token_out = nn_dot((column == slots).astype(f32).astype(bf16), home)
    token_grad = nn_dot((column == slots + CAP).astype(f32).astype(bf16), home)
    attended = attended_ref[...].astype(f32)
    hidden = hidden_ref[...].astype(f32) + attended
    share = gate_share_of(affinity_ref[...])
    layer_ref[...] = (hidden + share * token_out).astype(bf16)
    grad = (cotangent_ref[...].astype(f32) + token_grad).astype(bf16)
    grad_ref[...] = grad
    product = grad.astype(f32) * attended
    lane = lanes_of((rows, LANES))
    stats, pieces = jnp.zeros((rows, LANES), f32), jnp.zeros((rows, LANES), f32)
    for head in range(2):
        dot = jnp.sum(jnp.where(lane // VDIM == head, product, 0.0), 1, keepdims=True)
        log = log_ref[:, head * VDIM : head * VDIM + 1]
        stats = jnp.where(lane == 2 * head, dot, jnp.where(lane == 2 * head + 1, log, stats))
        for index, piece in enumerate(pieces_of(dot, 3) + pieces_of(log, 3)):
            pieces = jnp.where(lane == 6 * head + index, piece, pieces)
    stats_ref[...] = stats
    pieces = jnp.concatenate(
        [pieces.astype(bf16), jnp.zeros((2 * LANES - rows, LANES), bf16)], 0
    )
    lines = nt_dot(unit_matrix(LINES, LANES), pieces).astype(bf16)
    for index in range(message_ref.shape[0]):
        message_ref[index, 0:rows, :] = grad
        message_ref[index, rows : rows + LINES, :] = lines[:, LEFT]
        message_ref[index, rows + LINES :, :] = lines[:, RIGHT]


def query_kernel(
    place_ref,
    keys_ref,
    vals_ref,
    own_query_ref,
    grad_ref,
    stats_ref,
    query_nope_ref,
    query_rope_ref,
    query_ref,
    grads_ref,
    dq_ref,
):
    rows = own_query_ref.shape[0]
    place = place_ref[0]
    pair, core = place // 2, place % 2
    lane = lanes_of((rows, LANES))
    for head in range(2):
        query_ref[head] = own_query(own_query_ref[...], head)
        grads_ref[head] = jnp.where(
            lane // VDIM == head, grad_ref[...], jnp.zeros((rows, LANES), bf16)
        )

    def part(head, index, visible):
        dot = stats_ref[:, 2 * head : 2 * head + 1]
        log = stats_ref[:, 2 * head + 1 : 2 * head + 2]
        keys = keys_ref[index]
        prob = jnp.exp(nt_dot(query_ref[head], keys) * score_scale - log)
        if visible is not None:
            prob = jnp.where(visible, prob, 0.0)
        grad_prob = nt_dot(grads_ref[head], vals_ref[index])
        grad_score = (prob * (grad_prob - dot)).astype(bf16)
        return nn_dot(grad_score, keys)

    visible = pair_places(rows, core) <= lax.broadcasted_iota(jnp.int32, (rows, 2 * rows), 0)
    for head in range(2):
        dq_ref[head] = part(head, pair, visible)

    def step(index, carry):
        for head in range(2):
            dq_ref[head] += part(head, index, None)
        return carry

    lax.fori_loop(0, pair, step, 0)
    query_nope_ref[...] = (
        score_scale * jnp.where(lane < NOPE, dq_ref[0, :, LEFT], dq_ref[1, :, LEFT])
    ).astype(bf16)
    rot = jnp.where(lane < ROPE, dq_ref[0, :, RIGHT], pltpu.roll(dq_ref[1, :, RIGHT], ROPE, 1))
    rot = (score_scale * rot).astype(bf16)
    query_rope_ref[...] = nt_dot(unit_matrix(2 * ROPE, LANES), rot).astype(bf16)


def key_kernel(
    place_ref,
    same_ref,
    cross_ref,
    grad_same_ref,
    grad_cross_ref,
    own_key_ref,
    own_query_ref,
    values_ref,
    key_nope_ref,
    grad_values_ref,
    rope_ref,
):
    rows = own_key_ref.shape[0]
    place = place_ref[0]
    pair, core = place // 2, place % 2
    lane = lanes_of((rows, LANES))
    zero = jnp.zeros((rows, LANES), bf16)
    keys = [own_key(own_key_ref[...], head) for head in range(2)]
    vals = [jnp.where(lane // VDIM == head, values_ref[...], zero) for head in range(2)]

    def lines_of(first, second):
        zero = jnp.zeros((LINES, LANES), f32)
        parts = []
        for message in (first, second):
            low = message[rows : rows + LINES].astype(f32)
            high = message[rows + LINES :].astype(f32)
            parts.append(jnp.concatenate([low, high, zero], 1))
        moved = pltpu.roll(parts[1], rows, 1)
        return jnp.where(lanes_of(moved.shape) < rows, parts[0], moved)

    def part(head, queries, grads, lines, visible):
        at = 6 * head
        dot = lines[at : at + 1] + lines[at + 1 : at + 2] + lines[at + 2 : at + 3]
        log = lines[at + 3 : at + 4] + lines[at + 4 : at + 5] + lines[at + 5 : at + 6]
        prob = jnp.exp(nt_dot(keys[head], queries) * score_scale - log)
        prob = jnp.where(visible, prob, 0.0)
        grad_prob = nt_dot(vals[head], grads)
        grad_score = (prob * (grad_prob - dot)).astype(bf16)
        return nn_dot(grad_score, queries), nn_dot(prob.astype(bf16), grads)

    ahead = pair_places(rows, core) - lax.broadcasted_iota(jnp.int32, (rows, 2 * rows), 0)
    dk, dv = [0.0, 0.0], [0.0, 0.0]
    for index in range(same_ref.shape[0]):
        first = jnp.where(index == pair, own_query_ref[...], same_ref[index, 0:rows, :])
        queries = jnp.concatenate([first, cross_ref[index, 0:rows, :]], 0)
        first_grad, second_grad = grad_same_ref[index], grad_cross_ref[index]
        grads = jnp.concatenate([first_grad[0:rows], second_grad[0:rows]], 0)
        lines = lines_of(first_grad, second_grad)
        visible = ahead >= (pair - index) * (2 * rows)
        for head in range(2):
            more_dk, more_dv = part(head, queries, grads, lines, visible)
            dk[head] = dk[head] + more_dk
            dv[head] = dv[head] + more_dv
    key_nope_ref[...] = (
        score_scale * jnp.where(lane < NOPE, dk[0][:, LEFT], dk[1][:, LEFT])
    ).astype(bf16)
    grad_values_ref[...] = jnp.where(lane < VDIM, dv[0], dv[1]).astype(bf16)
    shared = dk[0][:, RIGHT] + pltpu.roll(dk[1][:, RIGHT], LANES - ROPE, 1)
    quarter = rows // 4
    packed = jnp.zeros((quarter, LANES), f32)
    small = lanes_of((quarter, LANES))
    for index in range(4):
        piece = shared[index * quarter : (index + 1) * quarter]
        if index:
            piece = pltpu.roll(piece, index * ROPE, 1)
        packed = jnp.where(small // ROPE == index, piece, packed)
    packed = (score_scale * packed).astype(bf16)
    for index in range(rope_ref.shape[0]):
        rope_ref[index] = packed


def rope_kernel(terms_ref, out_ref):
    total = terms_ref[0].astype(f32)
    for index in range(1, terms_ref.shape[0]):
        total = total + terms_ref[index].astype(f32)
    total = total.astype(bf16)
    quarter = total.shape[0]
    out = jnp.zeros((ROPE, 4 * quarter), f32)
    for index in range(4):
        part = nt_dot(unit_matrix(ROPE, LANES, index * ROPE), total).astype(bf16)
        out = out + nn_dot(part, unit_matrix(quarter, 4 * quarter, index * quarter))
    out_ref[...] = out.astype(bf16)


def call(body, limit, outs, scratch=(), scalars=0, count=0, space=pltpu.VMEM):
    place = [pl.BlockSpec(memory_space=pltpu.SMEM)] * scalars
    return pl.pallas_call(
        body,
        out_shape=outs,
        in_specs=place + [pl.BlockSpec(memory_space=space)] * count,
        out_specs=jax.tree.map(lambda _: pl.BlockSpec(memory_space=pltpu.VMEM), outs),
        scratch_shapes=list(scratch),
        compiler_params=pltpu.CompilerParams(vmem_limit_bytes=limit * MIB),
    )


def shape_of(*dims, dtype=bf16):
    return jax.ShapeDtypeStruct(dims, dtype)


def held(value):
    return pltpu.with_memory_space_constraint(value, pltpu.HBM)


def exchange(blocks, axis, groups=None):
    return lax.all_to_all(blocks, axis, 0, 0, tiled=True, axis_index_groups=groups)


def per_device(
    hidden_in,
    query_nope,
    query_rope,
    key_nope,
    key_rope,
    values,
    norm_gain,
    expert_route,
    affinity,
    gate_weight,
    up_weight,
    down_weight,
    cotangent,
):
    rows, width = hidden_in.shape
    ctx_count, experts = lax.axis_size("ctx"), lax.axis_size("exp")
    half = ctx_count // 2
    by_core = [[core + 2 * index for index in range(half)] for core in range(2)]
    across = [(index, index ^ 1) for index in range(ctx_count)]
    quarter = rows // 4

    def swap(value):
        return lax.ppermute(value, "ctx", across)

    place = lax.axis_index("ctx").astype(jnp.int32).reshape(1)
    route = expert_route.reshape(1, rows)
    affinity = affinity.T
    tall = rows + ROPE
    own_key_rows, own_query_rows, messages, weights = call(
        pack_kernel,
        12,
        (
            shape_of(rows, 2 * width),
            shape_of(rows, 2 * width),
            shape_of(half, tall, 2 * width),
            shape_of(3 * D, LANES),
        ),
        [
            pltpu.VMEM((rows, width), bf16),
            pltpu.VMEM((ROPE, rows), bf16),
            pltpu.VMEM((2 * ROPE, rows), bf16),
            pltpu.VMEM((rows, width), bf16),
            pltpu.VMEM((rows, width), bf16),
            pltpu.SemaphoreType.DMA((7 + D // LANES,)),
        ],
        1,
        8,
        pltpu.HBM,
    )(
        place,
        *(held(value) for value in (key_nope, key_rope.T, query_rope.T, query_nope, values)),
        *(held(value[0]) for value in (gate_weight, up_weight, down_weight)),
    )
    own = (own_key_rows, own_query_rows, held(values))
    same = exchange(messages, "ctx", by_core)
    weights = (weights, swap(weights))
    same, weights = lax.optimization_barrier((same, weights))
    cross = swap(same)

    attended, logs, send, all_keys, all_vals = call(
        functools.partial(forward_kernel, experts),
        24,
        (
            shape_of(rows, width),
            shape_of(rows, width, dtype=f32),
            shape_of(experts * TALL, width),
            shape_of(half, 2 * rows, 2 * width),
            shape_of(half, 2 * rows, width),
        ),
        [pltpu.VMEM((2, half, rows, 2 * rows), f32)],
        1,
        10,
    )(
        place,
        same,
        cross,
        *own,
        *(held(value) for value in (hidden_in, norm_gain.reshape(1, width))),
        *(held(value) for value in (route, affinity, cotangent)),
    )
    received = exchange(send.reshape(experts, TALL, width), "exp").reshape(-1, width)
    rows_all, own_rows, gain = call(
        unfold_kernel,
        6,
        (shape_of(half, PAIR, D), shape_of(PAIR, D), shape_of(1, D, dtype=f32)),
        count=1,
    )(received)
    rows_all = exchange(rows_all, "ctx", by_core).reshape(half * PAIR, D)
    partial = call(expert_kernel, 24, shape_of(half * PAIR, D), count=4)(
        rows_all, gain, *weights
    )
    terms = exchange(partial.reshape(half, PAIR, D), "ctx", by_core)
    back = call(reduce_kernel, 8, shape_of(experts, PAIR, width), count=3)(
        terms, own_rows, gain
    )
    home = exchange(back, "exp").reshape(experts * PAIR, width)
    layer_out, grad_hidden, stats, messages = call(
        functools.partial(combine_kernel, experts),
        8,
        (
            shape_of(rows, width),
            shape_of(rows, width),
            shape_of(rows, width, dtype=f32),
            shape_of(half, tall, width),
        ),
        count=7,
    )(home, hidden_in, attended, logs, route, affinity, cotangent)
    grad_same = exchange(messages, "ctx", by_core)
    grad_cross = swap(grad_same)
    gk_nope, g_values, rope_part = call(
        key_kernel,
        14,
        (shape_of(rows, width), shape_of(rows, width), shape_of(experts, quarter, LANES)),
        (),
        1,
        7,
    )(place, same, cross, grad_same, grad_cross, *own)
    rope_terms = exchange(rope_part, "exp")
    gq_nope, gq_rope = call(
        query_kernel,
        14,
        (shape_of(rows, width), shape_of(2 * ROPE, rows)),
        [
            pltpu.VMEM((2, rows, 2 * width), bf16),
            pltpu.VMEM((2, rows, width), bf16),
            pltpu.VMEM((2, rows, 2 * width), f32),
        ],
        1,
        5,
    )(place, all_keys, all_vals, own_query_rows, grad_hidden, stats)
    gk_rope = call(rope_kernel, 4, shape_of(ROPE, rows), count=1)(rope_terms)
    return (layer_out, grad_hidden, gq_nope, gq_rope.T, gk_nope, gk_rope.T, g_values)


def solution(mesh):
    placed = (
        P("ctx", "exp"),
        P("ctx", "exp"),
        P("ctx", "exp"),
        P("ctx", "exp"),
        P("ctx", None),
        P("ctx", "exp"),
        P("exp"),
        P("ctx"),
        P("ctx", None),
        P("exp", None, "ctx"),
        P("exp", None, "ctx"),
        P("exp", "ctx", None),
        P("ctx", "exp"),
    )
    return jax.shard_map(
        per_device,
        mesh=mesh,
        in_specs=placed,
        out_specs=(
            P("ctx", "exp"),
            P("ctx", "exp"),
            P("ctx", "exp"),
            P("ctx", "exp"),
            P("ctx", "exp"),
            P("ctx", None),
            P("ctx", "exp"),
        ),
        check_vma=False,
    )
```

```python
import functools
import math

import jax
import jax.numpy as jnp
from jax import lax
from jax.experimental import pallas as pl
from jax.experimental.pallas import tpu as pltpu
from jax.sharding import PartitionSpec as P

NOPE = 64
ROPE = 32
VDIM = 64
D = 4096
CAP = 12
PAIR = 2 * CAP
TALL = 32
LINES = 16
LANES = 128

norm_eps = 1e-06
route_scale = 2.5
masked_low = -1e30
score_scale = 1.0 / math.sqrt(NOPE + ROPE)

bf16 = jnp.bfloat16
f32 = jnp.float32
MIB = 1024 * 1024

LEFT = slice(0, LANES)
RIGHT = slice(LANES, 2 * LANES)


def nt_dot(a, b):
    return lax.dot_general(a, b, (((1,), (1,)), ((), ())), preferred_element_type=f32)


def nn_dot(a, b):
    return jnp.dot(a, b, preferred_element_type=f32)


def lanes_of(shape):
    return lax.broadcasted_iota(jnp.int32, shape, len(shape) - 1)


def pieces_of(value, count):
    pieces = []
    for _ in range(count):
        piece = value.astype(bf16).astype(f32)
        pieces.append(piece)
        value = value - piece
    return pieces


def own_query(queries, head):
    rows = queries.shape[0]
    lane = lanes_of((rows, LANES))
    nope = jnp.where(lane // NOPE == head, queries[:, LEFT], jnp.zeros((rows, LANES), bf16))
    rot = queries[:, RIGHT].astype(f32)
    if head:
        rot = pltpu.roll(rot, LANES - head * ROPE, 1)
    rot = jnp.where(lane < ROPE, rot, 0.0).astype(bf16)
    return jnp.concatenate([nope, rot], 1)


def own_key(keys, head):
    rows = keys.shape[0]
    lane = lanes_of((rows, LANES))
    nope = jnp.where(lane // NOPE == head, keys[:, LEFT], jnp.zeros((rows, LANES), bf16))
    rot = keys[:, RIGHT].astype(f32)
    if head:
        rot = pltpu.roll(rot, head * ROPE, 1)
    return jnp.concatenate([nope, rot.astype(bf16)], 1)


def upright(narrow):
    count, rows = narrow.shape
    full = jnp.concatenate([narrow, jnp.zeros((LANES - count, rows), bf16)], 0)
    return nt_dot(unit_matrix(rows, rows), full).astype(bf16)


def keys_of(message, rows):
    rot = upright(message[rows : rows + ROPE, :][:, 0:rows])
    return jnp.concatenate([message[0:rows, LEFT], rot], 1)


def lead_of(rows):
    shape = (rows, 2 * rows)
    lane = lanes_of(shape)
    return lane + jnp.where(lane >= rows, rows, 0) - lax.broadcasted_iota(jnp.int32, shape, 0)


def chunk_start(place, rows, index, cross):
    start = (place // 2 - 2 * index) * (2 * rows)
    if cross:
        start = start + (2 * (place % 2) - 1) * rows
    return start


def slots_along_rows(route_row, experts):
    count = route_row.shape[1]
    hits = (lax.broadcasted_iota(jnp.int32, (experts, count), 0) == route_row).astype(f32)
    before = lax.broadcasted_iota(jnp.int32, (count, count), 0) < lanes_of((count, count))
    ranks = nn_dot(hits.astype(bf16), before.astype(f32).astype(bf16))
    rank = jnp.sum(ranks * hits, 0, keepdims=True)
    return route_row * TALL + rank.astype(jnp.int32)


def column_of(row):
    count = row.shape[1]
    shape = (count, count)
    match = lax.broadcasted_iota(jnp.int32, shape, 0) == lanes_of(shape)
    return jnp.sum(jnp.where(match, row, jnp.zeros_like(row)), 1, keepdims=True)


def unit_matrix(rows, columns, offset=0):
    shape = (rows, columns)
    match = lax.broadcasted_iota(jnp.int32, shape, 0) + offset == lanes_of(shape)
    return match.astype(f32).astype(bf16)


def slots_along_columns(route_row, experts):
    route_column = column_of(route_row)
    count = route_column.shape[0]
    hits = (lanes_of((count, experts)) == route_column).astype(f32)
    before = lanes_of((count, count)) < lax.broadcasted_iota(jnp.int32, (count, count), 0)
    ranks = nn_dot(before.astype(f32).astype(bf16), hits.astype(bf16))
    rank = jnp.sum(ranks * hits, 1, keepdims=True)
    return route_column * PAIR + rank.astype(jnp.int32)


def gate_share_of(affinity):
    return column_of(route_scale * affinity[0:1] / jnp.sum(affinity, 0, keepdims=True))


def pack_kernel(
    place_ref,
    key_nope_hbm,
    key_rope_hbm,
    query_rope_hbm,
    query_nope_hbm,
    values_hbm,
    gate_hbm,
    up_hbm,
    down_hbm,
    own_key_ref,
    own_query_ref,
    message_ref,
    weights_ref,
    key_nope_ref,
    key_rope_ref,
    query_rope_ref,
    query_nope_ref,
    values_ref,
    sems,
):
    pairs = (
        (key_rope_hbm, key_rope_ref),
        (query_rope_hbm, query_rope_ref),
        (key_nope_hbm, key_nope_ref),
        (values_hbm, values_ref),
        (query_nope_hbm, query_nope_ref),
    )
    copies = [
        pltpu.make_async_copy(source, target, sems.at[index])
        for index, (source, target) in enumerate(pairs)
    ]
    moves = [(gate_hbm, weights_ref.at[0:D, :]), (up_hbm, weights_ref.at[D : 2 * D, :])]
    for index in range(D // LANES):
        start = 2 * D + index * LANES
        source = down_hbm.at[:, index * LANES : (index + 1) * LANES]
        moves.append((source, weights_ref.at[start : start + LANES, :]))
    moves = [
        pltpu.make_async_copy(source, target, sems.at[len(pairs) + index])
        for index, (source, target) in enumerate(moves)
    ]
    for copy in copies + moves:
        copy.start()
    for copy in copies:
        copy.wait()
    rows = key_nope_ref.shape[0]
    place = place_ref[0]
    pair, core = place // 2, place % 2
    own_key_ref[:, LEFT] = key_nope_ref[...]
    own_key_ref[:, RIGHT] = upright(key_rope_ref[...])
    own_query_ref[:, LEFT] = query_nope_ref[...]
    own_query_ref[:, RIGHT] = upright(query_rope_ref[...])
    rot = jnp.concatenate([key_rope_ref[...], jnp.zeros((ROPE, 2 * LANES - rows), bf16)], 1)
    empty = jnp.zeros((ROPE, 2 * LANES), bf16)
    for index in range(message_ref.shape[0]):
        to_later = (index > pair) | ((index == pair) & (core == 0))

        @pl.when(to_later)
        def _():
            message_ref[index, 0:rows, LEFT] = key_nope_ref[...]
            message_ref[index, 0:rows, RIGHT] = values_ref[...]
            message_ref[index, rows:, :] = rot

        @pl.when(jnp.logical_not(to_later))
        def _():
            message_ref[index, 0:rows, :] = own_query_ref[...]
            message_ref[index, rows:, :] = empty

    for copy in moves:
        copy.wait()


def unpack_messages(messages_ref, keys_ref, vals_ref, rows):
    for index in range(messages_ref.shape[0]):
        chunk, part = index // 2, index % 2
        at = slice(part * rows, (part + 1) * rows)
        rot = messages_ref[index, rows : rows + ROPE, :][:, 0:rows]
        keys_ref[chunk, at, LEFT] = messages_ref[index, 0:rows, LEFT]
        keys_ref[chunk, at, RIGHT] = upright(rot)
        vals_ref[chunk, at, :] = messages_ref[index, 0:rows, RIGHT]


def score_chunks(place, queries, keys_ref, scores_ref, tops, cross):
    rows = queries[0].shape[0]
    lead = lead_of(rows)
    for index in range(keys_ref.shape[0]):
        visible = lead <= chunk_start(place, rows, index, cross)
        for head in range(2):
            scores = nt_dot(queries[head], keys_ref[index]) * score_scale
            scores = jnp.where(visible, scores, masked_low)
            scores_ref[head, index] = scores
            tops[head] = scores if tops[head] is None else jnp.maximum(tops[head], scores)
    return tops


def same_scores_kernel(
    place_ref,
    same_ref,
    own_key_ref,
    own_query_ref,
    values_ref,
    keys_ref,
    vals_ref,
    scores_ref,
    tops_ref,
):
    rows = own_key_ref.shape[0]
    place = place_ref[0]
    unpack_messages(same_ref, keys_ref, vals_ref, rows)
    pair = place // 2
    at = pl.ds(pl.multiple_of(lax.rem(pair, 2) * rows, rows), rows)
    keys_ref[pair // 2, at, :] = own_key_ref[...]
    vals_ref[pair // 2, at, :] = values_ref[...]
    queries = [own_query(own_query_ref[...], head) for head in range(2)]
    tops = score_chunks(place, queries, keys_ref, scores_ref, [None, None], False)
    for head in range(2):
        tops_ref[head] = tops[head]


def forward_kernel(
    experts,
    place_ref,
    cross_ref,
    same_vals_ref,
    same_scores_ref,
    tops_ref,
    own_query_ref,
    hidden_ref,
    gain_ref,
    route_ref,
    affinity_ref,
    cotangent_ref,
    attended_ref,
    log_ref,
    send_ref,
    keys_ref,
    vals_ref,
    scores_ref,
):
    rows = own_query_ref.shape[0]
    place = place_ref[0]
    unpack_messages(cross_ref, keys_ref, vals_ref, rows)
    queries = [own_query(own_query_ref[...], head) for head in range(2)]
    tops = [tops_ref[head] for head in range(2)]
    tops = score_chunks(place, queries, keys_ref, scores_ref, tops, True)
    state = []
    for head in range(2):
        top = jnp.max(tops[head], 1, keepdims=True)
        total = jnp.zeros((rows, 2 * rows), f32)
        mixed = jnp.zeros((rows, LANES), f32)
        for some_scores, some_vals in ((same_scores_ref, same_vals_ref), (scores_ref, vals_ref)):
            for index in range(some_vals.shape[0]):
                weights = jnp.exp(some_scores[head, index] - top)
                total = total + weights
                mixed = mixed + nn_dot(weights.astype(bf16), some_vals[index])
        state.extend([top, jnp.sum(total, 1, keepdims=True), mixed])
    first = lanes_of((rows, LANES)) < VDIM
    attended = jnp.where(first, state[2] / state[1], state[5] / state[4]).astype(bf16)
    attended_ref[...] = attended
    log_ref[...] = jnp.where(
        first, state[0] + jnp.log(state[1]), state[3] + jnp.log(state[4])
    )
    hidden = hidden_ref[...].astype(f32) + attended.astype(f32)
    raised = (hidden * gain_ref[...]).astype(bf16)
    share = gate_share_of(affinity_ref[...])
    grad = (share * cotangent_ref[...].astype(f32)).astype(bf16)
    slots = slots_along_rows(route_ref[...], experts)
    line = lax.broadcasted_iota(jnp.int32, (experts * TALL, rows), 0)
    raised_table = (line == slots).astype(f32).astype(bf16)
    grad_table = (line == slots + CAP).astype(f32).astype(bf16)
    row = lax.broadcasted_iota(jnp.int32, (TALL, LANES), 0)
    gains = jnp.zeros((TALL, LANES), f32)
    for index, piece in enumerate(pieces_of(gain_ref[...], 3)):
        gains = jnp.where(row == PAIR + index, piece, gains)
    gains = jnp.broadcast_to(gains[None], (experts, TALL, LANES)).reshape(-1, LANES)
    sent = nn_dot(raised_table, raised) + nn_dot(grad_table, grad) + gains
    send_ref[...] = sent.astype(bf16)


def unfold_kernel(received_ref, rows_ref, own_ref, gain_ref):
    for index in range(received_ref.shape[0] // TALL):
        at = slice(index * LANES, (index + 1) * LANES)
        start = index * TALL
        tile = received_ref[start : start + PAIR, :]
        own_ref[:, at] = tile
        for copy in range(rows_ref.shape[0]):
            rows_ref[copy, :, at] = tile
        pieces = received_ref[start : start + TALL, :].astype(f32)[PAIR : PAIR + 3]
        gain_ref[:, at] = pieces[0:1] + pieces[1:2] + pieces[2:3]


def expert_kernel(rows_ref, gain_ref, own_ref, other_ref, out_ref):
    count = rows_ref.shape[0]
    wide = 2 * LANES
    refs = (own_ref, other_ref)

    def side_by_side(base, index):
        at = slice(base + index * wide, base + (index + 1) * wide)
        return jnp.concatenate([ref[at, :] for ref in refs], 1)

    def down_block(index):
        at = 2 * D + index * wide
        halves = [
            jnp.concatenate([ref[at : at + LANES, :], ref[at + LANES : at + wide, :]], 1)
            for ref in refs
        ]
        return jnp.concatenate(halves, 0)

    zero = jnp.zeros((count, wide), f32)
    gate_val, up_val, grad_active, squares = zero, zero, zero, zero
    for index in range(D // wide):
        at = slice(index * wide, (index + 1) * wide)
        rows = rows_ref[:, at]
        hidden = rows.astype(f32) / gain_ref[:, at]
        squares = squares + hidden * hidden
        gate_val = gate_val + nn_dot(rows, side_by_side(0, index))
        up_val = up_val + nn_dot(rows, side_by_side(D, index))
        grad_active = grad_active + nt_dot(rows, down_block(index))
    inverse = lax.rsqrt(jnp.sum(squares, 1, keepdims=True) / D + norm_eps)
    gate_val, up_val = inverse * gate_val, inverse * up_val
    grad_active = pltpu.roll(grad_active, count - CAP, 0)
    upper = lax.rem(lax.broadcasted_iota(jnp.int32, (count, wide), 0), PAIR) < CAP
    sig = 1.0 / (1.0 + jnp.exp(-gate_val))
    silu = gate_val * sig
    active = jnp.where(upper, silu * up_val, 0.0).astype(bf16)
    grad_gate = grad_active * up_val * (sig * (1.0 + gate_val * (1.0 - sig)))
    grad_gate = pltpu.roll(jnp.where(upper, grad_gate, 0.0), CAP, 0).astype(bf16)
    grad_up = pltpu.roll(jnp.where(upper, grad_active * silu, 0.0), CAP, 0).astype(bf16)
    for index in range(D // wide):
        out = nn_dot(active, down_block(index))
        out = out + nt_dot(grad_gate, side_by_side(0, index))
        out = out + nt_dot(grad_up, side_by_side(D, index))
        out_ref[:, index * wide : (index + 1) * wide] = out.astype(bf16)


def reduce_kernel(terms_ref, own_ref, gain_ref, out_ref):
    total = terms_ref[0].astype(f32)
    for index in range(1, terms_ref.shape[0]):
        total = total + terms_ref[index].astype(f32)
    raised = own_ref[...].astype(f32)
    gain = gain_ref[...]
    back = jnp.concatenate([total[CAP:], total[:CAP]], 0)
    hidden = raised / gain
    inverse = lax.rsqrt(jnp.sum(hidden * hidden, 1, keepdims=True) / D + norm_eps)
    cross = jnp.sum(back * raised, 1, keepdims=True) / D
    grad = inverse * (back * gain - hidden * (inverse * inverse * cross))
    out = jnp.concatenate([total[:CAP], grad[:CAP]], 0).astype(bf16)
    for index in range(out_ref.shape[0]):
        out_ref[index] = out[:, index * LANES : (index + 1) * LANES]


def combine_kernel(
    experts,
    home_ref,
    hidden_ref,
    attended_ref,
    log_ref,
    route_ref,
    affinity_ref,
    cotangent_ref,
    layer_ref,
    grad_ref,
    stats_ref,
    message_ref,
):
    rows = hidden_ref.shape[0]
    slots = slots_along_columns(route_ref[...], experts)
    column = lanes_of((rows, experts * PAIR))
    home = home_ref[...]
    token_out = nn_dot((column == slots).astype(f32).astype(bf16), home)
    token_grad = nn_dot((column == slots + CAP).astype(f32).astype(bf16), home)
    attended = attended_ref[...].astype(f32)
    hidden = hidden_ref[...].astype(f32) + attended
    share = gate_share_of(affinity_ref[...])
    layer_ref[...] = (hidden + share * token_out).astype(bf16)
    grad = (cotangent_ref[...].astype(f32) + token_grad).astype(bf16)
    grad_ref[...] = grad
    product = grad.astype(f32) * attended
    lane = lanes_of((rows, LANES))
    stats, pieces = jnp.zeros((rows, LANES), f32), jnp.zeros((rows, LANES), f32)
    for head in range(2):
        dot = jnp.sum(jnp.where(lane // VDIM == head, product, 0.0), 1, keepdims=True)
        log = log_ref[:, head * VDIM : head * VDIM + 1]
        stats = jnp.where(lane == 2 * head, dot, jnp.where(lane == 2 * head + 1, log, stats))
        for index, piece in enumerate(pieces_of(dot, 3) + pieces_of(log, 3)):
            pieces = jnp.where(lane == 6 * head + index, piece, pieces)
    stats_ref[...] = stats
    pieces = jnp.concatenate(
        [pieces.astype(bf16), jnp.zeros((2 * LANES - rows, LANES), bf16)], 0
    )
    lines = nt_dot(unit_matrix(LINES, LANES), pieces).astype(bf16)
    for index in range(message_ref.shape[0]):
        message_ref[index, 0:rows, :] = grad
        message_ref[index, rows : rows + LINES, :] = lines[:, LEFT]
        message_ref[index, rows + LINES :, :] = lines[:, RIGHT]


def query_kernel(
    place_ref,
    same_keys_ref,
    same_vals_ref,
    cross_keys_ref,
    cross_vals_ref,
    own_query_ref,
    grad_ref,
    stats_ref,
    query_nope_ref,
    query_rope_ref,
    query_ref,
    grads_ref,
    dq_ref,
):
    rows = own_query_ref.shape[0]
    place = place_ref[0]
    lane = lanes_of((rows, LANES))
    lead = lead_of(rows)
    for head in range(2):
        query_ref[head] = own_query(own_query_ref[...], head)
        grads_ref[head] = jnp.where(
            lane // VDIM == head, grad_ref[...], jnp.zeros((rows, LANES), bf16)
        )
    dq_ref[...] = jnp.zeros_like(dq_ref)

    def step(index, carry):
        for cross in range(2):
            keys_ref, vals_ref = (
                (cross_keys_ref, cross_vals_ref) if cross else (same_keys_ref, same_vals_ref)
            )
            visible = lead <= chunk_start(place, rows, index, cross)
            keys, vals = keys_ref[index], vals_ref[index]
            for head in range(2):
                dot = stats_ref[:, 2 * head : 2 * head + 1]
                log = stats_ref[:, 2 * head + 1 : 2 * head + 2]
                prob = jnp.exp(nt_dot(query_ref[head], keys) * score_scale - log)
                prob = jnp.where(visible, prob, 0.0)
                grad_prob = nt_dot(grads_ref[head], vals)
                grad_score = (prob * (grad_prob - dot)).astype(bf16)
                dq_ref[head] += nn_dot(grad_score, keys)
        return carry

    lax.fori_loop(0, place // 4 + 1, step, 0)
    query_nope_ref[...] = (
        score_scale * jnp.where(lane < NOPE, dq_ref[0, :, LEFT], dq_ref[1, :, LEFT])
    ).astype(bf16)
    rot = jnp.where(lane < ROPE, dq_ref[0, :, RIGHT], pltpu.roll(dq_ref[1, :, RIGHT], ROPE, 1))
    rot = (score_scale * rot).astype(bf16)
    query_rope_ref[...] = nt_dot(unit_matrix(2 * ROPE, LANES), rot).astype(bf16)


def key_chunks(place, messages_ref, grads_ref, own_key_ref, own_query_ref, values_ref, dk, dv):
    rows = own_key_ref.shape[0]
    cross = own_query_ref is None
    lane = lanes_of((rows, LANES))
    keys = [own_key(own_key_ref[...], head) for head in range(2)]
    zero = jnp.zeros((rows, LANES), bf16)
    vals = [jnp.where(lane // VDIM == head, values_ref[...], zero) for head in range(2)]
    lead = lead_of(rows)

    def lines_of(first, second):
        zero = jnp.zeros((LINES, LANES), f32)
        parts = []
        for message in (first, second):
            low = message[rows : rows + LINES].astype(f32)
            high = message[rows + LINES :].astype(f32)
            parts.append(jnp.concatenate([low, high, zero], 1))
        moved = pltpu.roll(parts[1], rows, 1)
        return jnp.where(lanes_of(moved.shape) < rows, parts[0], moved)

    def queries_of(index):
        queries = messages_ref[index, 0:rows, :]
        if cross:
            return queries
        return jnp.where(index == place // 2, own_query_ref[...], queries)

    for chunk in range(messages_ref.shape[0] // 2):
        index = 2 * chunk
        queries = jnp.concatenate([queries_of(index), queries_of(index + 1)], 0)
        first, second = grads_ref[index], grads_ref[index + 1]
        grads = jnp.concatenate([first[0:rows], second[0:rows]], 0)
        lines = lines_of(first, second)
        visible = lead >= chunk_start(place, rows, chunk, cross)
        for head in range(2):
            at = 6 * head
            dot = lines[at : at + 1] + lines[at + 1 : at + 2] + lines[at + 2 : at + 3]
            log = lines[at + 3 : at + 4] + lines[at + 4 : at + 5] + lines[at + 5 : at + 6]
            prob = jnp.exp(nt_dot(keys[head], queries) * score_scale - log)
            prob = jnp.where(visible, prob, 0.0)
            grad_prob = nt_dot(vals[head], grads)
            grad_score = (prob * (grad_prob - dot)).astype(bf16)
            dk[head] = dk[head] + nn_dot(grad_score, queries)
            dv[head] = dv[head] + nn_dot(prob.astype(bf16), grads)
    return dk, dv


def same_key_kernel(
    place_ref,
    same_ref,
    grad_same_ref,
    own_key_ref,
    own_query_ref,
    values_ref,
    dk_ref,
    dv_ref,
):
    dk, dv = key_chunks(
        place_ref[0],
        same_ref,
        grad_same_ref,
        own_key_ref,
        own_query_ref,
        values_ref,
        [0.0, 0.0],
        [0.0, 0.0],
    )
    for head in range(2):
        dk_ref[head] = dk[head]
        dv_ref[head] = dv[head]


def key_kernel(
    place_ref,
    cross_ref,
    grad_cross_ref,
    own_key_ref,
    values_ref,
    dk_ref,
    dv_ref,
    key_nope_ref,
    grad_values_ref,
    rope_ref,
):
    rows = own_key_ref.shape[0]
    lane = lanes_of((rows, LANES))
    dk, dv = key_chunks(
        place_ref[0],
        cross_ref,
        grad_cross_ref,
        own_key_ref,
        None,
        values_ref,
        [dk_ref[head] for head in range(2)],
        [dv_ref[head] for head in range(2)],
    )
    key_nope_ref[...] = (
        score_scale * jnp.where(lane < NOPE, dk[0][:, LEFT], dk[1][:, LEFT])
    ).astype(bf16)
    grad_values_ref[...] = jnp.where(lane < VDIM, dv[0], dv[1]).astype(bf16)
    shared = dk[0][:, RIGHT] + pltpu.roll(dk[1][:, RIGHT], LANES - ROPE, 1)
    quarter = rows // 4
    packed = jnp.zeros((quarter, LANES), f32)
    small = lanes_of((quarter, LANES))
    for index in range(4):
        piece = shared[index * quarter : (index + 1) * quarter]
        if index:
            piece = pltpu.roll(piece, index * ROPE, 1)
        packed = jnp.where(small // ROPE == index, piece, packed)
    rope_ref[...] = (score_scale * packed).astype(bf16)


def pair_sum_kernel(own_ref, other_ref, out_ref):
    total = (own_ref[...].astype(f32) + other_ref[...].astype(f32)).astype(bf16)
    for index in range(out_ref.shape[0]):
        out_ref[index] = total


def rope_kernel(terms_ref, out_ref):
    total = terms_ref[0].astype(f32)
    for index in range(1, terms_ref.shape[0]):
        total = total + terms_ref[index].astype(f32)
    total = total.astype(bf16)
    quarter = total.shape[0]
    out = jnp.zeros((ROPE, 4 * quarter), f32)
    for index in range(4):
        part = nt_dot(unit_matrix(ROPE, LANES, index * ROPE), total).astype(bf16)
        out = out + nn_dot(part, unit_matrix(quarter, 4 * quarter, index * quarter))
    out_ref[...] = out.astype(bf16)


def call(body, limit, outs, scratch=(), scalars=0, count=0, space=pltpu.VMEM):
    place = [pl.BlockSpec(memory_space=pltpu.SMEM)] * scalars
    return pl.pallas_call(
        body,
        out_shape=outs,
        in_specs=place + [pl.BlockSpec(memory_space=space)] * count,
        out_specs=jax.tree.map(lambda _: pl.BlockSpec(memory_space=pltpu.VMEM), outs),
        scratch_shapes=list(scratch),
        compiler_params=pltpu.CompilerParams(vmem_limit_bytes=limit * MIB),
    )


def shape_of(*dims, dtype=bf16):
    return jax.ShapeDtypeStruct(dims, dtype)


def held(value):
    return pltpu.with_memory_space_constraint(value, pltpu.HBM)


def exchange(blocks, axis, groups=None):
    return lax.all_to_all(blocks, axis, 0, 0, tiled=True, axis_index_groups=groups)


def per_device(
    hidden_in,
    query_nope,
    query_rope,
    key_nope,
    key_rope,
    values,
    norm_gain,
    expert_route,
    affinity,
    gate_weight,
    up_weight,
    down_weight,
    cotangent,
):
    rows, width = hidden_in.shape
    ctx_count, experts = lax.axis_size("ctx"), lax.axis_size("exp")
    half = ctx_count // 2
    by_core = [[core + 2 * index for index in range(half)] for core in range(2)]
    across = [(index, index ^ 1) for index in range(ctx_count)]
    quarter = rows // 4

    def swap(value):
        return lax.ppermute(value, "ctx", across)

    place = lax.axis_index("ctx").astype(jnp.int32).reshape(1)
    route = expert_route.reshape(1, rows)
    affinity = affinity.T
    tall = rows + ROPE
    own_key_rows, own_query_rows, messages, weights = call(
        pack_kernel,
        12,
        (
            shape_of(rows, 2 * width),
            shape_of(rows, 2 * width),
            shape_of(half, tall, 2 * width),
            shape_of(3 * D, LANES),
        ),
        [
            pltpu.VMEM((rows, width), bf16),
            pltpu.VMEM((ROPE, rows), bf16),
            pltpu.VMEM((2 * ROPE, rows), bf16),
            pltpu.VMEM((rows, width), bf16),
            pltpu.VMEM((rows, width), bf16),
            pltpu.SemaphoreType.DMA((7 + D // LANES,)),
        ],
        1,
        8,
        pltpu.HBM,
    )(
        place,
        *(held(value) for value in (key_nope, key_rope.T, query_rope.T, query_nope, values)),
        *(held(value[0]) for value in (gate_weight, up_weight, down_weight)),
    )
    own = (own_key_rows, own_query_rows, held(values))
    same = exchange(messages, "ctx", by_core)
    weights = (weights, swap(weights))
    same, weights = lax.optimization_barrier((same, weights))
    cross = swap(same)

    chunks = half // 2
    same_keys, same_vals, same_scores, tops = call(
        same_scores_kernel,
        20,
        (
            shape_of(chunks, 2 * rows, 2 * width),
            shape_of(chunks, 2 * rows, width),
            shape_of(2, chunks, rows, 2 * rows, dtype=f32),
            shape_of(2, rows, 2 * rows, dtype=f32),
        ),
        (),
        1,
        4,
    )(place, same, *own)
    attended, logs, send, cross_keys, cross_vals = call(
        functools.partial(forward_kernel, experts),
        20,
        (
            shape_of(rows, width),
            shape_of(rows, width, dtype=f32),
            shape_of(experts * TALL, width),
            shape_of(chunks, 2 * rows, 2 * width),
            shape_of(chunks, 2 * rows, width),
        ),
        [pltpu.VMEM((2, chunks, rows, 2 * rows), f32)],
        1,
        10,
    )(
        place,
        cross,
        same_vals,
        same_scores,
        tops,
        own_query_rows,
        *(held(value) for value in (hidden_in, norm_gain.reshape(1, width))),
        *(held(value) for value in (route, affinity, cotangent)),
    )
    received = exchange(send.reshape(experts, TALL, width), "exp").reshape(-1, width)
    rows_all, own_rows, gain = call(
        unfold_kernel,
        6,
        (shape_of(half, PAIR, D), shape_of(PAIR, D), shape_of(1, D, dtype=f32)),
        count=1,
    )(received)
    rows_all = exchange(rows_all, "ctx", by_core).reshape(half * PAIR, D)
    partial = call(expert_kernel, 24, shape_of(half * PAIR, D), count=4)(
        rows_all, gain, *weights
    )
    terms = exchange(partial.reshape(half, PAIR, D), "ctx", by_core)
    back = call(reduce_kernel, 8, shape_of(experts, PAIR, width), count=3)(
        terms, own_rows, gain
    )
    home = exchange(back, "exp").reshape(experts * PAIR, width)
    layer_out, grad_hidden, stats, messages = call(
        functools.partial(combine_kernel, experts),
        8,
        (
            shape_of(rows, width),
            shape_of(rows, width),
            shape_of(rows, width, dtype=f32),
            shape_of(half, tall, width),
        ),
        count=7,
    )(home, hidden_in, attended, logs, route, affinity, cotangent)
    grad_same = exchange(messages, "ctx", by_core)
    grad_cross = swap(grad_same)
    dk, dv = call(
        same_key_kernel,
        14,
        (
            shape_of(2, rows, 2 * width, dtype=f32),
            shape_of(2, rows, width, dtype=f32),
        ),
        (),
        1,
        5,
    )(place, same, grad_same, *own)
    gk_nope, g_values, rope_part = call(
        key_kernel,
        14,
        (shape_of(rows, width), shape_of(rows, width), shape_of(quarter, LANES)),
        (),
        1,
        6,
    )(place, cross, grad_cross, own_key_rows, own[2], dk, dv)
    line = experts // 2
    rope_other = lax.ppermute(
        rope_part, "exp", [(index, (index + line) % experts) for index in range(experts)]
    )
    rope_pairs = call(pair_sum_kernel, 2, shape_of(line, quarter, LANES), count=2)(
        rope_part, rope_other
    )
    by_line = [[part * line + index for index in range(line)] for part in range(2)]
    rope_terms = exchange(rope_pairs, "exp", by_line)
    gq_nope, gq_rope = call(
        query_kernel,
        14,
        (shape_of(rows, width), shape_of(2 * ROPE, rows)),
        [
            pltpu.VMEM((2, rows, 2 * width), bf16),
            pltpu.VMEM((2, rows, width), bf16),
            pltpu.VMEM((2, rows, 2 * width), f32),
        ],
        1,
        7,
    )(place, same_keys, same_vals, cross_keys, cross_vals, own_query_rows, grad_hidden, stats)
    gk_rope = call(rope_kernel, 4, shape_of(ROPE, rows), count=1)(rope_terms)
    return (layer_out, grad_hidden, gq_nope, gq_rope.T, gk_nope, gk_rope.T, g_values)


def solution(mesh):
    placed = (
        P("ctx", "exp"),
        P("ctx", "exp"),
        P("ctx", "exp"),
        P("ctx", "exp"),
        P("ctx", None),
        P("ctx", "exp"),
        P("exp"),
        P("ctx"),
        P("ctx", None),
        P("exp", None, "ctx"),
        P("exp", None, "ctx"),
        P("exp", "ctx", None),
        P("ctx", "exp"),
    )
    return jax.shard_map(
        per_device,
        mesh=mesh,
        in_specs=placed,
        out_specs=(
            P("ctx", "exp"),
            P("ctx", "exp"),
            P("ctx", "exp"),
            P("ctx", "exp"),
            P("ctx", "exp"),
            P("ctx", None),
            P("ctx", "exp"),
        ),
        check_vma=False,
    )
```

```python
import functools
import math

import jax
import jax.numpy as jnp
from jax import lax
from jax.experimental import pallas as pl
from jax.experimental.pallas import tpu as pltpu
from jax.sharding import PartitionSpec as P

NOPE = 64
ROPE = 32
VDIM = 64
D = 4096
CAP = 12
PAIR = 2 * CAP
TALL = 32
LINES = 16
LANES = 128

norm_eps = 1e-06
route_scale = 2.5
masked_low = -1e30
score_scale = 1.0 / math.sqrt(NOPE + ROPE)

bf16 = jnp.bfloat16
f32 = jnp.float32
MIB = 1024 * 1024

LEFT = slice(0, LANES)
RIGHT = slice(LANES, 2 * LANES)


def nt_dot(a, b):
    return lax.dot_general(a, b, (((1,), (1,)), ((), ())), preferred_element_type=f32)


def nn_dot(a, b):
    return jnp.dot(a, b, preferred_element_type=f32)


def lanes_of(shape):
    return lax.broadcasted_iota(jnp.int32, shape, len(shape) - 1)


def pieces_of(value, count):
    pieces = []
    for _ in range(count):
        piece = value.astype(bf16).astype(f32)
        pieces.append(piece)
        value = value - piece
    return pieces


def own_query(queries, head):
    rows = queries.shape[0]
    lane = lanes_of((rows, LANES))
    nope = jnp.where(lane // NOPE == head, queries[:, LEFT], jnp.zeros((rows, LANES), bf16))
    rot = queries[:, RIGHT].astype(f32)
    if head:
        rot = pltpu.roll(rot, LANES - head * ROPE, 1)
    rot = jnp.where(lane < ROPE, rot, 0.0).astype(bf16)
    return jnp.concatenate([nope, rot], 1)


def own_key(keys, head):
    rows = keys.shape[0]
    lane = lanes_of((rows, LANES))
    nope = jnp.where(lane // NOPE == head, keys[:, LEFT], jnp.zeros((rows, LANES), bf16))
    rot = keys[:, RIGHT].astype(f32)
    if head:
        rot = pltpu.roll(rot, head * ROPE, 1)
    return jnp.concatenate([nope, rot.astype(bf16)], 1)


def upright(narrow):
    count, rows = narrow.shape
    full = jnp.concatenate([narrow, jnp.zeros((LANES - count, rows), bf16)], 0)
    return nt_dot(unit_matrix(rows, rows), full).astype(bf16)


def keys_of(message, rows):
    rot = upright(message[rows : rows + ROPE, :][:, 0:rows])
    return jnp.concatenate([message[0:rows, LEFT], rot], 1)


def lead_of(rows):
    shape = (rows, 2 * rows)
    lane = lanes_of(shape)
    return lane + jnp.where(lane >= rows, rows, 0) - lax.broadcasted_iota(jnp.int32, shape, 0)


def chunk_start(place, rows, index, cross):
    start = (place // 2 - 2 * index) * (2 * rows)
    if cross:
        start = start + (2 * (place % 2) - 1) * rows
    return start


def slots_along_rows(route_row, experts):
    count = route_row.shape[1]
    hits = (lax.broadcasted_iota(jnp.int32, (experts, count), 0) == route_row).astype(f32)
    before = lax.broadcasted_iota(jnp.int32, (count, count), 0) < lanes_of((count, count))
    ranks = nn_dot(hits.astype(bf16), before.astype(f32).astype(bf16))
    rank = jnp.sum(ranks * hits, 0, keepdims=True)
    return route_row * TALL + rank.astype(jnp.int32)


def column_of(row):
    count = row.shape[1]
    shape = (count, count)
    match = lax.broadcasted_iota(jnp.int32, shape, 0) == lanes_of(shape)
    return jnp.sum(jnp.where(match, row, jnp.zeros_like(row)), 1, keepdims=True)


def unit_matrix(rows, columns, offset=0):
    shape = (rows, columns)
    match = lax.broadcasted_iota(jnp.int32, shape, 0) + offset == lanes_of(shape)
    return match.astype(f32).astype(bf16)


def slots_along_columns(route_row, experts):
    route_column = column_of(route_row)
    count = route_column.shape[0]
    hits = (lanes_of((count, experts)) == route_column).astype(f32)
    before = lanes_of((count, count)) < lax.broadcasted_iota(jnp.int32, (count, count), 0)
    ranks = nn_dot(before.astype(f32).astype(bf16), hits.astype(bf16))
    rank = jnp.sum(ranks * hits, 1, keepdims=True)
    return route_column * PAIR + rank.astype(jnp.int32)


def gate_share_of(affinity):
    return column_of(route_scale * affinity[0:1] / jnp.sum(affinity, 0, keepdims=True))


def pack_kernel(
    place_ref,
    key_nope_hbm,
    key_rope_hbm,
    query_rope_hbm,
    query_nope_hbm,
    values_hbm,
    gate_hbm,
    up_hbm,
    down_hbm,
    own_key_ref,
    own_query_ref,
    message_ref,
    weights_ref,
    key_nope_ref,
    key_rope_ref,
    query_rope_ref,
    query_nope_ref,
    values_ref,
    sems,
):
    pairs = (
        (key_rope_hbm, key_rope_ref),
        (query_rope_hbm, query_rope_ref),
        (key_nope_hbm, key_nope_ref),
        (values_hbm, values_ref),
        (query_nope_hbm, query_nope_ref),
    )
    copies = [
        pltpu.make_async_copy(source, target, sems.at[index])
        for index, (source, target) in enumerate(pairs)
    ]
    moves = [(gate_hbm, weights_ref.at[0:D, :]), (up_hbm, weights_ref.at[D : 2 * D, :])]
    for index in range(D // LANES):
        start = 2 * D + index * LANES
        source = down_hbm.at[:, index * LANES : (index + 1) * LANES]
        moves.append((source, weights_ref.at[start : start + LANES, :]))
    moves = [
        pltpu.make_async_copy(source, target, sems.at[len(pairs) + index])
        for index, (source, target) in enumerate(moves)
    ]
    for copy in copies + moves:
        copy.start()
    for copy in copies:
        copy.wait()
    rows = key_nope_ref.shape[0]
    place = place_ref[0]
    pair, core = place // 2, place % 2
    own_key_ref[:, LEFT] = key_nope_ref[...]
    own_key_ref[:, RIGHT] = upright(key_rope_ref[...])
    own_query_ref[:, LEFT] = query_nope_ref[...]
    own_query_ref[:, RIGHT] = upright(query_rope_ref[...])
    rot = jnp.concatenate([key_rope_ref[...], jnp.zeros((ROPE, 2 * LANES - rows), bf16)], 1)
    empty = jnp.zeros((ROPE, 2 * LANES), bf16)
    for index in range(message_ref.shape[0]):
        to_later = (index > pair) | ((index == pair) & (core == 0))

        @pl.when(to_later)
        def _():
            message_ref[index, 0:rows, LEFT] = key_nope_ref[...]
            message_ref[index, 0:rows, RIGHT] = values_ref[...]
            message_ref[index, rows:, :] = rot

        @pl.when(jnp.logical_not(to_later))
        def _():
            message_ref[index, 0:rows, :] = own_query_ref[...]
            message_ref[index, rows:, :] = empty

    for copy in moves:
        copy.wait()


def prepare_kernel(
    experts,
    route_ref,
    affinity_ref,
    cotangent_ref,
    gain_ref,
    table_ref,
    base_ref,
    home_ref,
    share_ref,
):
    rows = cotangent_ref.shape[0]
    share = gate_share_of(affinity_ref[...])
    share_ref[...] = jnp.broadcast_to(share, (rows, LANES))
    grad = (share * cotangent_ref[...].astype(f32)).astype(bf16)
    slots = slots_along_rows(route_ref[...], experts)
    line = lax.broadcasted_iota(jnp.int32, (experts * TALL, rows), 0)
    table_ref[...] = (line == slots).astype(f32).astype(bf16)
    grad_table = (line == slots + CAP).astype(f32).astype(bf16)
    row = lax.broadcasted_iota(jnp.int32, (TALL, LANES), 0)
    gains = jnp.zeros((TALL, LANES), f32)
    for index, piece in enumerate(pieces_of(gain_ref[...], 3)):
        gains = jnp.where(row == PAIR + index, piece, gains)
    gains = jnp.broadcast_to(gains[None], (experts, TALL, LANES)).reshape(-1, LANES)
    base_ref[...] = nn_dot(grad_table, grad) + gains
    slots = slots_along_columns(route_ref[...], experts)
    column = lanes_of((rows, experts * PAIR))
    for index in range(2):
        home_ref[index] = (column == slots + index * CAP).astype(f32).astype(bf16)


def unpack_messages(messages_ref, keys_ref, vals_ref, rows):
    for index in range(messages_ref.shape[0]):
        chunk, part = index // 2, index % 2
        at = slice(part * rows, (part + 1) * rows)
        rot = messages_ref[index, rows : rows + ROPE, :][:, 0:rows]
        keys_ref[chunk, at, LEFT] = messages_ref[index, 0:rows, LEFT]
        keys_ref[chunk, at, RIGHT] = upright(rot)
        vals_ref[chunk, at, :] = messages_ref[index, 0:rows, RIGHT]


def score_chunks(place, queries, keys_ref, scores_ref, tops, cross):
    rows = queries[0].shape[0]
    lead = lead_of(rows)
    for index in range(keys_ref.shape[0]):
        visible = lead <= chunk_start(place, rows, index, cross)
        for head in range(2):
            scores = nt_dot(queries[head], keys_ref[index]) * score_scale
            scores = jnp.where(visible, scores, masked_low)
            scores_ref[head, index] = scores
            tops[head] = scores if tops[head] is None else jnp.maximum(tops[head], scores)
    return tops


def same_scores_kernel(
    place_ref,
    same_ref,
    own_key_ref,
    own_query_ref,
    values_ref,
    keys_ref,
    vals_ref,
    scores_ref,
    tops_ref,
):
    rows = own_key_ref.shape[0]
    place = place_ref[0]
    unpack_messages(same_ref, keys_ref, vals_ref, rows)
    pair = place // 2
    at = pl.ds(pl.multiple_of(lax.rem(pair, 2) * rows, rows), rows)
    keys_ref[pair // 2, at, :] = own_key_ref[...]
    vals_ref[pair // 2, at, :] = values_ref[...]
    queries = [own_query(own_query_ref[...], head) for head in range(2)]
    tops = score_chunks(place, queries, keys_ref, scores_ref, [None, None], False)
    for head in range(2):
        tops_ref[head] = tops[head]


def forward_kernel(
    place_ref,
    cross_ref,
    same_vals_ref,
    same_scores_ref,
    tops_ref,
    own_query_ref,
    table_ref,
    base_ref,
    hidden_ref,
    gain_ref,
    attended_ref,
    log_ref,
    send_ref,
    keys_ref,
    vals_ref,
    scores_ref,
):
    rows = own_query_ref.shape[0]
    place = place_ref[0]
    unpack_messages(cross_ref, keys_ref, vals_ref, rows)
    queries = [own_query(own_query_ref[...], head) for head in range(2)]
    tops = [tops_ref[head] for head in range(2)]
    tops = score_chunks(place, queries, keys_ref, scores_ref, tops, True)
    state = []
    for head in range(2):
        top = jnp.max(tops[head], 1, keepdims=True)
        total = jnp.zeros((rows, 2 * rows), f32)
        mixed = jnp.zeros((rows, LANES), f32)
        for some_scores, some_vals in ((same_scores_ref, same_vals_ref), (scores_ref, vals_ref)):
            for index in range(some_vals.shape[0]):
                weights = jnp.exp(some_scores[head, index] - top)
                total = total + weights
                mixed = mixed + nn_dot(weights.astype(bf16), some_vals[index])
        state.extend([top, jnp.sum(total, 1, keepdims=True), mixed])
    first = lanes_of((rows, LANES)) < VDIM
    attended = jnp.where(first, state[2] / state[1], state[5] / state[4]).astype(bf16)
    attended_ref[...] = attended
    log_ref[...] = jnp.where(
        first, state[0] + jnp.log(state[1]), state[3] + jnp.log(state[4])
    )
    hidden = hidden_ref[...].astype(f32) + attended.astype(f32)
    raised = (hidden * gain_ref[...]).astype(bf16)
    send_ref[...] = (nn_dot(table_ref[...], raised) + base_ref[...]).astype(bf16)


def unfold_kernel(received_ref, rows_ref, own_ref, gain_ref):
    for index in range(received_ref.shape[0] // TALL):
        at = slice(index * LANES, (index + 1) * LANES)
        start = index * TALL
        tile = received_ref[start : start + PAIR, :]
        own_ref[:, at] = tile
        for copy in range(rows_ref.shape[0]):
            rows_ref[copy, :, at] = tile
        pieces = received_ref[start : start + TALL, :].astype(f32)[PAIR : PAIR + 3]
        gain_ref[:, at] = pieces[0:1] + pieces[1:2] + pieces[2:3]


def expert_kernel(rows_ref, gain_ref, own_ref, other_ref, out_ref):
    count = rows_ref.shape[0]
    wide = 2 * LANES
    refs = (own_ref, other_ref)

    def side_by_side(base, index):
        at = slice(base + index * wide, base + (index + 1) * wide)
        return jnp.concatenate([ref[at, :] for ref in refs], 1)

    def down_block(index):
        at = 2 * D + index * wide
        halves = [
            jnp.concatenate([ref[at : at + LANES, :], ref[at + LANES : at + wide, :]], 1)
            for ref in refs
        ]
        return jnp.concatenate(halves, 0)

    zero = jnp.zeros((count, wide), f32)
    gate_val, up_val, grad_active, squares = zero, zero, zero, zero
    for index in range(D // wide):
        at = slice(index * wide, (index + 1) * wide)
        rows = rows_ref[:, at]
        hidden = rows.astype(f32) / gain_ref[:, at]
        squares = squares + hidden * hidden
        gate_val = gate_val + nn_dot(rows, side_by_side(0, index))
        up_val = up_val + nn_dot(rows, side_by_side(D, index))
        grad_active = grad_active + nt_dot(rows, down_block(index))
    inverse = lax.rsqrt(jnp.sum(squares, 1, keepdims=True) / D + norm_eps)
    gate_val, up_val = inverse * gate_val, inverse * up_val
    grad_active = pltpu.roll(grad_active, count - CAP, 0)
    upper = lax.rem(lax.broadcasted_iota(jnp.int32, (count, wide), 0), PAIR) < CAP
    sig = 1.0 / (1.0 + jnp.exp(-gate_val))
    silu = gate_val * sig
    active = jnp.where(upper, silu * up_val, 0.0).astype(bf16)
    grad_gate = grad_active * up_val * (sig * (1.0 + gate_val * (1.0 - sig)))
    grad_gate = pltpu.roll(jnp.where(upper, grad_gate, 0.0), CAP, 0).astype(bf16)
    grad_up = pltpu.roll(jnp.where(upper, grad_active * silu, 0.0), CAP, 0).astype(bf16)
    for index in range(D // wide):
        out = nn_dot(active, down_block(index))
        out = out + nt_dot(grad_gate, side_by_side(0, index))
        out = out + nt_dot(grad_up, side_by_side(D, index))
        out_ref[:, index * wide : (index + 1) * wide] = out.astype(bf16)


def reduce_kernel(terms_ref, own_ref, gain_ref, out_ref):
    total = terms_ref[0].astype(f32)
    for index in range(1, terms_ref.shape[0]):
        total = total + terms_ref[index].astype(f32)
    raised = own_ref[...].astype(f32)
    gain = gain_ref[...]
    back = jnp.concatenate([total[CAP:], total[:CAP]], 0)
    hidden = raised / gain
    inverse = lax.rsqrt(jnp.sum(hidden * hidden, 1, keepdims=True) / D + norm_eps)
    cross = jnp.sum(back * raised, 1, keepdims=True) / D
    grad = inverse * (back * gain - hidden * (inverse * inverse * cross))
    out = jnp.concatenate([total[:CAP], grad[:CAP]], 0).astype(bf16)
    for index in range(out_ref.shape[0]):
        out_ref[index] = out[:, index * LANES : (index + 1) * LANES]


def combine_kernel(
    home_ref,
    table_ref,
    share_ref,
    hidden_ref,
    attended_ref,
    log_ref,
    cotangent_ref,
    layer_ref,
    grad_ref,
    stats_ref,
    message_ref,
):
    rows = hidden_ref.shape[0]
    home = home_ref[...]
    token_out = nn_dot(table_ref[0], home)
    token_grad = nn_dot(table_ref[1], home)
    attended = attended_ref[...].astype(f32)
    hidden = hidden_ref[...].astype(f32) + attended
    share = share_ref[...]
    layer_ref[...] = (hidden + share * token_out).astype(bf16)
    grad = (cotangent_ref[...].astype(f32) + token_grad).astype(bf16)
    grad_ref[...] = grad
    product = grad.astype(f32) * attended
    lane = lanes_of((rows, LANES))
    stats, pieces = jnp.zeros((rows, LANES), f32), jnp.zeros((rows, LANES), f32)
    for head in range(2):
        dot = jnp.sum(jnp.where(lane // VDIM == head, product, 0.0), 1, keepdims=True)
        log = log_ref[:, head * VDIM : head * VDIM + 1]
        stats = jnp.where(lane == 2 * head, dot, jnp.where(lane == 2 * head + 1, log, stats))
        for index, piece in enumerate(pieces_of(dot, 3) + pieces_of(log, 3)):
            pieces = jnp.where(lane == 6 * head + index, piece, pieces)
    stats_ref[...] = stats
    pieces = jnp.concatenate(
        [pieces.astype(bf16), jnp.zeros((2 * LANES - rows, LANES), bf16)], 0
    )
    lines = nt_dot(unit_matrix(LINES, LANES), pieces).astype(bf16)
    for index in range(message_ref.shape[0]):
        message_ref[index, 0:rows, :] = grad
        message_ref[index, rows : rows + LINES, :] = lines[:, LEFT]
        message_ref[index, rows + LINES :, :] = lines[:, RIGHT]


def query_kernel(
    place_ref,
    same_keys_ref,
    same_vals_ref,
    cross_keys_ref,
    cross_vals_ref,
    own_query_ref,
    grad_ref,
    stats_ref,
    query_nope_ref,
    query_rope_ref,
    query_ref,
    grads_ref,
    dq_ref,
):
    rows = own_query_ref.shape[0]
    place = place_ref[0]
    lane = lanes_of((rows, LANES))
    lead = lead_of(rows)
    for head in range(2):
        query_ref[head] = own_query(own_query_ref[...], head)
        grads_ref[head] = jnp.where(
            lane // VDIM == head, grad_ref[...], jnp.zeros((rows, LANES), bf16)
        )
    dq_ref[...] = jnp.zeros_like(dq_ref)

    def step(index, carry):
        for cross in range(2):
            keys_ref, vals_ref = (
                (cross_keys_ref, cross_vals_ref) if cross else (same_keys_ref, same_vals_ref)
            )
            visible = lead <= chunk_start(place, rows, index, cross)
            keys, vals = keys_ref[index], vals_ref[index]
            for head in range(2):
                dot = stats_ref[:, 2 * head : 2 * head + 1]
                log = stats_ref[:, 2 * head + 1 : 2 * head + 2]
                prob = jnp.exp(nt_dot(query_ref[head], keys) * score_scale - log)
                prob = jnp.where(visible, prob, 0.0)
                grad_prob = nt_dot(grads_ref[head], vals)
                grad_score = (prob * (grad_prob - dot)).astype(bf16)
                dq_ref[head] += nn_dot(grad_score, keys)
        return carry

    lax.fori_loop(0, place // 4 + 1, step, 0)
    query_nope_ref[...] = (
        score_scale * jnp.where(lane < NOPE, dq_ref[0, :, LEFT], dq_ref[1, :, LEFT])
    ).astype(bf16)
    rot = jnp.where(lane < ROPE, dq_ref[0, :, RIGHT], pltpu.roll(dq_ref[1, :, RIGHT], ROPE, 1))
    rot = (score_scale * rot).astype(bf16)
    query_rope_ref[...] = nt_dot(unit_matrix(2 * ROPE, LANES), rot).astype(bf16)


def key_chunks(place, messages_ref, grads_ref, own_key_ref, own_query_ref, values_ref, dk, dv):
    rows = own_key_ref.shape[0]
    cross = own_query_ref is None
    lane = lanes_of((rows, LANES))
    keys = [own_key(own_key_ref[...], head) for head in range(2)]
    zero = jnp.zeros((rows, LANES), bf16)
    vals = [jnp.where(lane // VDIM == head, values_ref[...], zero) for head in range(2)]
    lead = lead_of(rows)

    def lines_of(first, second):
        zero = jnp.zeros((LINES, LANES), f32)
        parts = []
        for message in (first, second):
            low = message[rows : rows + LINES].astype(f32)
            high = message[rows + LINES :].astype(f32)
            parts.append(jnp.concatenate([low, high, zero], 1))
        moved = pltpu.roll(parts[1], rows, 1)
        return jnp.where(lanes_of(moved.shape) < rows, parts[0], moved)

    def queries_of(index):
        queries = messages_ref[index, 0:rows, :]
        if cross:
            return queries
        return jnp.where(index == place // 2, own_query_ref[...], queries)

    for chunk in range(messages_ref.shape[0] // 2):
        index = 2 * chunk
        queries = jnp.concatenate([queries_of(index), queries_of(index + 1)], 0)
        first, second = grads_ref[index], grads_ref[index + 1]
        grads = jnp.concatenate([first[0:rows], second[0:rows]], 0)
        lines = lines_of(first, second)
        visible = lead >= chunk_start(place, rows, chunk, cross)
        for head in range(2):
            at = 6 * head
            dot = lines[at : at + 1] + lines[at + 1 : at + 2] + lines[at + 2 : at + 3]
            log = lines[at + 3 : at + 4] + lines[at + 4 : at + 5] + lines[at + 5 : at + 6]
            prob = jnp.exp(nt_dot(keys[head], queries) * score_scale - log)
            prob = jnp.where(visible, prob, 0.0)
            grad_prob = nt_dot(vals[head], grads)
            grad_score = (prob * (grad_prob - dot)).astype(bf16)
            dk[head] = dk[head] + nn_dot(grad_score, queries)
            dv[head] = dv[head] + nn_dot(prob.astype(bf16), grads)
    return dk, dv


def same_key_kernel(
    place_ref,
    same_ref,
    grad_same_ref,
    own_key_ref,
    own_query_ref,
    values_ref,
    dk_ref,
    dv_ref,
):
    dk, dv = key_chunks(
        place_ref[0],
        same_ref,
        grad_same_ref,
        own_key_ref,
        own_query_ref,
        values_ref,
        [0.0, 0.0],
        [0.0, 0.0],
    )
    for head in range(2):
        dk_ref[head] = dk[head]
        dv_ref[head] = dv[head]


def key_kernel(
    place_ref,
    cross_ref,
    grad_cross_ref,
    own_key_ref,
    values_ref,
    dk_ref,
    dv_ref,
    key_nope_ref,
    grad_values_ref,
    rope_ref,
):
    rows = own_key_ref.shape[0]
    lane = lanes_of((rows, LANES))
    dk, dv = key_chunks(
        place_ref[0],
        cross_ref,
        grad_cross_ref,
        own_key_ref,
        None,
        values_ref,
        [dk_ref[head] for head in range(2)],
        [dv_ref[head] for head in range(2)],
    )
    key_nope_ref[...] = (
        score_scale * jnp.where(lane < NOPE, dk[0][:, LEFT], dk[1][:, LEFT])
    ).astype(bf16)
    grad_values_ref[...] = jnp.where(lane < VDIM, dv[0], dv[1]).astype(bf16)
    shared = dk[0][:, RIGHT] + pltpu.roll(dk[1][:, RIGHT], LANES - ROPE, 1)
    quarter = rows // 4
    packed = jnp.zeros((quarter, LANES), f32)
    small = lanes_of((quarter, LANES))
    for index in range(4):
        piece = shared[index * quarter : (index + 1) * quarter]
        if index:
            piece = pltpu.roll(piece, index * ROPE, 1)
        packed = jnp.where(small // ROPE == index, piece, packed)
    rope_ref[...] = (score_scale * packed).astype(bf16)


def pair_sum_kernel(own_ref, other_ref, out_ref):
    total = (own_ref[...].astype(f32) + other_ref[...].astype(f32)).astype(bf16)
    for index in range(out_ref.shape[0]):
        out_ref[index] = total


def rope_kernel(terms_ref, out_ref):
    total = terms_ref[0].astype(f32)
    for index in range(1, terms_ref.shape[0]):
        total = total + terms_ref[index].astype(f32)
    total = total.astype(bf16)
    quarter = total.shape[0]
    out = jnp.zeros((ROPE, 4 * quarter), f32)
    for index in range(4):
        part = nt_dot(unit_matrix(ROPE, LANES, index * ROPE), total).astype(bf16)
        out = out + nn_dot(part, unit_matrix(quarter, 4 * quarter, index * quarter))
    out_ref[...] = out.astype(bf16)


def call(body, limit, outs, scratch=(), scalars=0, count=0, space=pltpu.VMEM):
    place = [pl.BlockSpec(memory_space=pltpu.SMEM)] * scalars
    return pl.pallas_call(
        body,
        out_shape=outs,
        in_specs=place + [pl.BlockSpec(memory_space=space)] * count,
        out_specs=jax.tree.map(lambda _: pl.BlockSpec(memory_space=pltpu.VMEM), outs),
        scratch_shapes=list(scratch),
        compiler_params=pltpu.CompilerParams(vmem_limit_bytes=limit * MIB),
    )


def shape_of(*dims, dtype=bf16):
    return jax.ShapeDtypeStruct(dims, dtype)


def held(value):
    return pltpu.with_memory_space_constraint(value, pltpu.HBM)


def exchange(blocks, axis, groups=None):
    return lax.all_to_all(blocks, axis, 0, 0, tiled=True, axis_index_groups=groups)


def per_device(
    hidden_in,
    query_nope,
    query_rope,
    key_nope,
    key_rope,
    values,
    norm_gain,
    expert_route,
    affinity,
    gate_weight,
    up_weight,
    down_weight,
    cotangent,
):
    rows, width = hidden_in.shape
    ctx_count, experts = lax.axis_size("ctx"), lax.axis_size("exp")
    half = ctx_count // 2
    by_core = [[core + 2 * index for index in range(half)] for core in range(2)]
    across = [(index, index ^ 1) for index in range(ctx_count)]
    quarter = rows // 4

    def swap(value):
        return lax.ppermute(value, "ctx", across)

    place = lax.axis_index("ctx").astype(jnp.int32).reshape(1)
    route = expert_route.reshape(1, rows)
    affinity = affinity.T
    tall = rows + ROPE
    own_key_rows, own_query_rows, messages, weights = call(
        pack_kernel,
        12,
        (
            shape_of(rows, 2 * width),
            shape_of(rows, 2 * width),
            shape_of(half, tall, 2 * width),
            shape_of(3 * D, LANES),
        ),
        [
            pltpu.VMEM((rows, width), bf16),
            pltpu.VMEM((ROPE, rows), bf16),
            pltpu.VMEM((2 * ROPE, rows), bf16),
            pltpu.VMEM((rows, width), bf16),
            pltpu.VMEM((rows, width), bf16),
            pltpu.SemaphoreType.DMA((7 + D // LANES,)),
        ],
        1,
        8,
        pltpu.HBM,
    )(
        place,
        *(held(value) for value in (key_nope, key_rope.T, query_rope.T, query_nope, values)),
        *(held(value[0]) for value in (gate_weight, up_weight, down_weight)),
    )
    own = (own_key_rows, own_query_rows, held(values))
    gain_row = held(norm_gain.reshape(1, width))
    table, base, home_tables, share = call(
        functools.partial(prepare_kernel, experts),
        8,
        (
            shape_of(experts * TALL, rows),
            shape_of(experts * TALL, width, dtype=f32),
            shape_of(2, rows, experts * PAIR),
            shape_of(rows, width, dtype=f32),
        ),
        count=4,
    )(held(route), held(affinity), held(cotangent), gain_row)
    same = exchange(messages, "ctx", by_core)
    weights = (weights, swap(weights))
    prepared = (table, base, home_tables, share)
    same, weights, prepared = lax.optimization_barrier((same, weights, prepared))
    table, base, home_tables, share = prepared
    cross = swap(same)

    chunks = half // 2
    same_keys, same_vals, same_scores, tops = call(
        same_scores_kernel,
        20,
        (
            shape_of(chunks, 2 * rows, 2 * width),
            shape_of(chunks, 2 * rows, width),
            shape_of(2, chunks, rows, 2 * rows, dtype=f32),
            shape_of(2, rows, 2 * rows, dtype=f32),
        ),
        (),
        1,
        4,
    )(place, same, *own)
    attended, logs, send, cross_keys, cross_vals = call(
        forward_kernel,
        20,
        (
            shape_of(rows, width),
            shape_of(rows, width, dtype=f32),
            shape_of(experts * TALL, width),
            shape_of(chunks, 2 * rows, 2 * width),
            shape_of(chunks, 2 * rows, width),
        ),
        [pltpu.VMEM((2, chunks, rows, 2 * rows), f32)],
        1,
        9,
    )(
        place,
        cross,
        same_vals,
        same_scores,
        tops,
        own_query_rows,
        held(table),
        held(base),
        held(hidden_in),
        gain_row,
    )
    received = exchange(send.reshape(experts, TALL, width), "exp").reshape(-1, width)
    rows_all, own_rows, gain = call(
        unfold_kernel,
        6,
        (shape_of(half, PAIR, D), shape_of(PAIR, D), shape_of(1, D, dtype=f32)),
        count=1,
    )(received)
    rows_all = exchange(rows_all, "ctx", by_core).reshape(half * PAIR, D)
    partial = call(expert_kernel, 24, shape_of(half * PAIR, D), count=4)(
        rows_all, gain, *weights
    )
    terms = exchange(partial.reshape(half, PAIR, D), "ctx", by_core)
    back = call(reduce_kernel, 8, shape_of(experts, PAIR, width), count=3)(
        terms, own_rows, gain
    )
    home = exchange(back, "exp").reshape(experts * PAIR, width)
    layer_out, grad_hidden, stats, messages = call(
        combine_kernel,
        8,
        (
            shape_of(rows, width),
            shape_of(rows, width),
            shape_of(rows, width, dtype=f32),
            shape_of(half, tall, width),
        ),
        count=7,
    )(home, home_tables, share, hidden_in, attended, logs, cotangent)
    grad_same = exchange(messages, "ctx", by_core)
    grad_cross = swap(grad_same)
    dk, dv = call(
        same_key_kernel,
        14,
        (
            shape_of(2, rows, 2 * width, dtype=f32),
            shape_of(2, rows, width, dtype=f32),
        ),
        (),
        1,
        5,
    )(place, same, grad_same, *own)
    gk_nope, g_values, rope_part = call(
        key_kernel,
        14,
        (shape_of(rows, width), shape_of(rows, width), shape_of(quarter, LANES)),
        (),
        1,
        6,
    )(place, cross, grad_cross, own_key_rows, own[2], dk, dv)
    line = experts // 2
    rope_other = lax.ppermute(
        rope_part, "exp", [(index, (index + line) % experts) for index in range(experts)]
    )
    rope_pairs = call(pair_sum_kernel, 2, shape_of(line, quarter, LANES), count=2)(
        rope_part, rope_other
    )
    by_line = [[part * line + index for index in range(line)] for part in range(2)]
    rope_terms = exchange(rope_pairs, "exp", by_line)
    gq_nope, gq_rope = call(
        query_kernel,
        14,
        (shape_of(rows, width), shape_of(2 * ROPE, rows)),
        [
            pltpu.VMEM((2, rows, 2 * width), bf16),
            pltpu.VMEM((2, rows, width), bf16),
            pltpu.VMEM((2, rows, 2 * width), f32),
        ],
        1,
        7,
    )(place, same_keys, same_vals, cross_keys, cross_vals, own_query_rows, grad_hidden, stats)
    gk_rope = call(rope_kernel, 4, shape_of(ROPE, rows), count=1)(rope_terms)
    return (layer_out, grad_hidden, gq_nope, gq_rope.T, gk_nope, gk_rope.T, g_values)


def solution(mesh):
    placed = (
        P("ctx", "exp"),
        P("ctx", "exp"),
        P("ctx", "exp"),
        P("ctx", "exp"),
        P("ctx", None),
        P("ctx", "exp"),
        P("exp"),
        P("ctx"),
        P("ctx", None),
        P("exp", None, "ctx"),
        P("exp", None, "ctx"),
        P("exp", "ctx", None),
        P("ctx", "exp"),
    )
    return jax.shard_map(
        per_device,
        mesh=mesh,
        in_specs=placed,
        out_specs=(
            P("ctx", "exp"),
            P("ctx", "exp"),
            P("ctx", "exp"),
            P("ctx", "exp"),
            P("ctx", "exp"),
            P("ctx", None),
            P("ctx", "exp"),
        ),
        check_vma=False,
    )
```

```python
import functools
import math

import jax
import jax.numpy as jnp
from jax import lax
from jax.experimental import pallas as pl
from jax.experimental.pallas import tpu as pltpu
from jax.sharding import PartitionSpec as P

NOPE = 64
ROPE = 32
VDIM = 64
D = 4096
CAP = 12
PAIR = 2 * CAP
TALL = 32
LINES = 16
LANES = 128

norm_eps = 1e-06
route_scale = 2.5
masked_low = -1e30
score_scale = 1.0 / math.sqrt(NOPE + ROPE)

bf16 = jnp.bfloat16
f32 = jnp.float32
MIB = 1024 * 1024

LEFT = slice(0, LANES)
RIGHT = slice(LANES, 2 * LANES)


def nt_dot(a, b):
    return lax.dot_general(a, b, (((1,), (1,)), ((), ())), preferred_element_type=f32)


def nn_dot(a, b):
    return jnp.dot(a, b, preferred_element_type=f32)


def lanes_of(shape):
    return lax.broadcasted_iota(jnp.int32, shape, len(shape) - 1)


def pieces_of(value, count):
    pieces = []
    for _ in range(count):
        piece = value.astype(bf16).astype(f32)
        pieces.append(piece)
        value = value - piece
    return pieces


def own_query(queries, head):
    rows = queries.shape[0]
    lane = lanes_of((rows, LANES))
    nope = jnp.where(lane // NOPE == head, queries[:, LEFT], jnp.zeros((rows, LANES), bf16))
    rot = queries[:, RIGHT].astype(f32)
    if head:
        rot = pltpu.roll(rot, LANES - head * ROPE, 1)
    rot = jnp.where(lane < ROPE, rot, 0.0).astype(bf16)
    return jnp.concatenate([nope, rot], 1)


def own_key(keys, head):
    rows = keys.shape[0]
    lane = lanes_of((rows, LANES))
    nope = jnp.where(lane // NOPE == head, keys[:, LEFT], jnp.zeros((rows, LANES), bf16))
    rot = keys[:, RIGHT].astype(f32)
    if head:
        rot = pltpu.roll(rot, head * ROPE, 1)
    return jnp.concatenate([nope, rot.astype(bf16)], 1)


def upright(narrow):
    count, rows = narrow.shape
    full = jnp.concatenate([narrow, jnp.zeros((LANES - count, rows), bf16)], 0)
    return nt_dot(unit_matrix(rows, rows), full).astype(bf16)


def keys_of(message, rows):
    rot = upright(message[rows : rows + ROPE, :][:, 0:rows])
    return jnp.concatenate([message[0:rows, LEFT], rot], 1)


def lead_of(rows):
    shape = (rows, 2 * rows)
    lane = lanes_of(shape)
    return lane + jnp.where(lane >= rows, rows, 0) - lax.broadcasted_iota(jnp.int32, shape, 0)


def chunk_start(place, rows, index, cross):
    start = (place // 2 - 2 * index) * (2 * rows)
    if cross:
        start = start + (2 * (place % 2) - 1) * rows
    return start


def slots_along_rows(route_row, experts):
    count = route_row.shape[1]
    hits = (lax.broadcasted_iota(jnp.int32, (experts, count), 0) == route_row).astype(f32)
    before = lax.broadcasted_iota(jnp.int32, (count, count), 0) < lanes_of((count, count))
    ranks = nn_dot(hits.astype(bf16), before.astype(f32).astype(bf16))
    rank = jnp.sum(ranks * hits, 0, keepdims=True)
    return route_row * TALL + rank.astype(jnp.int32)


def column_of(row):
    count = row.shape[1]
    shape = (count, count)
    match = lax.broadcasted_iota(jnp.int32, shape, 0) == lanes_of(shape)
    return jnp.sum(jnp.where(match, row, jnp.zeros_like(row)), 1, keepdims=True)


def unit_matrix(rows, columns, offset=0):
    shape = (rows, columns)
    match = lax.broadcasted_iota(jnp.int32, shape, 0) + offset == lanes_of(shape)
    return match.astype(f32).astype(bf16)


def slots_along_columns(route_row, experts):
    route_column = column_of(route_row)
    count = route_column.shape[0]
    hits = (lanes_of((count, experts)) == route_column).astype(f32)
    before = lanes_of((count, count)) < lax.broadcasted_iota(jnp.int32, (count, count), 0)
    ranks = nn_dot(before.astype(f32).astype(bf16), hits.astype(bf16))
    rank = jnp.sum(ranks * hits, 1, keepdims=True)
    return route_column * PAIR + rank.astype(jnp.int32)


def gate_share_of(affinity):
    return column_of(route_scale * affinity[0:1] / jnp.sum(affinity, 0, keepdims=True))


def pack_kernel(
    place_ref,
    key_nope_hbm,
    key_rope_hbm,
    query_rope_hbm,
    query_nope_hbm,
    values_hbm,
    gate_hbm,
    up_hbm,
    down_hbm,
    own_key_ref,
    own_query_ref,
    message_ref,
    weights_ref,
    key_nope_ref,
    key_rope_ref,
    query_rope_ref,
    query_nope_ref,
    values_ref,
    sems,
):
    pairs = (
        (key_rope_hbm, key_rope_ref),
        (query_rope_hbm, query_rope_ref),
        (key_nope_hbm, key_nope_ref),
        (values_hbm, values_ref),
        (query_nope_hbm, query_nope_ref),
    )
    copies = [
        pltpu.make_async_copy(source, target, sems.at[index])
        for index, (source, target) in enumerate(pairs)
    ]
    moves = [(gate_hbm, weights_ref.at[0:D, :]), (up_hbm, weights_ref.at[D : 2 * D, :])]
    for index in range(D // LANES):
        start = 2 * D + index * LANES
        source = down_hbm.at[:, index * LANES : (index + 1) * LANES]
        moves.append((source, weights_ref.at[start : start + LANES, :]))
    moves = [
        pltpu.make_async_copy(source, target, sems.at[len(pairs) + index])
        for index, (source, target) in enumerate(moves)
    ]
    for copy in copies + moves:
        copy.start()
    for copy in copies:
        copy.wait()
    rows = key_nope_ref.shape[0]
    place = place_ref[0]
    pair, core = place // 2, place % 2
    own_key_ref[:, LEFT] = key_nope_ref[...]
    own_key_ref[:, RIGHT] = upright(key_rope_ref[...])
    own_query_ref[:, LEFT] = query_nope_ref[...]
    own_query_ref[:, RIGHT] = upright(query_rope_ref[...])
    rot = jnp.concatenate([key_rope_ref[...], jnp.zeros((ROPE, 2 * LANES - rows), bf16)], 1)
    empty = jnp.zeros((ROPE, 2 * LANES), bf16)
    for index in range(message_ref.shape[0]):
        to_later = (index > pair) | ((index == pair) & (core == 0))

        @pl.when(to_later)
        def _():
            message_ref[index, 0:rows, LEFT] = key_nope_ref[...]
            message_ref[index, 0:rows, RIGHT] = values_ref[...]
            message_ref[index, rows:, :] = rot

        @pl.when(jnp.logical_not(to_later))
        def _():
            message_ref[index, 0:rows, :] = own_query_ref[...]
            message_ref[index, rows:, :] = empty

    for copy in moves:
        copy.wait()


def unpack_messages(messages_ref, keys_ref, vals_ref, rows):
    for index in range(messages_ref.shape[0]):
        chunk, part = index // 2, index % 2
        at = slice(part * rows, (part + 1) * rows)
        rot = messages_ref[index, rows : rows + ROPE, :][:, 0:rows]
        keys_ref[chunk, at, LEFT] = messages_ref[index, 0:rows, LEFT]
        keys_ref[chunk, at, RIGHT] = upright(rot)
        vals_ref[chunk, at, :] = messages_ref[index, 0:rows, RIGHT]


def score_chunks(place, queries, keys_ref, scores_ref, tops, cross):
    rows = queries[0].shape[0]
    lead = lead_of(rows)
    for index in range(keys_ref.shape[0]):
        visible = lead <= chunk_start(place, rows, index, cross)
        for head in range(2):
            scores = nt_dot(queries[head], keys_ref[index]) * score_scale
            scores = jnp.where(visible, scores, masked_low)
            scores_ref[head, index] = scores
            tops[head] = scores if tops[head] is None else jnp.maximum(tops[head], scores)
    return tops


def same_scores_kernel(
    place_ref,
    same_ref,
    own_key_ref,
    own_query_ref,
    values_ref,
    keys_ref,
    vals_ref,
    scores_ref,
    tops_ref,
):
    rows = own_key_ref.shape[0]
    place = place_ref[0]
    unpack_messages(same_ref, keys_ref, vals_ref, rows)
    pair = place // 2
    at = pl.ds(pl.multiple_of(lax.rem(pair, 2) * rows, rows), rows)
    keys_ref[pair // 2, at, :] = own_key_ref[...]
    vals_ref[pair // 2, at, :] = values_ref[...]
    queries = [own_query(own_query_ref[...], head) for head in range(2)]
    tops = score_chunks(place, queries, keys_ref, scores_ref, [None, None], False)
    for head in range(2):
        tops_ref[head] = tops[head]


def forward_kernel(
    experts,
    place_ref,
    cross_ref,
    same_vals_ref,
    same_scores_ref,
    tops_ref,
    own_query_ref,
    hidden_ref,
    gain_ref,
    route_ref,
    affinity_ref,
    cotangent_ref,
    attended_ref,
    log_ref,
    send_ref,
    keys_ref,
    vals_ref,
    scores_ref,
):
    rows = own_query_ref.shape[0]
    place = place_ref[0]
    unpack_messages(cross_ref, keys_ref, vals_ref, rows)
    queries = [own_query(own_query_ref[...], head) for head in range(2)]
    tops = [tops_ref[head] for head in range(2)]
    tops = score_chunks(place, queries, keys_ref, scores_ref, tops, True)
    state = []
    for head in range(2):
        top = jnp.max(tops[head], 1, keepdims=True)
        total = jnp.zeros((rows, 2 * rows), f32)
        mixed = jnp.zeros((rows, LANES), f32)
        for some_scores, some_vals in ((same_scores_ref, same_vals_ref), (scores_ref, vals_ref)):
            for index in range(some_vals.shape[0]):
                weights = jnp.exp(some_scores[head, index] - top)
                total = total + weights
                mixed = mixed + nn_dot(weights.astype(bf16), some_vals[index])
        state.extend([top, jnp.sum(total, 1, keepdims=True), mixed])
    first = lanes_of((rows, LANES)) < VDIM
    attended = jnp.where(first, state[2] / state[1], state[5] / state[4]).astype(bf16)
    attended_ref[...] = attended
    log_ref[...] = jnp.where(
        first, state[0] + jnp.log(state[1]), state[3] + jnp.log(state[4])
    )
    hidden = hidden_ref[...].astype(f32) + attended.astype(f32)
    raised = (hidden * gain_ref[...]).astype(bf16)
    share = gate_share_of(affinity_ref[...])
    grad = (share * cotangent_ref[...].astype(f32)).astype(bf16)
    slots = slots_along_rows(route_ref[...], experts)
    line = lax.broadcasted_iota(jnp.int32, (experts * TALL, rows), 0)
    raised_table = (line == slots).astype(f32).astype(bf16)
    grad_table = (line == slots + CAP).astype(f32).astype(bf16)
    row = lax.broadcasted_iota(jnp.int32, (TALL, LANES), 0)
    gains = jnp.zeros((TALL, LANES), f32)
    for index, piece in enumerate(pieces_of(gain_ref[...], 3)):
        gains = jnp.where(row == PAIR + index, piece, gains)
    gains = jnp.broadcast_to(gains[None], (experts, TALL, LANES)).reshape(-1, LANES)
    sent = nn_dot(raised_table, raised) + nn_dot(grad_table, grad) + gains
    send_ref[...] = sent.astype(bf16)


def unfold_kernel(received_ref, rows_ref, own_ref, gain_ref):
    for index in range(received_ref.shape[0] // TALL):
        at = slice(index * LANES, (index + 1) * LANES)
        start = index * TALL
        tile = received_ref[start : start + PAIR, :]
        own_ref[:, at] = tile
        for copy in range(rows_ref.shape[0]):
            rows_ref[copy, :, at] = tile
        pieces = received_ref[start : start + TALL, :].astype(f32)[PAIR : PAIR + 3]
        gain = pieces[0:1] + pieces[1:2] + pieces[2:3]
        gain_ref[0:1, at] = gain
        gain_ref[1:2, at] = 1.0 / gain


def expert_kernel(rows_ref, gain_ref, own_ref, other_ref, out_ref):
    count = rows_ref.shape[0]
    wide = 2 * LANES
    refs = (own_ref, other_ref)

    def side_by_side(base, index):
        at = slice(base + index * wide, base + (index + 1) * wide)
        return jnp.concatenate([ref[at, :] for ref in refs], 1)

    def down_block(index):
        at = 2 * D + index * wide
        halves = [
            jnp.concatenate([ref[at : at + LANES, :], ref[at + LANES : at + wide, :]], 1)
            for ref in refs
        ]
        return jnp.concatenate(halves, 0)

    zero = jnp.zeros((count, wide), f32)
    gate_val, up_val, grad_active, squares = zero, zero, zero, zero
    for index in range(D // wide):
        at = slice(index * wide, (index + 1) * wide)
        rows = rows_ref[:, at]
        hidden = rows.astype(f32) * gain_ref[1:2, at]
        squares = squares + hidden * hidden
        gate_val = gate_val + nn_dot(rows, side_by_side(0, index))
        up_val = up_val + nn_dot(rows, side_by_side(D, index))
        grad_active = grad_active + nt_dot(rows, down_block(index))
    inverse = lax.rsqrt(jnp.sum(squares, 1, keepdims=True) / D + norm_eps)
    gate_val, up_val = inverse * gate_val, inverse * up_val
    grad_active = pltpu.roll(grad_active, count - CAP, 0)
    upper = lax.rem(lax.broadcasted_iota(jnp.int32, (count, wide), 0), PAIR) < CAP
    sig = 1.0 / (1.0 + jnp.exp(-gate_val))
    silu = gate_val * sig
    active = jnp.where(upper, silu * up_val, 0.0).astype(bf16)
    grad_gate = grad_active * up_val * (sig * (1.0 + gate_val * (1.0 - sig)))
    grad_gate = pltpu.roll(jnp.where(upper, grad_gate, 0.0), CAP, 0).astype(bf16)
    grad_up = pltpu.roll(jnp.where(upper, grad_active * silu, 0.0), CAP, 0).astype(bf16)
    for index in range(D // wide):
        out = nn_dot(active, down_block(index))
        out = out + nt_dot(grad_gate, side_by_side(0, index))
        out = out + nt_dot(grad_up, side_by_side(D, index))
        out_ref[:, index * wide : (index + 1) * wide] = out.astype(bf16)


def reduce_kernel(terms_ref, own_ref, gain_ref, out_ref):
    total = terms_ref[0].astype(f32)
    for index in range(1, terms_ref.shape[0]):
        total = total + terms_ref[index].astype(f32)
    raised = own_ref[...].astype(f32)
    gain = gain_ref[0:1, :]
    back = jnp.concatenate([total[CAP:], total[:CAP]], 0)
    hidden = raised * gain_ref[1:2, :]
    inverse = lax.rsqrt(jnp.sum(hidden * hidden, 1, keepdims=True) / D + norm_eps)
    cross = jnp.sum(back * raised, 1, keepdims=True) / D
    grad = inverse * (back * gain - hidden * (inverse * inverse * cross))
    out = jnp.concatenate([total[:CAP], grad[:CAP]], 0).astype(bf16)
    for index in range(out_ref.shape[0]):
        out_ref[index] = out[:, index * LANES : (index + 1) * LANES]


def combine_kernel(
    experts,
    home_ref,
    hidden_ref,
    attended_ref,
    log_ref,
    route_ref,
    affinity_ref,
    cotangent_ref,
    layer_ref,
    grad_ref,
    stats_ref,
    message_ref,
):
    rows = hidden_ref.shape[0]
    slots = slots_along_columns(route_ref[...], experts)
    column = lanes_of((rows, experts * PAIR))
    home = home_ref[...]
    token_out = nn_dot((column == slots).astype(f32).astype(bf16), home)
    token_grad = nn_dot((column == slots + CAP).astype(f32).astype(bf16), home)
    attended = attended_ref[...].astype(f32)
    hidden = hidden_ref[...].astype(f32) + attended
    share = gate_share_of(affinity_ref[...])
    layer_ref[...] = (hidden + share * token_out).astype(bf16)
    grad = (cotangent_ref[...].astype(f32) + token_grad).astype(bf16)
    grad_ref[...] = grad
    product = grad.astype(f32) * attended
    lane = lanes_of((rows, LANES))
    stats, pieces = jnp.zeros((rows, LANES), f32), jnp.zeros((rows, LANES), f32)
    for head in range(2):
        dot = jnp.sum(jnp.where(lane // VDIM == head, product, 0.0), 1, keepdims=True)
        log = log_ref[:, head * VDIM : head * VDIM + 1]
        stats = jnp.where(lane == 2 * head, dot, jnp.where(lane == 2 * head + 1, log, stats))
        for index, piece in enumerate(pieces_of(dot, 3) + pieces_of(log, 3)):
            pieces = jnp.where(lane == 6 * head + index, piece, pieces)
    stats_ref[...] = stats
    pieces = jnp.concatenate(
        [pieces.astype(bf16), jnp.zeros((2 * LANES - rows, LANES), bf16)], 0
    )
    lines = nt_dot(unit_matrix(LINES, LANES), pieces).astype(bf16)
    for index in range(message_ref.shape[0]):
        message_ref[index, 0:rows, :] = grad
        message_ref[index, rows : rows + LINES, :] = lines[:, LEFT]
        message_ref[index, rows + LINES :, :] = lines[:, RIGHT]


def query_kernel(
    place_ref,
    same_keys_ref,
    same_vals_ref,
    cross_keys_ref,
    cross_vals_ref,
    own_query_ref,
    grad_ref,
    stats_ref,
    query_nope_ref,
    query_rope_ref,
    query_ref,
    grads_ref,
    dq_ref,
):
    rows = own_query_ref.shape[0]
    place = place_ref[0]
    lane = lanes_of((rows, LANES))
    lead = lead_of(rows)
    for head in range(2):
        query_ref[head] = own_query(own_query_ref[...], head)
        grads_ref[head] = jnp.where(
            lane // VDIM == head, grad_ref[...], jnp.zeros((rows, LANES), bf16)
        )
    dq_ref[...] = jnp.zeros_like(dq_ref)

    def step(index, carry):
        for cross in range(2):
            keys_ref, vals_ref = (
                (cross_keys_ref, cross_vals_ref) if cross else (same_keys_ref, same_vals_ref)
            )
            visible = lead <= chunk_start(place, rows, index, cross)
            keys, vals = keys_ref[index], vals_ref[index]
            for head in range(2):
                dot = stats_ref[:, 2 * head : 2 * head + 1]
                log = stats_ref[:, 2 * head + 1 : 2 * head + 2]
                prob = jnp.exp(nt_dot(query_ref[head], keys) * score_scale - log)
                prob = jnp.where(visible, prob, 0.0)
                grad_prob = nt_dot(grads_ref[head], vals)
                grad_score = (prob * (grad_prob - dot)).astype(bf16)
                dq_ref[head] += nn_dot(grad_score, keys)
        return carry

    lax.fori_loop(0, place // 4 + 1, step, 0)
    query_nope_ref[...] = (
        score_scale * jnp.where(lane < NOPE, dq_ref[0, :, LEFT], dq_ref[1, :, LEFT])
    ).astype(bf16)
    rot = jnp.where(lane < ROPE, dq_ref[0, :, RIGHT], pltpu.roll(dq_ref[1, :, RIGHT], ROPE, 1))
    rot = (score_scale * rot).astype(bf16)
    query_rope_ref[...] = nt_dot(unit_matrix(2 * ROPE, LANES), rot).astype(bf16)


def key_chunks(place, messages_ref, grads_ref, own_key_ref, own_query_ref, values_ref, dk, dv):
    rows = own_key_ref.shape[0]
    cross = own_query_ref is None
    lane = lanes_of((rows, LANES))
    keys = [own_key(own_key_ref[...], head) for head in range(2)]
    zero = jnp.zeros((rows, LANES), bf16)
    vals = [jnp.where(lane // VDIM == head, values_ref[...], zero) for head in range(2)]
    lead = lead_of(rows)

    def lines_of(first, second):
        zero = jnp.zeros((LINES, LANES), f32)
        parts = []
        for message in (first, second):
            low = message[rows : rows + LINES].astype(f32)
            high = message[rows + LINES :].astype(f32)
            parts.append(jnp.concatenate([low, high, zero], 1))
        moved = pltpu.roll(parts[1], rows, 1)
        return jnp.where(lanes_of(moved.shape) < rows, parts[0], moved)

    def queries_of(index):
        queries = messages_ref[index, 0:rows, :]
        if cross:
            return queries
        return jnp.where(index == place // 2, own_query_ref[...], queries)

    for chunk in range(messages_ref.shape[0] // 2):
        index = 2 * chunk
        queries = jnp.concatenate([queries_of(index), queries_of(index + 1)], 0)
        first, second = grads_ref[index], grads_ref[index + 1]
        grads = jnp.concatenate([first[0:rows], second[0:rows]], 0)
        lines = lines_of(first, second)
        visible = lead >= chunk_start(place, rows, chunk, cross)
        for head in range(2):
            at = 6 * head
            dot = lines[at : at + 1] + lines[at + 1 : at + 2] + lines[at + 2 : at + 3]
            log = lines[at + 3 : at + 4] + lines[at + 4 : at + 5] + lines[at + 5 : at + 6]
            prob = jnp.exp(nt_dot(keys[head], queries) * score_scale - log)
            prob = jnp.where(visible, prob, 0.0)
            grad_prob = nt_dot(vals[head], grads)
            grad_score = (prob * (grad_prob - dot)).astype(bf16)
            dk[head] = dk[head] + nn_dot(grad_score, queries)
            dv[head] = dv[head] + nn_dot(prob.astype(bf16), grads)
    return dk, dv


def same_key_kernel(
    place_ref,
    same_ref,
    grad_same_ref,
    own_key_ref,
    own_query_ref,
    values_ref,
    dk_ref,
    dv_ref,
):
    dk, dv = key_chunks(
        place_ref[0],
        same_ref,
        grad_same_ref,
        own_key_ref,
        own_query_ref,
        values_ref,
        [0.0, 0.0],
        [0.0, 0.0],
    )
    for head in range(2):
        dk_ref[head] = dk[head]
        dv_ref[head] = dv[head]


def key_kernel(
    place_ref,
    cross_ref,
    grad_cross_ref,
    own_key_ref,
    values_ref,
    dk_ref,
    dv_ref,
    key_nope_ref,
    grad_values_ref,
    rope_ref,
):
    rows = own_key_ref.shape[0]
    lane = lanes_of((rows, LANES))
    dk, dv = key_chunks(
        place_ref[0],
        cross_ref,
        grad_cross_ref,
        own_key_ref,
        None,
        values_ref,
        [dk_ref[head] for head in range(2)],
        [dv_ref[head] for head in range(2)],
    )
    key_nope_ref[...] = (
        score_scale * jnp.where(lane < NOPE, dk[0][:, LEFT], dk[1][:, LEFT])
    ).astype(bf16)
    grad_values_ref[...] = jnp.where(lane < VDIM, dv[0], dv[1]).astype(bf16)
    shared = dk[0][:, RIGHT] + pltpu.roll(dk[1][:, RIGHT], LANES - ROPE, 1)
    quarter = rows // 4
    packed = jnp.zeros((quarter, LANES), f32)
    small = lanes_of((quarter, LANES))
    for index in range(4):
        piece = shared[index * quarter : (index + 1) * quarter]
        if index:
            piece = pltpu.roll(piece, index * ROPE, 1)
        packed = jnp.where(small // ROPE == index, piece, packed)
    rope_ref[...] = (score_scale * packed).astype(bf16)


def pair_sum_kernel(own_ref, other_ref, out_ref):
    total = (own_ref[...].astype(f32) + other_ref[...].astype(f32)).astype(bf16)
    for index in range(out_ref.shape[0]):
        out_ref[index] = total


def rope_kernel(terms_ref, out_ref):
    total = terms_ref[0].astype(f32)
    for index in range(1, terms_ref.shape[0]):
        total = total + terms_ref[index].astype(f32)
    total = total.astype(bf16)
    quarter = total.shape[0]
    out = jnp.zeros((ROPE, 4 * quarter), f32)
    for index in range(4):
        part = nt_dot(unit_matrix(ROPE, LANES, index * ROPE), total).astype(bf16)
        out = out + nn_dot(part, unit_matrix(quarter, 4 * quarter, index * quarter))
    out_ref[...] = out.astype(bf16)


def call(body, limit, outs, scratch=(), scalars=0, count=0, space=pltpu.VMEM):
    place = [pl.BlockSpec(memory_space=pltpu.SMEM)] * scalars
    return pl.pallas_call(
        body,
        out_shape=outs,
        in_specs=place + [pl.BlockSpec(memory_space=space)] * count,
        out_specs=jax.tree.map(lambda _: pl.BlockSpec(memory_space=pltpu.VMEM), outs),
        scratch_shapes=list(scratch),
        compiler_params=pltpu.CompilerParams(vmem_limit_bytes=limit * MIB),
    )


def shape_of(*dims, dtype=bf16):
    return jax.ShapeDtypeStruct(dims, dtype)


def held(value):
    return pltpu.with_memory_space_constraint(value, pltpu.HBM)


def exchange(blocks, axis, groups=None):
    return lax.all_to_all(blocks, axis, 0, 0, tiled=True, axis_index_groups=groups)


def per_device(
    hidden_in,
    query_nope,
    query_rope,
    key_nope,
    key_rope,
    values,
    norm_gain,
    expert_route,
    affinity,
    gate_weight,
    up_weight,
    down_weight,
    cotangent,
):
    rows, width = hidden_in.shape
    ctx_count, experts = lax.axis_size("ctx"), lax.axis_size("exp")
    half = ctx_count // 2
    by_core = [[core + 2 * index for index in range(half)] for core in range(2)]
    across = [(index, index ^ 1) for index in range(ctx_count)]
    quarter = rows // 4

    def swap(value):
        return lax.ppermute(value, "ctx", across)

    place = lax.axis_index("ctx").astype(jnp.int32).reshape(1)
    route = expert_route.reshape(1, rows)
    affinity = affinity.T
    tall = rows + ROPE
    own_key_rows, own_query_rows, messages, weights = call(
        pack_kernel,
        12,
        (
            shape_of(rows, 2 * width),
            shape_of(rows, 2 * width),
            shape_of(half, tall, 2 * width),
            shape_of(3 * D, LANES),
        ),
        [
            pltpu.VMEM((rows, width), bf16),
            pltpu.VMEM((ROPE, rows), bf16),
            pltpu.VMEM((2 * ROPE, rows), bf16),
            pltpu.VMEM((rows, width), bf16),
            pltpu.VMEM((rows, width), bf16),
            pltpu.SemaphoreType.DMA((7 + D // LANES,)),
        ],
        1,
        8,
        pltpu.HBM,
    )(
        place,
        *(held(value) for value in (key_nope, key_rope.T, query_rope.T, query_nope, values)),
        *(held(value[0]) for value in (gate_weight, up_weight, down_weight)),
    )
    own = (own_key_rows, own_query_rows, held(values))
    same = exchange(messages, "ctx", by_core)
    cross = swap(same)

    chunks = half // 2
    same_keys, same_vals, same_scores, tops = call(
        same_scores_kernel,
        20,
        (
            shape_of(chunks, 2 * rows, 2 * width),
            shape_of(chunks, 2 * rows, width),
            shape_of(2, chunks, rows, 2 * rows, dtype=f32),
            shape_of(2, rows, 2 * rows, dtype=f32),
        ),
        (),
        1,
        4,
    )(place, same, *own)
    attended, logs, send, cross_keys, cross_vals = call(
        functools.partial(forward_kernel, experts),
        20,
        (
            shape_of(rows, width),
            shape_of(rows, width, dtype=f32),
            shape_of(experts * TALL, width),
            shape_of(chunks, 2 * rows, 2 * width),
            shape_of(chunks, 2 * rows, width),
        ),
        [pltpu.VMEM((2, chunks, rows, 2 * rows), f32)],
        1,
        10,
    )(
        place,
        cross,
        same_vals,
        same_scores,
        tops,
        own_query_rows,
        *(held(value) for value in (hidden_in, norm_gain.reshape(1, width))),
        *(held(value) for value in (route, affinity, cotangent)),
    )
    send, weights = lax.optimization_barrier((send, weights))
    weights = (weights, swap(weights))
    received = exchange(send.reshape(experts, TALL, width), "exp").reshape(-1, width)
    rows_all, own_rows, gain = call(
        unfold_kernel,
        6,
        (shape_of(half, PAIR, D), shape_of(PAIR, D), shape_of(2, D, dtype=f32)),
        count=1,
    )(received)
    rows_all = exchange(rows_all, "ctx", by_core).reshape(half * PAIR, D)
    partial = call(expert_kernel, 24, shape_of(half * PAIR, D), count=4)(
        rows_all, gain, *weights
    )
    terms = exchange(partial.reshape(half, PAIR, D), "ctx", by_core)
    back = call(reduce_kernel, 8, shape_of(experts, PAIR, width), count=3)(
        terms, own_rows, gain
    )
    home = exchange(back, "exp").reshape(experts * PAIR, width)
    layer_out, grad_hidden, stats, messages = call(
        functools.partial(combine_kernel, experts),
        8,
        (
            shape_of(rows, width),
            shape_of(rows, width),
            shape_of(rows, width, dtype=f32),
            shape_of(half, tall, width),
        ),
        count=7,
    )(home, hidden_in, attended, logs, route, affinity, cotangent)
    grad_same = exchange(messages, "ctx", by_core)
    grad_cross = swap(grad_same)
    dk, dv = call(
        same_key_kernel,
        14,
        (
            shape_of(2, rows, 2 * width, dtype=f32),
            shape_of(2, rows, width, dtype=f32),
        ),
        (),
        1,
        5,
    )(place, same, grad_same, *own)
    gk_nope, g_values, rope_part = call(
        key_kernel,
        14,
        (shape_of(rows, width), shape_of(rows, width), shape_of(quarter, LANES)),
        (),
        1,
        6,
    )(place, cross, grad_cross, own_key_rows, own[2], dk, dv)
    line = experts // 2
    rope_other = lax.ppermute(
        rope_part, "exp", [(index, (index + line) % experts) for index in range(experts)]
    )
    rope_pairs = call(pair_sum_kernel, 2, shape_of(line, quarter, LANES), count=2)(
        rope_part, rope_other
    )
    by_line = [[part * line + index for index in range(line)] for part in range(2)]
    rope_terms = exchange(rope_pairs, "exp", by_line)
    gq_nope, gq_rope = call(
        query_kernel,
        14,
        (shape_of(rows, width), shape_of(2 * ROPE, rows)),
        [
            pltpu.VMEM((2, rows, 2 * width), bf16),
            pltpu.VMEM((2, rows, width), bf16),
            pltpu.VMEM((2, rows, 2 * width), f32),
        ],
        1,
        7,
    )(place, same_keys, same_vals, cross_keys, cross_vals, own_query_rows, grad_hidden, stats)
    gk_rope = call(rope_kernel, 4, shape_of(ROPE, rows), count=1)(rope_terms)
    return (layer_out, grad_hidden, gq_nope, gq_rope.T, gk_nope, gk_rope.T, g_values)


def solution(mesh):
    placed = (
        P("ctx", "exp"),
        P("ctx", "exp"),
        P("ctx", "exp"),
        P("ctx", "exp"),
        P("ctx", None),
        P("ctx", "exp"),
        P("exp"),
        P("ctx"),
        P("ctx", None),
        P("exp", None, "ctx"),
        P("exp", None, "ctx"),
        P("exp", "ctx", None),
        P("ctx", "exp"),
    )
    return jax.shard_map(
        per_device,
        mesh=mesh,
        in_specs=placed,
        out_specs=(
            P("ctx", "exp"),
            P("ctx", "exp"),
            P("ctx", "exp"),
            P("ctx", "exp"),
            P("ctx", "exp"),
            P("ctx", None),
            P("ctx", "exp"),
        ),
        check_vma=False,
    )
```

```python
import functools
import math

import jax
import jax.numpy as jnp
from jax import lax
from jax.experimental import pallas as pl
from jax.experimental.pallas import tpu as pltpu
from jax.sharding import PartitionSpec as P

NOPE = 64
ROPE = 32
VDIM = 64
D = 4096
CAP = 12
PAIR = 2 * CAP
TALL = 32
LINES = 16
LANES = 128

norm_eps = 1e-06
route_scale = 2.5
masked_low = -1e30
score_scale = 1.0 / math.sqrt(NOPE + ROPE)
log2_e = math.log2(math.e)

bf16 = jnp.bfloat16
f32 = jnp.float32
MIB = 1024 * 1024

LEFT = slice(0, LANES)
RIGHT = slice(LANES, 2 * LANES)


def nt_dot(a, b):
    return lax.dot_general(a, b, (((1,), (1,)), ((), ())), preferred_element_type=f32)


def nn_dot(a, b):
    return jnp.dot(a, b, preferred_element_type=f32)


def lanes_of(shape):
    return lax.broadcasted_iota(jnp.int32, shape, len(shape) - 1)


def pieces_of(value, count):
    pieces = []
    for _ in range(count):
        piece = value.astype(bf16).astype(f32)
        pieces.append(piece)
        value = value - piece
    return pieces


def own_query(queries, head):
    rows = queries.shape[0]
    lane = lanes_of((rows, LANES))
    nope = jnp.where(lane // NOPE == head, queries[:, LEFT], jnp.zeros((rows, LANES), bf16))
    rot = queries[:, RIGHT].astype(f32)
    if head:
        rot = pltpu.roll(rot, LANES - head * ROPE, 1)
    rot = jnp.where(lane < ROPE, rot, 0.0).astype(bf16)
    return jnp.concatenate([nope, rot], 1)


def own_key(keys, head):
    rows = keys.shape[0]
    lane = lanes_of((rows, LANES))
    nope = jnp.where(lane // NOPE == head, keys[:, LEFT], jnp.zeros((rows, LANES), bf16))
    rot = keys[:, RIGHT].astype(f32)
    if head:
        rot = pltpu.roll(rot, head * ROPE, 1)
    return jnp.concatenate([nope, rot.astype(bf16)], 1)


def upright(narrow):
    count, rows = narrow.shape
    full = jnp.concatenate([narrow, jnp.zeros((LANES - count, rows), bf16)], 0)
    return nt_dot(unit_matrix(rows, rows), full).astype(bf16)


def keys_of(message, rows):
    rot = upright(message[rows : rows + ROPE, :][:, 0:rows])
    return jnp.concatenate([message[0:rows, LEFT], rot], 1)


def lead_of(rows):
    shape = (rows, 2 * rows)
    lane = lanes_of(shape)
    return lane + jnp.where(lane >= rows, rows, 0) - lax.broadcasted_iota(jnp.int32, shape, 0)


def chunk_start(place, rows, index, cross):
    start = (place // 2 - 2 * index) * (2 * rows)
    if cross:
        start = start + (2 * (place % 2) - 1) * rows
    return start


def slots_along_rows(route_row, experts):
    count = route_row.shape[1]
    hits = (lax.broadcasted_iota(jnp.int32, (experts, count), 0) == route_row).astype(f32)
    before = lax.broadcasted_iota(jnp.int32, (count, count), 0) < lanes_of((count, count))
    ranks = nn_dot(hits.astype(bf16), before.astype(f32).astype(bf16))
    rank = jnp.sum(ranks * hits, 0, keepdims=True)
    return route_row * TALL + rank.astype(jnp.int32)


def column_of(row):
    count = row.shape[1]
    shape = (count, count)
    match = lax.broadcasted_iota(jnp.int32, shape, 0) == lanes_of(shape)
    return jnp.sum(jnp.where(match, row, jnp.zeros_like(row)), 1, keepdims=True)


def unit_matrix(rows, columns, offset=0):
    shape = (rows, columns)
    match = lax.broadcasted_iota(jnp.int32, shape, 0) + offset == lanes_of(shape)
    return match.astype(f32).astype(bf16)


def slots_along_columns(route_row, experts):
    route_column = column_of(route_row)
    count = route_column.shape[0]
    hits = (lanes_of((count, experts)) == route_column).astype(f32)
    before = lanes_of((count, count)) < lax.broadcasted_iota(jnp.int32, (count, count), 0)
    ranks = nn_dot(before.astype(f32).astype(bf16), hits.astype(bf16))
    rank = jnp.sum(ranks * hits, 1, keepdims=True)
    return route_column * PAIR + rank.astype(jnp.int32)


def gate_share_of(affinity):
    return column_of(route_scale * affinity[0:1] / jnp.sum(affinity, 0, keepdims=True))


def pack_kernel(
    place_ref,
    key_nope_hbm,
    key_rope_hbm,
    query_rope_hbm,
    query_nope_hbm,
    values_hbm,
    own_key_ref,
    own_query_ref,
    message_ref,
    key_nope_ref,
    key_rope_ref,
    query_rope_ref,
    query_nope_ref,
    values_ref,
    sems,
):
    pairs = (
        (key_rope_hbm, key_rope_ref),
        (query_rope_hbm, query_rope_ref),
        (key_nope_hbm, key_nope_ref),
        (values_hbm, values_ref),
        (query_nope_hbm, query_nope_ref),
    )
    copies = [
        pltpu.make_async_copy(source, target, sems.at[index])
        for index, (source, target) in enumerate(pairs)
    ]
    for copy in copies:
        copy.start()
    for copy in copies:
        copy.wait()
    rows = key_nope_ref.shape[0]
    place = place_ref[0]
    pair, core = place // 2, place % 2
    own_key_ref[:, LEFT] = key_nope_ref[...]
    own_key_ref[:, RIGHT] = upright(key_rope_ref[...])
    own_query_ref[:, LEFT] = query_nope_ref[...]
    own_query_ref[:, RIGHT] = upright(query_rope_ref[...])
    rot = jnp.concatenate([key_rope_ref[...], jnp.zeros((ROPE, 2 * LANES - rows), bf16)], 1)
    empty = jnp.zeros((ROPE, 2 * LANES), bf16)
    for index in range(message_ref.shape[0]):
        to_later = (index > pair) | ((index == pair) & (core == 0))

        @pl.when(to_later)
        def _():
            message_ref[index, 0:rows, LEFT] = key_nope_ref[...]
            message_ref[index, 0:rows, RIGHT] = values_ref[...]
            message_ref[index, rows:, :] = rot

        @pl.when(jnp.logical_not(to_later))
        def _():
            message_ref[index, 0:rows, :] = own_query_ref[...]
            message_ref[index, rows:, :] = empty


def unpack_messages(messages_ref, keys_ref, vals_ref, rows):
    for index in range(messages_ref.shape[0]):
        chunk, part = index // 2, index % 2
        at = slice(part * rows, (part + 1) * rows)
        rot = messages_ref[index, rows : rows + ROPE, :][:, 0:rows]
        keys_ref[chunk, at, LEFT] = messages_ref[index, 0:rows, LEFT]
        keys_ref[chunk, at, RIGHT] = upright(rot)
        vals_ref[chunk, at, :] = messages_ref[index, 0:rows, RIGHT]


def score_chunks(place, queries, keys_ref, scores_ref, tops, cross):
    rows = queries[0].shape[0]
    lead = lead_of(rows)
    for index in range(keys_ref.shape[0]):
        visible = lead <= chunk_start(place, rows, index, cross)
        for head in range(2):
            scores = jnp.where(visible, nt_dot(queries[head], keys_ref[index]), masked_low)
            scores_ref[head, index] = scores
            tops[head] = scores if tops[head] is None else jnp.maximum(tops[head], scores)
    return tops


def same_scores_kernel(
    place_ref,
    same_ref,
    own_key_ref,
    own_query_ref,
    values_ref,
    gate_hbm,
    up_hbm,
    down_hbm,
    keys_ref,
    vals_ref,
    scores_ref,
    tops_ref,
    weights_ref,
    sems,
):
    moves = [(gate_hbm, weights_ref.at[0:D, :]), (up_hbm, weights_ref.at[D : 2 * D, :])]
    for index in range(D // LANES):
        start = 2 * D + index * LANES
        source = down_hbm.at[:, index * LANES : (index + 1) * LANES]
        moves.append((source, weights_ref.at[start : start + LANES, :]))
    moves = [
        pltpu.make_async_copy(source, target, sems.at[index])
        for index, (source, target) in enumerate(moves)
    ]
    for copy in moves:
        copy.start()
    rows = own_key_ref.shape[0]
    place = place_ref[0]
    unpack_messages(same_ref, keys_ref, vals_ref, rows)
    pair = place // 2
    at = pl.ds(pl.multiple_of(lax.rem(pair, 2) * rows, rows), rows)
    keys_ref[pair // 2, at, :] = own_key_ref[...]
    vals_ref[pair // 2, at, :] = values_ref[...]
    queries = [own_query(own_query_ref[...], head) for head in range(2)]
    tops = score_chunks(place, queries, keys_ref, scores_ref, [None, None], False)
    for head in range(2):
        tops_ref[head] = tops[head]
    for copy in moves:
        copy.wait()


def forward_kernel(
    experts,
    place_ref,
    cross_ref,
    same_vals_ref,
    same_scores_ref,
    tops_ref,
    own_query_ref,
    hidden_ref,
    gain_ref,
    route_ref,
    affinity_ref,
    cotangent_ref,
    attended_ref,
    log_ref,
    send_ref,
    keys_ref,
    vals_ref,
    scores_ref,
):
    rows = own_query_ref.shape[0]
    place = place_ref[0]
    unpack_messages(cross_ref, keys_ref, vals_ref, rows)
    queries = [own_query(own_query_ref[...], head) for head in range(2)]
    tops = [tops_ref[head] for head in range(2)]
    tops = score_chunks(place, queries, keys_ref, scores_ref, tops, True)
    state = []
    for head in range(2):
        top = jnp.max(tops[head], 1, keepdims=True)
        total = jnp.zeros((rows, 2 * rows), f32)
        mixed = jnp.zeros((rows, LANES), f32)
        for some_scores, some_vals in ((same_scores_ref, same_vals_ref), (scores_ref, vals_ref)):
            for index in range(some_vals.shape[0]):
                weights = jnp.exp2((some_scores[head, index] - top) * (score_scale * log2_e))
                total = total + weights
                mixed = mixed + nn_dot(weights.astype(bf16), some_vals[index])
        state.extend([top * score_scale, jnp.sum(total, 1, keepdims=True), mixed])
    first = lanes_of((rows, LANES)) < VDIM
    attended = jnp.where(first, state[2] / state[1], state[5] / state[4]).astype(bf16)
    attended_ref[...] = attended
    log_ref[...] = jnp.where(
        first, state[0] + jnp.log(state[1]), state[3] + jnp.log(state[4])
    )
    hidden = hidden_ref[...].astype(f32) + attended.astype(f32)
    raised = (hidden * gain_ref[...]).astype(bf16)
    share = gate_share_of(affinity_ref[...])
    grad = (share * cotangent_ref[...].astype(f32)).astype(bf16)
    slots = slots_along_rows(route_ref[...], experts)
    line = lax.broadcasted_iota(jnp.int32, (experts * TALL, rows), 0)
    raised_table = (line == slots).astype(f32).astype(bf16)
    grad_table = (line == slots + CAP).astype(f32).astype(bf16)
    row = lax.broadcasted_iota(jnp.int32, (TALL, LANES), 0)
    gains = jnp.zeros((TALL, LANES), f32)
    for index, piece in enumerate(pieces_of(gain_ref[...], 3)):
        gains = jnp.where(row == PAIR + index, piece, gains)
    gains = jnp.broadcast_to(gains[None], (experts, TALL, LANES)).reshape(-1, LANES)
    sent = nn_dot(raised_table, raised) + nn_dot(grad_table, grad) + gains
    send_ref[...] = sent.astype(bf16)


def unfold_kernel(received_ref, rows_ref, own_ref, gain_ref):
    for index in range(received_ref.shape[0] // TALL):
        at = slice(index * LANES, (index + 1) * LANES)
        start = index * TALL
        tile = received_ref[start : start + PAIR, :]
        own_ref[:, at] = tile
        for copy in range(rows_ref.shape[0]):
            rows_ref[copy, :, at] = tile
        pieces = received_ref[start : start + TALL, :].astype(f32)[PAIR : PAIR + 3]
        gain = pieces[0:1] + pieces[1:2] + pieces[2:3]
        gain_ref[0:1, at] = gain
        gain_ref[1:2, at] = 1.0 / gain


def expert_kernel(rows_ref, gain_ref, own_ref, other_ref, out_ref):
    count = rows_ref.shape[0]
    wide = 2 * LANES
    refs = (own_ref, other_ref)

    def side_by_side(base, index):
        at = slice(base + index * wide, base + (index + 1) * wide)
        return jnp.concatenate([ref[at, :] for ref in refs], 1)

    def down_block(index):
        at = 2 * D + index * wide
        halves = [
            jnp.concatenate([ref[at : at + LANES, :], ref[at + LANES : at + wide, :]], 1)
            for ref in refs
        ]
        return jnp.concatenate(halves, 0)

    zero = jnp.zeros((count, wide), f32)
    gate_val, up_val, grad_active, squares = zero, zero, zero, zero
    for index in range(D // wide):
        at = slice(index * wide, (index + 1) * wide)
        rows = rows_ref[:, at]
        hidden = rows.astype(f32) * gain_ref[1:2, at]
        squares = squares + hidden * hidden
        gate_val = gate_val + nn_dot(rows, side_by_side(0, index))
        up_val = up_val + nn_dot(rows, side_by_side(D, index))
        grad_active = grad_active + nt_dot(rows, down_block(index))
    inverse = lax.rsqrt(jnp.sum(squares, 1, keepdims=True) / D + norm_eps)
    gate_val, up_val = inverse * gate_val, inverse * up_val
    grad_active = pltpu.roll(grad_active, count - CAP, 0)
    upper = lax.rem(lax.broadcasted_iota(jnp.int32, (count, wide), 0), PAIR) < CAP
    sig = 1.0 / (1.0 + jnp.exp(-gate_val))
    silu = gate_val * sig
    active = jnp.where(upper, silu * up_val, 0.0).astype(bf16)
    grad_gate = grad_active * up_val * (sig * (1.0 + gate_val * (1.0 - sig)))
    grad_gate = pltpu.roll(jnp.where(upper, grad_gate, 0.0), CAP, 0).astype(bf16)
    grad_up = pltpu.roll(jnp.where(upper, grad_active * silu, 0.0), CAP, 0).astype(bf16)
    for index in range(D // wide):
        out = nn_dot(active, down_block(index))
        out = out + nt_dot(grad_gate, side_by_side(0, index))
        out = out + nt_dot(grad_up, side_by_side(D, index))
        out_ref[:, index * wide : (index + 1) * wide] = out.astype(bf16)


def reduce_kernel(terms_ref, own_ref, gain_ref, out_ref):
    total = terms_ref[0].astype(f32)
    for index in range(1, terms_ref.shape[0]):
        total = total + terms_ref[index].astype(f32)
    raised = own_ref[...].astype(f32)
    gain = gain_ref[0:1, :]
    back = jnp.concatenate([total[CAP:], total[:CAP]], 0)
    hidden = raised * gain_ref[1:2, :]
    inverse = lax.rsqrt(jnp.sum(hidden * hidden, 1, keepdims=True) / D + norm_eps)
    cross = jnp.sum(back * raised, 1, keepdims=True) / D
    grad = inverse * (back * gain - hidden * (inverse * inverse * cross))
    out = jnp.concatenate([total[:CAP], grad[:CAP]], 0).astype(bf16)
    for index in range(out_ref.shape[0]):
        out_ref[index] = out[:, index * LANES : (index + 1) * LANES]


def combine_kernel(
    experts,
    home_ref,
    hidden_ref,
    attended_ref,
    log_ref,
    route_ref,
    affinity_ref,
    cotangent_ref,
    layer_ref,
    grad_ref,
    stats_ref,
    message_ref,
):
    rows = hidden_ref.shape[0]
    slots = slots_along_columns(route_ref[...], experts)
    column = lanes_of((rows, experts * PAIR))
    home = home_ref[...]
    token_out = nn_dot((column == slots).astype(f32).astype(bf16), home)
    token_grad = nn_dot((column == slots + CAP).astype(f32).astype(bf16), home)
    attended = attended_ref[...].astype(f32)
    hidden = hidden_ref[...].astype(f32) + attended
    share = gate_share_of(affinity_ref[...])
    layer_ref[...] = (hidden + share * token_out).astype(bf16)
    grad = (cotangent_ref[...].astype(f32) + token_grad).astype(bf16)
    grad_ref[...] = grad
    product = grad.astype(f32) * attended
    lane = lanes_of((rows, LANES))
    stats, pieces = jnp.zeros((rows, LANES), f32), jnp.zeros((rows, LANES), f32)
    for head in range(2):
        dot = jnp.sum(jnp.where(lane // VDIM == head, product, 0.0), 1, keepdims=True)
        log = log_ref[:, head * VDIM : head * VDIM + 1]
        stats = jnp.where(lane == 2 * head, dot, jnp.where(lane == 2 * head + 1, log, stats))
        for index, piece in enumerate(pieces_of(dot, 3) + pieces_of(log, 3)):
            pieces = jnp.where(lane == 6 * head + index, piece, pieces)
    stats_ref[...] = stats
    pieces = jnp.concatenate(
        [pieces.astype(bf16), jnp.zeros((2 * LANES - rows, LANES), bf16)], 0
    )
    lines = nt_dot(unit_matrix(LINES, LANES), pieces).astype(bf16)
    for index in range(message_ref.shape[0]):
        message_ref[index, 0:rows, :] = grad
        message_ref[index, rows : rows + LINES, :] = lines[:, LEFT]
        message_ref[index, rows + LINES :, :] = lines[:, RIGHT]


def query_kernel(
    place_ref,
    same_keys_ref,
    same_vals_ref,
    cross_keys_ref,
    cross_vals_ref,
    own_query_ref,
    grad_ref,
    stats_ref,
    query_nope_ref,
    query_rope_ref,
    query_ref,
    grads_ref,
    dq_ref,
):
    rows = own_query_ref.shape[0]
    place = place_ref[0]
    lane = lanes_of((rows, LANES))
    lead = lead_of(rows)
    for head in range(2):
        query_ref[head] = own_query(own_query_ref[...], head)
        grads_ref[head] = jnp.where(
            lane // VDIM == head, grad_ref[...], jnp.zeros((rows, LANES), bf16)
        )
    dq_ref[...] = jnp.zeros_like(dq_ref)

    def step(index, carry):
        for cross in range(2):
            keys_ref, vals_ref = (
                (cross_keys_ref, cross_vals_ref) if cross else (same_keys_ref, same_vals_ref)
            )
            visible = lead <= chunk_start(place, rows, index, cross)
            keys, vals = keys_ref[index], vals_ref[index]
            for head in range(2):
                dot = stats_ref[:, 2 * head : 2 * head + 1]
                log = stats_ref[:, 2 * head + 1 : 2 * head + 2] * log2_e
                prob = jnp.exp2(nt_dot(query_ref[head], keys) * (score_scale * log2_e) - log)
                prob = jnp.where(visible, prob, 0.0)
                grad_prob = nt_dot(grads_ref[head], vals)
                grad_score = (prob * (grad_prob - dot)).astype(bf16)
                dq_ref[head] += nn_dot(grad_score, keys)
        return carry

    lax.fori_loop(0, place // 4 + 1, step, 0)
    query_nope_ref[...] = (
        score_scale * jnp.where(lane < NOPE, dq_ref[0, :, LEFT], dq_ref[1, :, LEFT])
    ).astype(bf16)
    rot = jnp.where(lane < ROPE, dq_ref[0, :, RIGHT], pltpu.roll(dq_ref[1, :, RIGHT], ROPE, 1))
    rot = (score_scale * rot).astype(bf16)
    query_rope_ref[...] = nt_dot(unit_matrix(2 * ROPE, LANES), rot).astype(bf16)


def key_chunks(place, messages_ref, grads_ref, own_key_ref, own_query_ref, values_ref, dk, dv):
    rows = own_key_ref.shape[0]
    cross = own_query_ref is None
    lane = lanes_of((rows, LANES))
    keys = [own_key(own_key_ref[...], head) for head in range(2)]
    zero = jnp.zeros((rows, LANES), bf16)
    vals = [jnp.where(lane // VDIM == head, values_ref[...], zero) for head in range(2)]
    lead = lead_of(rows)

    def lines_of(first, second):
        zero = jnp.zeros((LINES, LANES), f32)
        parts = []
        for message in (first, second):
            low = message[rows : rows + LINES].astype(f32)
            high = message[rows + LINES :].astype(f32)
            parts.append(jnp.concatenate([low, high, zero], 1))
        moved = pltpu.roll(parts[1], rows, 1)
        return jnp.where(lanes_of(moved.shape) < rows, parts[0], moved)

    def queries_of(index):
        queries = messages_ref[index, 0:rows, :]
        if cross:
            return queries
        return jnp.where(index == place // 2, own_query_ref[...], queries)

    for chunk in range(messages_ref.shape[0] // 2):
        index = 2 * chunk
        queries = jnp.concatenate([queries_of(index), queries_of(index + 1)], 0)
        first, second = grads_ref[index], grads_ref[index + 1]
        grads = jnp.concatenate([first[0:rows], second[0:rows]], 0)
        lines = lines_of(first, second)
        visible = lead >= chunk_start(place, rows, chunk, cross)
        for head in range(2):
            at = 6 * head
            dot = lines[at : at + 1] + lines[at + 1 : at + 2] + lines[at + 2 : at + 3]
            log = lines[at + 3 : at + 4] + lines[at + 4 : at + 5] + lines[at + 5 : at + 6]
            prob = nt_dot(keys[head], queries) * (score_scale * log2_e)
            prob = jnp.exp2(prob - log * log2_e)
            prob = jnp.where(visible, prob, 0.0)
            grad_prob = nt_dot(vals[head], grads)
            grad_score = (prob * (grad_prob - dot)).astype(bf16)
            dk[head] = dk[head] + nn_dot(grad_score, queries)
            dv[head] = dv[head] + nn_dot(prob.astype(bf16), grads)
    return dk, dv


def same_key_kernel(
    place_ref,
    same_ref,
    grad_same_ref,
    own_key_ref,
    own_query_ref,
    values_ref,
    dk_ref,
    dv_ref,
):
    dk, dv = key_chunks(
        place_ref[0],
        same_ref,
        grad_same_ref,
        own_key_ref,
        own_query_ref,
        values_ref,
        [0.0, 0.0],
        [0.0, 0.0],
    )
    for head in range(2):
        dk_ref[head] = dk[head]
        dv_ref[head] = dv[head]


def key_kernel(
    place_ref,
    cross_ref,
    grad_cross_ref,
    own_key_ref,
    values_ref,
    dk_ref,
    dv_ref,
    key_nope_ref,
    grad_values_ref,
    rope_ref,
):
    rows = own_key_ref.shape[0]
    lane = lanes_of((rows, LANES))
    dk, dv = key_chunks(
        place_ref[0],
        cross_ref,
        grad_cross_ref,
        own_key_ref,
        None,
        values_ref,
        [dk_ref[head] for head in range(2)],
        [dv_ref[head] for head in range(2)],
    )
    key_nope_ref[...] = (
        score_scale * jnp.where(lane < NOPE, dk[0][:, LEFT], dk[1][:, LEFT])
    ).astype(bf16)
    grad_values_ref[...] = jnp.where(lane < VDIM, dv[0], dv[1]).astype(bf16)
    shared = dk[0][:, RIGHT] + pltpu.roll(dk[1][:, RIGHT], LANES - ROPE, 1)
    quarter = rows // 4
    packed = jnp.zeros((quarter, LANES), f32)
    small = lanes_of((quarter, LANES))
    for index in range(4):
        piece = shared[index * quarter : (index + 1) * quarter]
        if index:
            piece = pltpu.roll(piece, index * ROPE, 1)
        packed = jnp.where(small // ROPE == index, piece, packed)
    rope_ref[...] = (score_scale * packed).astype(bf16)


def pair_sum_kernel(own_ref, other_ref, out_ref):
    total = (own_ref[...].astype(f32) + other_ref[...].astype(f32)).astype(bf16)
    for index in range(out_ref.shape[0]):
        out_ref[index] = total


def rope_kernel(terms_ref, out_ref):
    total = terms_ref[0].astype(f32)
    for index in range(1, terms_ref.shape[0]):
        total = total + terms_ref[index].astype(f32)
    total = total.astype(bf16)
    quarter = total.shape[0]
    out = jnp.zeros((ROPE, 4 * quarter), f32)
    for index in range(4):
        part = nt_dot(unit_matrix(ROPE, LANES, index * ROPE), total).astype(bf16)
        out = out + nn_dot(part, unit_matrix(quarter, 4 * quarter, index * quarter))
    out_ref[...] = out.astype(bf16)


def call(body, limit, outs, scratch=(), scalars=0, count=0, far=0):
    spaces = [pltpu.SMEM] * scalars + [pltpu.VMEM] * count + [pltpu.HBM] * far
    return pl.pallas_call(
        body,
        out_shape=outs,
        in_specs=[pl.BlockSpec(memory_space=space) for space in spaces],
        out_specs=jax.tree.map(lambda _: pl.BlockSpec(memory_space=pltpu.VMEM), outs),
        scratch_shapes=list(scratch),
        compiler_params=pltpu.CompilerParams(vmem_limit_bytes=limit * MIB),
    )


def shape_of(*dims, dtype=bf16):
    return jax.ShapeDtypeStruct(dims, dtype)


def held(value):
    return pltpu.with_memory_space_constraint(value, pltpu.HBM)


def exchange(blocks, axis, groups=None):
    return lax.all_to_all(blocks, axis, 0, 0, tiled=True, axis_index_groups=groups)


def per_device(
    hidden_in,
    query_nope,
    query_rope,
    key_nope,
    key_rope,
    values,
    norm_gain,
    expert_route,
    affinity,
    gate_weight,
    up_weight,
    down_weight,
    cotangent,
):
    rows, width = hidden_in.shape
    ctx_count, experts = lax.axis_size("ctx"), lax.axis_size("exp")
    half = ctx_count // 2
    by_core = [[core + 2 * index for index in range(half)] for core in range(2)]
    across = [(index, index ^ 1) for index in range(ctx_count)]
    quarter = rows // 4

    def swap(value):
        return lax.ppermute(value, "ctx", across)

    place = lax.axis_index("ctx").astype(jnp.int32).reshape(1)
    route = expert_route.reshape(1, rows)
    affinity = affinity.T
    tall = rows + ROPE
    own_key_rows, own_query_rows, messages = call(
        pack_kernel,
        6,
        (
            shape_of(rows, 2 * width),
            shape_of(rows, 2 * width),
            shape_of(half, tall, 2 * width),
        ),
        [
            pltpu.VMEM((rows, width), bf16),
            pltpu.VMEM((ROPE, rows), bf16),
            pltpu.VMEM((2 * ROPE, rows), bf16),
            pltpu.VMEM((rows, width), bf16),
            pltpu.VMEM((rows, width), bf16),
            pltpu.SemaphoreType.DMA((5,)),
        ],
        1,
        0,
        5,
    )(
        place,
        *(held(value) for value in (key_nope, key_rope.T, query_rope.T, query_nope, values)),
    )
    own = (own_key_rows, own_query_rows, held(values))
    same = exchange(messages, "ctx", by_core)
    cross = swap(same)

    chunks = half // 2
    same_keys, same_vals, same_scores, tops, weights = call(
        same_scores_kernel,
        26,
        (
            shape_of(chunks, 2 * rows, 2 * width),
            shape_of(chunks, 2 * rows, width),
            shape_of(2, chunks, rows, 2 * rows, dtype=f32),
            shape_of(2, rows, 2 * rows, dtype=f32),
            shape_of(3 * D, LANES),
        ),
        [pltpu.SemaphoreType.DMA((2 + D // LANES,))],
        1,
        4,
        3,
    )(
        place,
        same,
        *own,
        *(held(value[0]) for value in (gate_weight, up_weight, down_weight)),
    )
    attended, logs, send, cross_keys, cross_vals = call(
        functools.partial(forward_kernel, experts),
        20,
        (
            shape_of(rows, width),
            shape_of(rows, width, dtype=f32),
            shape_of(experts * TALL, width),
            shape_of(chunks, 2 * rows, 2 * width),
            shape_of(chunks, 2 * rows, width),
        ),
        [pltpu.VMEM((2, chunks, rows, 2 * rows), f32)],
        1,
        10,
    )(
        place,
        cross,
        same_vals,
        same_scores,
        tops,
        own_query_rows,
        *(held(value) for value in (hidden_in, norm_gain.reshape(1, width))),
        *(held(value) for value in (route, affinity, cotangent)),
    )
    send, weights = lax.optimization_barrier((send, weights))
    weights = (weights, swap(weights))
    received = exchange(send.reshape(experts, TALL, width), "exp").reshape(-1, width)
    rows_all, own_rows, gain = call(
        unfold_kernel,
        6,
        (shape_of(half, PAIR, D), shape_of(PAIR, D), shape_of(2, D, dtype=f32)),
        count=1,
    )(received)
    rows_all = exchange(rows_all, "ctx", by_core).reshape(half * PAIR, D)
    partial = call(expert_kernel, 24, shape_of(half * PAIR, D), count=4)(
        rows_all, gain, *weights
    )
    terms = exchange(partial.reshape(half, PAIR, D), "ctx", by_core)
    back = call(reduce_kernel, 8, shape_of(experts, PAIR, width), count=3)(
        terms, own_rows, gain
    )
    home = exchange(back, "exp").reshape(experts * PAIR, width)
    layer_out, grad_hidden, stats, messages = call(
        functools.partial(combine_kernel, experts),
        8,
        (
            shape_of(rows, width),
            shape_of(rows, width),
            shape_of(rows, width, dtype=f32),
            shape_of(half, tall, width),
        ),
        count=7,
    )(home, hidden_in, attended, logs, route, affinity, cotangent)
    grad_same = exchange(messages, "ctx", by_core)
    grad_cross = swap(grad_same)
    dk, dv = call(
        same_key_kernel,
        14,
        (
            shape_of(2, rows, 2 * width, dtype=f32),
            shape_of(2, rows, width, dtype=f32),
        ),
        (),
        1,
        5,
    )(place, same, grad_same, *own)
    gk_nope, g_values, rope_part = call(
        key_kernel,
        14,
        (shape_of(rows, width), shape_of(rows, width), shape_of(quarter, LANES)),
        (),
        1,
        6,
    )(place, cross, grad_cross, own_key_rows, own[2], dk, dv)
    line = experts // 2
    rope_other = lax.ppermute(
        rope_part, "exp", [(index, (index + line) % experts) for index in range(experts)]
    )
    rope_pairs = call(pair_sum_kernel, 2, shape_of(line, quarter, LANES), count=2)(
        rope_part, rope_other
    )
    by_line = [[part * line + index for index in range(line)] for part in range(2)]
    rope_terms = exchange(rope_pairs, "exp", by_line)
    gq_nope, gq_rope = call(
        query_kernel,
        14,
        (shape_of(rows, width), shape_of(2 * ROPE, rows)),
        [
            pltpu.VMEM((2, rows, 2 * width), bf16),
            pltpu.VMEM((2, rows, width), bf16),
            pltpu.VMEM((2, rows, 2 * width), f32),
        ],
        1,
        7,
    )(place, same_keys, same_vals, cross_keys, cross_vals, own_query_rows, grad_hidden, stats)
    gk_rope = call(rope_kernel, 4, shape_of(ROPE, rows), count=1)(rope_terms)
    return (layer_out, grad_hidden, gq_nope, gq_rope.T, gk_nope, gk_rope.T, g_values)


def solution(mesh):
    placed = (
        P("ctx", "exp"),
        P("ctx", "exp"),
        P("ctx", "exp"),
        P("ctx", "exp"),
        P("ctx", None),
        P("ctx", "exp"),
        P("exp"),
        P("ctx"),
        P("ctx", None),
        P("exp", None, "ctx"),
        P("exp", None, "ctx"),
        P("exp", "ctx", None),
        P("ctx", "exp"),
    )
    return jax.shard_map(
        per_device,
        mesh=mesh,
        in_specs=placed,
        out_specs=(
            P("ctx", "exp"),
            P("ctx", "exp"),
            P("ctx", "exp"),
            P("ctx", "exp"),
            P("ctx", "exp"),
            P("ctx", None),
            P("ctx", "exp"),
        ),
        check_vma=False,
    )
```
